256 devices in a mesh: pair: 8 (over y, x_lo), tm: 32 (over x_hi, z, core).
Axes of the slice: x: 4 (x_hi: 2, x_lo: 2; x = x_hi * 2 + x_lo), y: 4, z: 8, core: 2. Of those that a mesh axis runs over, the one named last changes fastest.
Arguments:
- records: bfloat16 [4, 512, 65536], P(None, 'pair', 'tm'), may hold values from -6 to 6
- tile_blocks: int32 [2], replicated, may hold values from 0 to 3, as said below
- live_len: int32 [32], replicated, may hold values from 256 to 512, as said below
Outputs:
- correlations: float32 [512, 512, 801], P('pair', 'tm')
The draws below stay inside these ranges and needn't reach their ends.
Inputs may be any that keep to these rules, and one draw needn't show every extreme that they name: `live_len`: some segment has exactly 512 live samples. `tile_blocks`: the two blocks differ, and one of them is block 3.
All inputs are finite; a program needn't handle non-finite values.
Results may differ from the reference program's by a relative error of at most 0.0036.
Values may be sent and summed in bfloat16 or wider, within the bound.
A program may use at most 384 MiB of HBM per device.

```python
import math
import jax
import jax.numpy as jnp
from jax import lax

NBLK = 4
DECIM = 4
TAPS = 64
SEG = 512
NFT = 1024
MAXLAG = 400
SMOOTH = 4
BINS = 512
LAGS = 801
BLOCK = 512
NSEG = 32


def draw_live_len(key, part):
    values = jax.random.randint(key, (NSEG,), SEG // 2, SEG + 1).astype(jnp.int32)
    chosen = jax.random.randint(jax.random.fold_in(key, 7), (), 0, NSEG)
    return jnp.where(jnp.arange(NSEG) == chosen, SEG, values).astype(jnp.int32)


def draw_tile_blocks(key, part):
    other = jax.random.randint(jax.random.fold_in(key, 11), (), 0, NBLK - 1).astype(jnp.int32)
    flip = jax.random.randint(jax.random.fold_in(key, 13), (), 0, 2).astype(jnp.int32)
    last = jnp.array(NBLK - 1, jnp.int32)
    first = jnp.where(flip == 1, last, other)
    second = jnp.where(flip == 1, other, last)
    return jnp.stack([first, second]).astype(jnp.int32)


def block_scale(stream_key, extent, cuts, low, high):
    gain = 1.0
    for position, parts in cuts:
        steps = jax.random.uniform(jax.random.fold_in(jax.random.fold_in(stream_key, 6), position), (parts,), jnp.float32, low / len(cuts), high / len(cuts))
        gain = gain * jnp.repeat(jnp.exp(steps), extent[position] // parts).reshape((-1,) + (1,) * (len(extent) - 1 - position))
    return gain


def normal_values(own_key, dims, spread, limit, shards=(), kind=jnp.bfloat16):
    factor_of = block_scale(own_key, dims, shards, -0.22, 0.18) if shards else 1.0
    values = jax.random.normal(own_key, dims, jnp.float32) * spread * factor_of
    return jnp.minimum(jnp.maximum(values, -limit), limit).astype(kind)


def setup_inputs(seed: int = 0) -> dict:
    seeds = jax.random.split(jax.random.key(seed), 4)
    return {
        "records": normal_values(seeds[0], (NBLK, BLOCK, NSEG * DECIM * SEG), 1.0, 6.0, ((1, 8), (2, 32))),
        "tile_blocks": draw_tile_blocks(jax.random.fold_in(seeds[3], 71), 0),
        "live_len": draw_live_len(jax.random.fold_in(seeds[3], 71), 0),
    }


def lowpass():
    index = jnp.arange(TAPS).astype(jnp.float32)
    centred = (index - (TAPS - 1) / 2.0) / DECIM
    window = 0.5 * (1.0 - jnp.cos(2.0 * jnp.pi * (index + 0.5) / TAPS))
    return window * jnp.sin(jnp.pi * centred) / (jnp.pi * centred) / DECIM

def forward_table():
    sample = jnp.arange(SEG, dtype=jnp.int32)
    bins = jnp.arange(BINS, dtype=jnp.int32)
    phase = (sample[:, None] * bins[None, :] % NFT).astype(jnp.float32) * (2.0 * jnp.pi / NFT)
    return jnp.concatenate([jnp.cos(phase), -jnp.sin(phase)], axis=1)

def lag_table():
    bins = jnp.arange(BINS, dtype=jnp.int32)
    shifts = jnp.arange(LAGS, dtype=jnp.int32) - MAXLAG
    phase = (bins[:, None] * shifts[None, :] % NFT).astype(jnp.float32) * (2.0 * jnp.pi / NFT)
    weights = jnp.where(bins == 0, 1.0, 2.0).astype(jnp.float32)[:, None] / math.sqrt(NFT)
    return jnp.concatenate([weights * jnp.cos(phase), -weights * jnp.sin(phase)], axis=0)

def whiten(spectra):
    real_part = spectra[..., :BINS]
    imag_part = spectra[..., BINS:]
    amplitude = jnp.sqrt(real_part * real_part + imag_part * imag_part)
    widths = [(0, 0)] * (amplitude.ndim - 1) + [(SMOOTH, SMOOTH)]
    padded = jnp.pad(amplitude, widths)
    smooth = padded[..., 0:BINS]
    for offset in range(1, 2 * SMOOTH + 1):
        smooth = smooth + padded[..., offset:offset + BINS]
    smooth = smooth / (2 * SMOOTH + 1)
    level = smooth + 0.05 * lax.optimization_barrier(jnp.mean(amplitude, axis=-1, keepdims=True)) + 1e-06
    return (spectra / jnp.concatenate([level, level], axis=-1)).astype(jnp.bfloat16)

def decimate(block, live_len):
    stations = block.shape[0]
    record = block.astype(jnp.float32).reshape(stations, NSEG, DECIM * SEG)
    tails = record[:, :, DECIM * SEG - TAPS:]
    before = jnp.concatenate([jnp.zeros((stations, 1, TAPS), jnp.float32), tails[:, :-1]], axis=1)
    extended = jnp.concatenate([before, record], axis=2).reshape(stations, NSEG, SEG + TAPS // DECIM, DECIM)
    filter_taps = lowpass().reshape(TAPS // DECIM, DECIM)
    filtered = jnp.zeros((stations, NSEG, SEG), jnp.float32)
    for offset in range(TAPS // DECIM):
        filtered = filtered + lax.optimization_barrier(jnp.sum(extended[:, :, offset:offset + SEG, :] * filter_taps[offset], axis=-1))
    mask = (jnp.arange(SEG, dtype=jnp.int32)[None, :] < live_len[:, None]).astype(jnp.float32)
    filtered = filtered * mask[None]
    spectra = jnp.dot(filtered.reshape(stations * NSEG, SEG), forward_table(), precision=lax.Precision.HIGHEST)
    return whiten(spectra.reshape(stations, NSEG, 2 * BINS))

def reference(records, tile_blocks, live_len):
    row_block = lax.dynamic_index_in_dim(records, tile_blocks[0], 0, keepdims=False)
    col_block = lax.dynamic_index_in_dim(records, tile_blocks[1], 0, keepdims=False)
    row_white = decimate(row_block, live_len).astype(jnp.float32)
    col_white = decimate(col_block, live_len).astype(jnp.float32)
    row_real, row_imag = (row_white[..., :BINS], row_white[..., BINS:])
    col_real, col_imag = (col_white[..., :BINS], col_white[..., BINS:])
    high = lax.Precision.HIGHEST
    real_cross = jnp.einsum('igk,jgk->ijk', row_real, col_real, precision=high) + jnp.einsum('igk,jgk->ijk', row_imag, col_imag, precision=high)
    imag_cross = jnp.einsum('igk,jgk->ijk', row_imag, col_real, precision=high) - jnp.einsum('igk,jgk->ijk', row_real, col_imag, precision=high)
    stacked = jnp.concatenate([real_cross, imag_cross], axis=-1).reshape(BLOCK * BLOCK, 2 * BINS)
    lagged = jnp.dot(stacked, lag_table(), precision=high)
    return lagged.reshape(BLOCK, BLOCK, LAGS)
```

```python
import functools
import math

import jax
import jax.numpy as jnp
import ml_dtypes
import numpy as np
from jax import lax
from jax.experimental import pallas as pl
from jax.experimental.pallas import tpu as pltpu
from jax.sharding import PartitionSpec as P

DECIM = 4
TAPS = 64
SEG = 512
NFT = 1024
MAXLAG = 400
SMOOTH = 4
BINS = 512
LAGS = 801
LANE = 128
QUARTERS = 4
CHUNKS = 4
KCHUNK = LANE // CHUNKS
TWO_PI = 2.0 * math.pi / NFT
F32 = jnp.float32
BF16 = jnp.bfloat16


def split_np(table):
    high = table.astype(ml_dtypes.bfloat16)
    low = (table - high.astype(np.float64)).astype(ml_dtypes.bfloat16)
    return high, low


def filter_table():
    index = np.arange(TAPS, dtype=np.float64)
    centred = (index - (TAPS - 1) / 2.0) / DECIM
    window = 0.5 * (1.0 - np.cos(2.0 * np.pi * (index + 0.5) / TAPS))
    taps = window * np.sin(np.pi * centred) / (np.pi * centred) / DECIM
    table = np.zeros((5 * LANE, LANE))
    for j in range(LANE):
        table[TAPS + DECIM * j : 2 * TAPS + DECIM * j, j] = taps
    high, low = split_np(table)
    return np.concatenate([high, low], axis=1)


def turn_tables():
    sample = np.arange(SEG)
    coarse = (8 * np.arange(BINS // 8))[:, None] * sample[None, :] % NFT
    fine = np.arange(8)[:, None] * sample[None, :] % NFT
    pick = lambda fn, phase: fn(phase * TWO_PI).astype(np.float32)
    return (
        pick(np.cos, coarse),
        pick(np.sin, coarse),
        pick(np.cos, fine),
        pick(np.sin, fine),
    )


def bin_order():
    chunk = np.arange(CHUNKS)[:, None, None]
    quarter = np.arange(QUARTERS)[None, :, None]
    inner = np.arange(KCHUNK)[None, None, :]
    return (quarter * LANE + chunk * KCHUNK + inner).reshape(-1)


def lag_table():
    bins = bin_order()
    shifts = np.arange(LAGS) - MAXLAG
    phase = (bins[:, None] * shifts[None, :] % NFT) * TWO_PI
    weights = np.where(bins == 0, 1.0, 2.0)[:, None] / math.sqrt(NFT)
    table = np.concatenate([weights * np.cos(phase), -weights * np.sin(phase)], axis=0)
    return table.astype(ml_dtypes.bfloat16)


def split(value):
    high = value.astype(BF16)
    return high, (value - high.astype(F32)).astype(BF16)


def dot(a, b, dims=((1,), (0,))):
    return lax.dot_general(a, b, (dims, ((), ())), preferred_element_type=F32)


def prepare_kernel(
    blocks, live, row_ref, col_ref, row_tail, col_tail, taps_ref,
    coarse_cos, coarse_sin, fine_cos, fine_sin,
    row_out, col_out, fwd_high, fwd_low, padded,
):
    del blocks
    fc, fs = fine_cos[...], fine_sin[...]
    for a in range(BINS // 8):
        cc = coarse_cos[a : a + 1, :]
        cs = coarse_sin[a : a + 1, :]
        rows = slice(8 * a, 8 * a + 8)
        for value, base in ((cc * fc - cs * fs, 0), (-(cs * fc + cc * fs), BINS)):
            high, low = split(value)
            fwd_high[base + rows.start : base + rows.stop, :] = high
            fwd_low[base + rows.start : base + rows.stop, :] = low

    record = jnp.concatenate([row_ref[0], col_ref[0]], axis=0)
    tail = jnp.concatenate([row_tail[0], col_tail[0]], axis=0)
    count = live[0]
    lane = lax.broadcasted_iota(jnp.int32, (1, LANE), 1)
    pieces = []
    for b in range(SEG // LANE):
        span = DECIM * LANE
        before = tail if b == 0 else record[:, b * span - LANE : b * span]
        both = dot(before, taps_ref[:LANE, :]) + dot(
            record[:, b * span : (b + 1) * span], taps_ref[LANE:, :]
        )
        value = both[:, :LANE] + both[:, LANE:]
        pieces.append(jnp.where(lane + b * LANE < count, value, 0.0))
    filtered = jnp.concatenate(pieces, axis=1)
    high, low = split(filtered)
    last = ((1,), (1,))
    spectra = (
        dot(fwd_high[...], low, last)
        + dot(fwd_low[...], high, last)
        + dot(fwd_high[...], high, last)
    )
    real, imag = spectra[:BINS], spectra[BINS:]
    amplitude = jnp.sqrt(real * real + imag * imag)
    padded[0:8, :] = jnp.zeros((8, LANE), F32)
    padded[8 + BINS : 16 + BINS, :] = jnp.zeros((8, LANE), F32)
    padded[8 : 8 + BINS, :] = amplitude
    smooth = padded[8 - SMOOTH : 8 - SMOOTH + BINS, :]
    for offset in range(1, 2 * SMOOTH + 1):
        start = 8 - SMOOTH + offset
        smooth = smooth + padded[start : start + BINS, :]
    mean = jnp.sum(amplitude, axis=0, keepdims=True) * (1.0 / BINS)
    level = smooth * (1.0 / (2 * SMOOTH + 1)) + 0.05 * mean + 1e-06
    inverse = 1.0 / level
    real = real * inverse
    imag = imag * inverse
    half = LANE // 2
    lower = lax.broadcasted_iota(jnp.int32, (BINS, LANE), 1) < half
    row_out[...] = jnp.where(lower, real, pltpu.roll(imag, half, 1)).astype(BF16)
    cols = jnp.where(lower, pltpu.roll(real, half, 1), imag)
    lanes = lax.broadcasted_iota(jnp.int32, (LANE, LANE), 1)
    for j in range(4):
        total = jnp.zeros((LANE, LANE), F32)
        for quarter in range(QUARTERS):
            part = cols[quarter * LANE : (quarter + 1) * LANE, :]
            for c in range(2):
                source = c * half + 16 * j
                target = quarter * 32 + 16 * c
                moved = part
                if (target - source) % LANE:
                    moved = pltpu.roll(part, (target - source) % LANE, 1)
                keep = (lanes >= target) & (lanes < target + 16)
                total = jnp.where(keep, moved, total)
        col_out[j] = total.astype(BF16)


def prepare(records, tails, tile_blocks, live):
    stations, length = records.shape[1], records.shape[2]
    whole = lambda *shape: pl.BlockSpec(shape, lambda i, b, l: (0,) * len(shape))
    taps = jnp.asarray(filter_table())
    tables = [jnp.asarray(table) for table in turn_tables()]
    return pl.pallas_call(
        prepare_kernel,
        grid_spec=pltpu.PrefetchScalarGridSpec(
            num_scalar_prefetch=2,
            grid=(1,),
            in_specs=[
                pl.BlockSpec((1, stations, length), lambda i, b, l: (b[0], 0, 0)),
                pl.BlockSpec((1, stations, length), lambda i, b, l: (b[1], 0, 0)),
                pl.BlockSpec((1, stations, LANE), lambda i, b, l: (b[0], 0, 0)),
                pl.BlockSpec((1, stations, LANE), lambda i, b, l: (b[1], 0, 0)),
                whole(5 * LANE, 2 * LANE),
                whole(BINS // 8, SEG),
                whole(BINS // 8, SEG),
                whole(8, SEG),
                whole(8, SEG),
            ],
            out_specs=[whole(BINS, LANE), whole(4, LANE, LANE)],
            scratch_shapes=[
                pltpu.VMEM((2 * BINS, SEG), BF16),
                pltpu.VMEM((2 * BINS, SEG), BF16),
                pltpu.VMEM((BINS + 16, LANE), F32),
            ],
        ),
        out_shape=[
            jax.ShapeDtypeStruct((BINS, LANE), BF16),
            jax.ShapeDtypeStruct((4, LANE, LANE), BF16),
        ],
        compiler_params=pltpu.CompilerParams(vmem_limit_bytes=40 << 20),
        name="prepare",
    )(tile_blocks, live, records, records, tails, tails, taps, *tables)


def correlate_kernel(segments, row_ref, col_ref, lag_ref, out_ref, rows, cols, cross, stacked):
    step = pl.program_id(0)
    half = LANE // 2
    group = 8
    count_k = QUARTERS * KCHUNK

    @pl.when(step < CHUNKS)
    def _():
        rows[...] = row_ref[...].reshape(segments * count_k, LANE).astype(F32)
        cols[...] = col_ref[...].reshape(segments * KCHUNK, LANE).astype(F32)
        lane = lax.broadcasted_iota(jnp.int32, (32, group * segments), 1)
        sign = jnp.where(
            lax.broadcasted_iota(jnp.int32, (1, LANE), 1) < half, 1.0, -1.0
        ).astype(F32)
        for block in range(KCHUNK // group):
            gathered = jnp.concatenate(
                [
                    cols[pl.ds(block * group + b, segments, stride=KCHUNK), :]
                    for b in range(group)
                ],
                axis=0,
            )
            turned = gathered.T.astype(BF16)
            for quarter in range(QUARTERS):
                left = turned[quarter * 32 : quarter * 32 + 32, :]
                zero = jnp.zeros_like(left)
                wide = jnp.concatenate(
                    [
                        jnp.where(
                            (lane >= b * segments) & (lane < (b + 1) * segments), left, zero
                        )
                        for b in range(group)
                    ],
                    axis=0,
                )
                base = quarter * KCHUNK + block * group
                right = jnp.concatenate(
                    [
                        rows[pl.ds(base + b, segments, stride=count_k), :]
                        for b in range(group)
                    ],
                    axis=0,
                ).astype(BF16)
                product = dot(wide, right)
                for b in range(group):
                    top = product[b * 32 : b * 32 + 16, :]
                    low = product[b * 32 + 16 : b * 32 + 32, :]
                    value = top + sign * pltpu.roll(low, half, 1)
                    cross[pl.ds(base + b, 16, stride=count_k), :] = value
        for q in range(16):
            turned = cross[q * count_k : (q + 1) * count_k, :].T.astype(BF16)
            for chunk in range(CHUNKS):

                @pl.when(step == chunk)
                def _():
                    at = chunk * count_k
                    stacked[q * half : (q + 1) * half, at : at + count_k] = turned[:half]
                    stacked[q * half : (q + 1) * half, BINS + at : BINS + at + count_k] = turned[half:]

    @pl.when(step >= CHUNKS)
    def _():
        for q in range(16):
            value = dot(stacked[q * half : (q + 1) * half, :], lag_ref[...])
            out_ref[pl.ds(q, half, stride=16), :] = value


def correlate(row_all, col_all):
    segments = row_all.shape[0]
    row_all = row_all.reshape(segments, QUARTERS, LANE, LANE)
    table = lag_table()
    width = LANE
    tiles = -(-LAGS // width)
    table = jnp.asarray(np.pad(table, ((0, 0), (0, tiles * width - LAGS))))
    pairs = 16 * (LANE // 2)

    body = functools.partial(correlate_kernel, segments)
    return pl.pallas_call(
        body,
        grid=(CHUNKS + tiles,),
        in_specs=[
            pl.BlockSpec(
                (segments, QUARTERS, KCHUNK, LANE),
                lambda i: (0, 0, jnp.minimum(i, CHUNKS - 1), 0),
            ),
            pl.BlockSpec(
                (segments, KCHUNK, LANE), lambda i: (0, jnp.minimum(i, CHUNKS - 1), 0)
            ),
            pl.BlockSpec((2 * BINS, width), lambda i: (0, jnp.maximum(i - CHUNKS, 0))),
        ],
        out_specs=pl.BlockSpec((pairs, width), lambda i: (0, jnp.maximum(i - CHUNKS, 0))),
        out_shape=jax.ShapeDtypeStruct((pairs, LAGS), F32),
        scratch_shapes=[
            pltpu.VMEM((segments * QUARTERS * KCHUNK, LANE), F32),
            pltpu.VMEM((segments * KCHUNK, LANE), F32),
            pltpu.VMEM((16 * QUARTERS * KCHUNK, LANE), F32),
            pltpu.VMEM((pairs, 2 * BINS), BF16),
        ],
        compiler_params=pltpu.CompilerParams(vmem_limit_bytes=48 << 20),
        name="correlate",
    )(row_all, col_all, table)


def shards(records, tile_blocks, live_len):
    length = records.shape[2]
    size = lax.axis_size("tm")
    tails = lax.ppermute(
        records[:, :, length - LANE :], "tm", [(i, i + 1) for i in range(size - 1)]
    )
    live = lax.dynamic_slice(live_len, (lax.axis_index("tm"),), (1,))
    row_own, col_own = prepare(records, tails, tile_blocks, live)
    row_all = lax.all_gather(row_own, "tm", axis=0)
    col_rows = lax.all_gather(col_own, "pair", axis=0, tiled=True)
    col_all = lax.all_to_all(col_rows, "tm", split_axis=0, concat_axis=0, tiled=True)
    result = correlate(row_all, col_all)
    return result.reshape(LANE // 2, 16, LAGS)


def solution(mesh):
    placed = (P(None, "pair", "tm"), P(), P())
    return jax.shard_map(
        shards, mesh=mesh, in_specs=placed, out_specs=P("pair", "tm", None), check_vma=False
    )
```

```python
import functools
import math

import jax
import jax.numpy as jnp
import ml_dtypes
import numpy as np
from jax import lax
from jax.experimental import pallas as pl
from jax.experimental.pallas import tpu as pltpu
from jax.sharding import PartitionSpec as P

DECIM = 4
TAPS = 64
SEG = 512
NFT = 1024
MAXLAG = 400
SMOOTH = 4
BINS = 512
LAGS = 801
LANE = 128
QUARTERS = 4
CHUNKS = 4
KCHUNK = LANE // CHUNKS
TWO_PI = 2.0 * math.pi / NFT
F32 = jnp.float32
BF16 = jnp.bfloat16
MESH = pl.DeviceIdType.MESH
RING = 8
YRING = 4
OFFSETS = (0, 1, -1, 2, -2, 3, -3, 4)


def split_np(table):
    high = table.astype(ml_dtypes.bfloat16)
    low = (table - high.astype(np.float64)).astype(ml_dtypes.bfloat16)
    return high, low


def filter_table():
    index = np.arange(TAPS, dtype=np.float64)
    centred = (index - (TAPS - 1) / 2.0) / DECIM
    window = 0.5 * (1.0 - np.cos(2.0 * np.pi * (index + 0.5) / TAPS))
    taps = window * np.sin(np.pi * centred) / (np.pi * centred) / DECIM
    table = np.zeros((5 * LANE, LANE))
    for j in range(LANE):
        table[TAPS + DECIM * j : 2 * TAPS + DECIM * j, j] = taps
    high, low = split_np(table)
    return np.concatenate([high, low], axis=1)


def turn_tables():
    sample = np.arange(SEG)
    coarse = (8 * np.arange(BINS // 8))[:, None] * sample[None, :] % NFT
    fine = np.arange(8)[:, None] * sample[None, :] % NFT
    pick = lambda fn, phase: fn(phase * TWO_PI).astype(np.float32)
    return (
        pick(np.cos, coarse),
        pick(np.sin, coarse),
        pick(np.cos, fine),
        pick(np.sin, fine),
    )


def bin_order():
    chunk = np.arange(CHUNKS)[:, None, None]
    quarter = np.arange(QUARTERS)[None, :, None]
    inner = np.arange(KCHUNK)[None, None, :]
    return (quarter * LANE + chunk * KCHUNK + inner).reshape(-1)


def lag_table():
    bins = bin_order()
    shifts = np.arange(LAGS) - MAXLAG
    phase = (bins[:, None] * shifts[None, :] % NFT) * TWO_PI
    weights = np.where(bins == 0, 1.0, 2.0)[:, None] / math.sqrt(NFT)
    table = np.concatenate([weights * np.cos(phase), -weights * np.sin(phase)], axis=0)
    return table.astype(ml_dtypes.bfloat16)


def split(value):
    high = value.astype(BF16)
    return high, (value - high.astype(F32)).astype(BF16)


def dot(a, b, dims=((1,), (0,))):
    return lax.dot_general(a, b, (dims, ((), ())), preferred_element_type=F32)


def prepare_kernel(
    blocks, live, row_ref, col_ref, row_tail, col_tail, taps_ref,
    coarse_cos, coarse_sin, fine_cos, fine_sin,
    row_out, col_out, fwd_high, fwd_low, padded,
):
    del blocks
    fc, fs = fine_cos[...], fine_sin[...]
    for a in range(BINS // 8):
        cc = coarse_cos[a : a + 1, :]
        cs = coarse_sin[a : a + 1, :]
        rows = slice(8 * a, 8 * a + 8)
        for value, base in ((cc * fc - cs * fs, 0), (-(cs * fc + cc * fs), BINS)):
            high, low = split(value)
            fwd_high[base + rows.start : base + rows.stop, :] = high
            fwd_low[base + rows.start : base + rows.stop, :] = low

    record = jnp.concatenate([row_ref[0], col_ref[0]], axis=0)
    tail = jnp.concatenate([row_tail[0], col_tail[0]], axis=0)
    count = live[0]
    lane = lax.broadcasted_iota(jnp.int32, (1, LANE), 1)
    pieces = []
    for b in range(SEG // LANE):
        span = DECIM * LANE
        before = tail if b == 0 else record[:, b * span - LANE : b * span]
        both = dot(before, taps_ref[:LANE, :]) + dot(
            record[:, b * span : (b + 1) * span], taps_ref[LANE:, :]
        )
        value = both[:, :LANE] + both[:, LANE:]
        pieces.append(jnp.where(lane + b * LANE < count, value, 0.0))
    filtered = jnp.concatenate(pieces, axis=1)
    high, low = split(filtered)
    last = ((1,), (1,))
    spectra = (
        dot(fwd_high[...], low, last)
        + dot(fwd_low[...], high, last)
        + dot(fwd_high[...], high, last)
    )
    real, imag = spectra[:BINS], spectra[BINS:]
    amplitude = jnp.sqrt(real * real + imag * imag)
    padded[0:8, :] = jnp.zeros((8, LANE), F32)
    padded[8 + BINS : 16 + BINS, :] = jnp.zeros((8, LANE), F32)
    padded[8 : 8 + BINS, :] = amplitude
    smooth = padded[8 - SMOOTH : 8 - SMOOTH + BINS, :]
    for offset in range(1, 2 * SMOOTH + 1):
        start = 8 - SMOOTH + offset
        smooth = smooth + padded[start : start + BINS, :]
    mean = jnp.sum(amplitude, axis=0, keepdims=True) * (1.0 / BINS)
    level = smooth * (1.0 / (2 * SMOOTH + 1)) + 0.05 * mean + 1e-06
    inverse = 1.0 / level
    real = real * inverse
    imag = imag * inverse
    half = LANE // 2
    lower = lax.broadcasted_iota(jnp.int32, (BINS, LANE), 1) < half
    row_out[...] = jnp.where(lower, real, pltpu.roll(imag, half, 1)).astype(BF16)
    cols = jnp.where(lower, pltpu.roll(real, half, 1), imag)
    lanes = lax.broadcasted_iota(jnp.int32, (LANE, LANE), 1)
    for j in range(4):
        total = jnp.zeros((LANE, LANE), F32)
        for quarter in range(QUARTERS):
            part = cols[quarter * LANE : (quarter + 1) * LANE, :]
            for c in range(2):
                source = c * half + 16 * j
                target = quarter * 32 + 16 * c
                moved = part
                if (target - source) % LANE:
                    moved = pltpu.roll(part, (target - source) % LANE, 1)
                keep = (lanes >= target) & (lanes < target + 16)
                total = jnp.where(keep, moved, total)
        col_out[j] = total.astype(BF16)


def prepare(records, tails, tile_blocks, live):
    stations, length = records.shape[1], records.shape[2]
    whole = lambda *shape: pl.BlockSpec(shape, lambda i, b, l: (0,) * len(shape))
    taps = jnp.asarray(filter_table())
    tables = [jnp.asarray(table) for table in turn_tables()]
    return pl.pallas_call(
        prepare_kernel,
        grid_spec=pltpu.PrefetchScalarGridSpec(
            num_scalar_prefetch=2,
            grid=(1,),
            in_specs=[
                pl.BlockSpec((1, stations, length), lambda i, b, l: (b[0], 0, 0)),
                pl.BlockSpec((1, stations, length), lambda i, b, l: (b[1], 0, 0)),
                pl.BlockSpec((1, stations, LANE), lambda i, b, l: (b[0], 0, 0)),
                pl.BlockSpec((1, stations, LANE), lambda i, b, l: (b[1], 0, 0)),
                whole(5 * LANE, 2 * LANE),
                whole(BINS // 8, SEG),
                whole(BINS // 8, SEG),
                whole(8, SEG),
                whole(8, SEG),
            ],
            out_specs=[whole(BINS, LANE), whole(4, LANE, LANE)],
            scratch_shapes=[
                pltpu.VMEM((2 * BINS, SEG), BF16),
                pltpu.VMEM((2 * BINS, SEG), BF16),
                pltpu.VMEM((BINS + 16, LANE), F32),
            ],
        ),
        out_shape=[
            jax.ShapeDtypeStruct((BINS, LANE), BF16),
            jax.ShapeDtypeStruct((4, LANE, LANE), BF16),
        ],
        compiler_params=pltpu.CompilerParams(vmem_limit_bytes=40 << 20),
        name="prepare",
    )(tile_blocks, live, records, records, tails, tails, taps, *tables)


class Place:
    def __init__(self):
        pair, tm = lax.axis_index("pair"), lax.axis_index("tm")
        self.y, self.xl = pair // 2, lax.rem(pair, 2)
        self.xh, self.z, self.c = tm // 16, lax.rem(tm // 2, RING), lax.rem(tm, 2)

    def at(self, y=None, xl=None, xh=None, z=None, c=None):
        pick = lambda new, old: old if new is None else new
        y, xl, xh = pick(y, self.y), pick(xl, self.xl), pick(xh, self.xh)
        z, c = pick(z, self.z), pick(c, self.c)
        return {"pair": y * 2 + xl, "tm": xh * 16 + z * 2 + c}


def slot_of(xh, c, z):
    return xh * 16 + c * RING + z


def schedule():
    events = []
    for i, base in enumerate((1.5, 3.5, 3.6, 6.5, 6.6, 9.5, 9.6, 12.5)):
        events.append((base, "root", i))
        events.append((base + 2.0, "other", i))
        events.append((base + 4.0, "near", i))
        events.append((base + 7.0, "chain", i))
    for d in range(1, 5):
        events.append((1.0 + 4.6 * d, "row", (0, d)))
        events.append((3.0 + 4.6 * d, "row", (1, d)))
    events.append((2.9, "opposite", None))
    events.sort(key=lambda e: e[0])
    return [(kind, arg) for _, kind, arg in events]


def exchange_kernel(
    row_ref, col_ref, row_all, col_all, stage,
    row_send, row_recv, stage_send, stage_recv, col_send, col_recv, local_sem,
):
    me = Place()
    half_rows = BINS // 2
    group_xh = me.y // 2
    home_y = me.xh * 2 + me.z // 4
    home_xl = lax.rem(me.z // 2, 2)
    dy = lax.rem(me.y - home_y + YRING, YRING)
    root_pair = lax.rem(me.y, 2) * 2 + me.xl
    is_root = (me.z // 2) == root_pair
    is_near = is_root & (me.xh == group_xh)
    is_far = is_root & (me.xh != group_xh)
    is_other = (dy == 0) & (me.xl != home_xl)
    up, down = lax.rem(me.y + 1, YRING), lax.rem(me.y + YRING - 1, YRING)
    right, left = lax.rem(me.z + 1, RING), lax.rem(me.z + RING - 1, RING)

    barrier = pltpu.get_barrier_semaphore()

    def greet(device):
        pl.semaphore_signal(barrier, inc=1, device_id=device, device_id_type=MESH)

    for step in range(1, 2 * RING):
        other = lax.rem(me.z * 2 + me.c + step, 2 * RING)
        greet(me.at(z=other // 2, c=lax.rem(other, 2)))
    greet(me.at(xh=1 - me.xh))
    greet(me.at(xl=1 - me.xl))
    greet(me.at(xh=1 - me.xh, xl=1 - me.xl))
    greet(me.at(y=up))
    greet(me.at(y=down))
    pl.semaphore_wait(barrier, 2 * RING - 1 + 5)

    def remote(src, dst, send, recv, device):
        return pltpu.make_async_remote_copy(
            src_ref=src, dst_ref=dst, send_sem=send, recv_sem=recv,
            device_id=device, device_id_type=MESH,
        )

    pending = []

    def start(copy, when=None):
        if when is None:
            copy.start()
        else:
            pl.when(when)(copy.start)
        pending.append((copy, when))

    for j in range(4):
        root_z, root_c = root_pair * 2 + j // 2, j % 2
        mine = (me.z == root_z) & (me.c == root_c)
        index = me.c * RING + me.z
        copy = remote(
            col_ref.at[j], stage.at[index], stage_send.at[j], stage_recv.at[index],
            me.at(z=root_z, c=root_c),
        )
        start(copy, jnp.logical_not(mine))

        @pl.when(mine)
        def _():
            pltpu.make_async_copy(col_ref.at[j], stage.at[index], stage_recv.at[index]).start()

    own = slot_of(me.xh, me.c, me.z)
    own_local = pltpu.make_async_copy(row_ref, row_all.at[own], local_sem.at[16])
    start(
        remote(row_ref, row_all.at[own], row_send.at[32], row_recv.at[own, 0], me.at(xh=1 - me.xh))
    )

    def spread(source, slot, h, d, direction):
        base = h * 16
        for sign, target, offset in ((1, right, 0), (-1, left, 4)):
            if direction not in (0, sign) or d > 3:
                continue
            send = row_send.at[base + offset + d]
            device = me.at(z=target)
            if d < 3:
                start(remote(source, row_all.at[slot], send, row_recv.at[slot, 0], device))
            else:
                part = 0 if sign == 1 else 1
                rows = pl.ds(part * half_rows, half_rows)
                start(
                    remote(
                        source.at[rows], row_all.at[slot, rows], send,
                        row_recv.at[slot, part], device,
                    )
                )
        number = 15 if d == 4 else 8 + (d + 3 if direction == -1 else d)
        start(
            remote(
                source, row_all.at[slot], row_send.at[base + number],
                row_recv.at[slot, 0], me.at(c=1 - me.c),
            )
        )

    def got_row(slot, part=None):
        if part is None:
            ref = row_all.at[slot]
        else:
            ref = row_all.at[slot, pl.ds(part * half_rows, half_rows)]
        remote(ref, ref, row_send.at[0], row_recv.at[slot, part or 0], me.at()).wait_recv()

    def got_col(slot):
        ref = col_all.at[slot]
        remote(ref, ref, col_send.at[0, 0], col_recv.at[slot], me.at()).wait_recv()

    spread(row_ref, own, 0, 0, 0)
    own_local.start()

    def zpiece(i):
        return lax.rem(me.z + OFFSETS[i] + RING, RING)

    def along(source, slot, c, when):
        start(
            remote(
                source, col_all.at[slot], col_send.at[slot, 1], col_recv.at[slot],
                me.at(y=up if c == 0 else down),
            ),
            when,
        )

    for kind, arg in schedule():
        if kind == "opposite":
            slot = slot_of(1 - me.xh, me.c, me.z)
            got_row(slot)
            spread(row_all.at[slot], slot, 1, 0, 0)
        elif kind == "row":
            h, d = arg
            xh = me.xh if h == 0 else 1 - me.xh
            if d < 4:
                for sign in (1, -1):
                    slot = slot_of(xh, me.c, lax.rem(me.z - sign * d + RING, RING))
                    got_row(slot)
                    spread(row_all.at[slot], slot, h, d, sign)
            else:
                slot = slot_of(xh, me.c, lax.rem(me.z + 4, RING))
                got_row(slot, 0)
                got_row(slot, 1)
                spread(row_all.at[slot], slot, h, d, 1)
        elif kind == "root":
            for c in range(2):
                index = c * RING + zpiece(arg)
                slot = slot_of(me.xh, c, zpiece(arg))

                @pl.when(is_root)
                def _():
                    pltpu.make_async_copy(
                        stage.at[index], stage.at[index], stage_recv.at[index]
                    ).wait()

                @pl.when(is_near)
                def _():
                    pltpu.make_async_copy(
                        stage.at[index], col_all.at[slot], local_sem.at[2 * arg + c]
                    ).start()

                start(
                    remote(
                        stage.at[index], col_all.at[slot], col_send.at[slot, 0],
                        col_recv.at[slot], me.at(xl=1 - me.xl),
                    ),
                    is_near,
                )
                start(
                    remote(
                        stage.at[index], col_all.at[slot], col_send.at[slot, 0],
                        col_recv.at[slot], me.at(xl=1 - me.xl, xh=1 - me.xh),
                    ),
                    is_far,
                )
                along(stage.at[index], slot, c, is_near)
        elif kind == "other":
            for far in (0, 1):
                xh = 1 - me.xh if far else me.xh
                for c in range(2):
                    slot = slot_of(xh, c, zpiece(arg))
                    pl.when(is_other)(lambda slot=slot: got_col(slot))
                    if far:
                        start(
                            remote(
                                col_all.at[slot], col_all.at[slot], col_send.at[slot, 0],
                                col_recv.at[slot], me.at(xl=1 - me.xl),
                            ),
                            is_other,
                        )
                    along(col_all.at[slot], slot, c, is_other)
        elif kind == "near":
            for c in range(2):
                slot = slot_of(1 - me.xh, c, zpiece(arg))
                pl.when(is_near)(lambda slot=slot: got_col(slot))
                along(col_all.at[slot], slot, c, is_near)
        elif kind == "chain":
            for far in (0, 1):
                xh = 1 - me.xh if far else me.xh
                first = slot_of(xh, 0, zpiece(arg))
                second = slot_of(xh, 1, zpiece(arg))

                @pl.when(dy == 3)
                def _():
                    got_col(second)

                along(col_all.at[second], second, 1, dy == 3)

                @pl.when(dy != 0)
                def _():
                    got_col(first)

                along(col_all.at[first], first, 0, (dy == 1) | (dy == 2))

                @pl.when((dy == 1) | (dy == 2))
                def _():
                    got_col(second)

                along(col_all.at[second], second, 1, dy == 2)

    for h in range(2):
        for z in range(RING):
            got_row(slot_of(h, 1 - me.c, z))
    own_local.wait()
    for i in range(RING):
        for c in range(2):
            index = c * RING + zpiece(i)
            slot = slot_of(me.xh, c, zpiece(i))

            @pl.when(is_near)
            def _():
                pltpu.make_async_copy(
                    stage.at[index], col_all.at[slot], local_sem.at[2 * i + c]
                ).wait()

    for copy, when in pending:
        if when is None:
            copy.wait_send()
        else:
            pl.when(when)(copy.wait_send)


def exchange(row_own, col_own):
    anywhere = pl.BlockSpec(memory_space=pl.ANY)
    dma = pltpu.SemaphoreType.DMA
    return pl.pallas_call(
        exchange_kernel,
        in_specs=[anywhere, anywhere],
        out_specs=[anywhere, anywhere],
        out_shape=[
            jax.ShapeDtypeStruct((32,) + row_own.shape, BF16),
            jax.ShapeDtypeStruct((32,) + col_own.shape[1:], BF16),
        ],
        scratch_shapes=[
            pltpu.VMEM((2 * RING,) + col_own.shape[1:], BF16),
            dma((33,)), dma((32, 2)), dma((4,)), dma((2 * RING,)),
            dma((32, 2)), dma((32,)), dma((17,)),
        ],
        compiler_params=pltpu.CompilerParams(collective_id=0, has_side_effects=True),
        name="exchange",
    )(row_own, col_own)


def correlate_kernel(segments, row_ref, col_ref, lag_ref, out_ref, rows, cols, cross, stacked):
    step = pl.program_id(0)
    half = LANE // 2
    group = 8
    count_k = QUARTERS * KCHUNK

    @pl.when(step < CHUNKS)
    def _():
        rows[...] = row_ref[...].reshape(segments * count_k, LANE).astype(F32)
        cols[...] = col_ref[...].reshape(segments * KCHUNK, LANE).astype(F32)
        lane = lax.broadcasted_iota(jnp.int32, (32, group * segments), 1)
        sign = jnp.where(
            lax.broadcasted_iota(jnp.int32, (1, LANE), 1) < half, 1.0, -1.0
        ).astype(F32)
        for block in range(KCHUNK // group):
            gathered = jnp.concatenate(
                [
                    cols[pl.ds(block * group + b, segments, stride=KCHUNK), :]
                    for b in range(group)
                ],
                axis=0,
            )
            turned = gathered.T.astype(BF16)
            for quarter in range(QUARTERS):
                left = turned[quarter * 32 : quarter * 32 + 32, :]
                zero = jnp.zeros_like(left)
                wide = jnp.concatenate(
                    [
                        jnp.where(
                            (lane >= b * segments) & (lane < (b + 1) * segments), left, zero
                        )
                        for b in range(group)
                    ],
                    axis=0,
                )
                base = quarter * KCHUNK + block * group
                right = jnp.concatenate(
                    [
                        rows[pl.ds(base + b, segments, stride=count_k), :]
                        for b in range(group)
                    ],
                    axis=0,
                ).astype(BF16)
                product = dot(wide, right)
                for b in range(group):
                    top = product[b * 32 : b * 32 + 16, :]
                    low = product[b * 32 + 16 : b * 32 + 32, :]
                    value = top + sign * pltpu.roll(low, half, 1)
                    cross[pl.ds(base + b, 16, stride=count_k), :] = value
        for q in range(16):
            turned = cross[q * count_k : (q + 1) * count_k, :].T.astype(BF16)
            for chunk in range(CHUNKS):

                @pl.when(step == chunk)
                def _():
                    at = chunk * count_k
                    stacked[q * half : (q + 1) * half, at : at + count_k] = turned[:half]
                    stacked[q * half : (q + 1) * half, BINS + at : BINS + at + count_k] = turned[half:]

    @pl.when(step >= CHUNKS)
    def _():
        for q in range(16):
            value = dot(stacked[q * half : (q + 1) * half, :], lag_ref[...])
            out_ref[pl.ds(q, half, stride=16), :] = value


def correlate(row_all, col_all):
    segments = row_all.shape[0]
    row_all = row_all.reshape(segments, QUARTERS, LANE, LANE)
    table = lag_table()
    width = LANE
    tiles = -(-LAGS // width)
    table = jnp.asarray(np.pad(table, ((0, 0), (0, tiles * width - LAGS))))
    pairs = 16 * (LANE // 2)

    body = functools.partial(correlate_kernel, segments)
    return pl.pallas_call(
        body,
        grid=(CHUNKS + tiles,),
        in_specs=[
            pl.BlockSpec(
                (segments, QUARTERS, KCHUNK, LANE),
                lambda i: (0, 0, jnp.minimum(i, CHUNKS - 1), 0),
            ),
            pl.BlockSpec(
                (segments, KCHUNK, LANE), lambda i: (0, jnp.minimum(i, CHUNKS - 1), 0)
            ),
            pl.BlockSpec((2 * BINS, width), lambda i: (0, jnp.maximum(i - CHUNKS, 0))),
        ],
        out_specs=pl.BlockSpec((pairs, width), lambda i: (0, jnp.maximum(i - CHUNKS, 0))),
        out_shape=jax.ShapeDtypeStruct((pairs, LAGS), F32),
        scratch_shapes=[
            pltpu.VMEM((segments * QUARTERS * KCHUNK, LANE), F32),
            pltpu.VMEM((segments * KCHUNK, LANE), F32),
            pltpu.VMEM((16 * QUARTERS * KCHUNK, LANE), F32),
            pltpu.VMEM((pairs, 2 * BINS), BF16),
        ],
        compiler_params=pltpu.CompilerParams(vmem_limit_bytes=48 << 20),
        name="correlate",
    )(row_all, col_all, table)


def shards(records, tile_blocks, live_len):
    length = records.shape[2]
    size = lax.axis_size("tm")
    tails = lax.ppermute(
        records[:, :, length - LANE :], "tm", [(i, i + 1) for i in range(size - 1)]
    )
    live = lax.dynamic_slice(live_len, (lax.axis_index("tm"),), (1,))
    row_own, col_own = prepare(records, tails, tile_blocks, live)
    row_all, col_all = exchange(row_own, col_own)
    result = correlate(row_all, col_all)
    return result.reshape(LANE // 2, 16, LAGS)


def solution(mesh):
    placed = (P(None, "pair", "tm"), P(), P())
    return jax.shard_map(
        shards, mesh=mesh, in_specs=placed, out_specs=P("pair", "tm", None), check_vma=False
    )
```

```python
import functools
import math

import jax
import jax.numpy as jnp
import ml_dtypes
import numpy as np
from jax import lax
from jax.experimental import pallas as pl
from jax.experimental.pallas import tpu as pltpu
from jax.sharding import PartitionSpec as P

DECIM = 4
TAPS = 64
SEG = 512
NFT = 1024
MAXLAG = 400
SMOOTH = 4
BINS = 512
LAGS = 801
LANE = 128
QUARTERS = 4
CHUNKS = 4
KCHUNK = LANE // CHUNKS
TWO_PI = 2.0 * math.pi / NFT
F32 = jnp.float32
BF16 = jnp.bfloat16
MESH = pl.DeviceIdType.MESH
RING = 8
YRING = 4
OFFSETS = (0, 1, -1, 2, -2, 3, -3, 4)
PARTS = 2
OPP_TIME = 3.0
ROW_START, ROW_STEP = 5.0, 5.0
COL_STEP = 1.5
COL_TIMES = (
    ("root", 1.5),
    ("other", 8.0),
    ("near", 10.5),
    ("hop1", 13.0),
    ("hop2", 16.0),
    ("last", 40.0),
)


def split_np(table):
    high = table.astype(ml_dtypes.bfloat16)
    low = (table - high.astype(np.float64)).astype(ml_dtypes.bfloat16)
    return high, low


def filter_table():
    index = np.arange(TAPS, dtype=np.float64)
    centred = (index - (TAPS - 1) / 2.0) / DECIM
    window = 0.5 * (1.0 - np.cos(2.0 * np.pi * (index + 0.5) / TAPS))
    taps = window * np.sin(np.pi * centred) / (np.pi * centred) / DECIM
    table = np.zeros((5 * LANE, LANE))
    for j in range(LANE):
        table[TAPS + DECIM * j : 2 * TAPS + DECIM * j, j] = taps
    high, low = split_np(table)
    return np.concatenate([high, low], axis=1)


def turn_tables():
    sample = np.arange(SEG)
    coarse = (8 * np.arange(BINS // 8))[:, None] * sample[None, :] % NFT
    fine = np.arange(8)[:, None] * sample[None, :] % NFT
    pick = lambda fn, phase: fn(phase * TWO_PI).astype(np.float32)
    return (
        pick(np.cos, coarse),
        pick(np.sin, coarse),
        pick(np.cos, fine),
        pick(np.sin, fine),
    )


def bin_order():
    chunk = np.arange(CHUNKS)[:, None, None]
    quarter = np.arange(QUARTERS)[None, :, None]
    inner = np.arange(KCHUNK)[None, None, :]
    return (quarter * LANE + chunk * KCHUNK + inner).reshape(-1)


def lag_table():
    bins = bin_order()
    shifts = np.arange(LAGS) - MAXLAG
    phase = (bins[:, None] * shifts[None, :] % NFT) * TWO_PI
    weights = np.where(bins == 0, 1.0, 2.0)[:, None] / math.sqrt(NFT)
    table = np.concatenate([weights * np.cos(phase), -weights * np.sin(phase)], axis=0)
    return table.astype(ml_dtypes.bfloat16)


def split(value):
    high = value.astype(BF16)
    return high, (value - high.astype(F32)).astype(BF16)


def dot(a, b, dims=((1,), (0,))):
    return lax.dot_general(a, b, (dims, ((), ())), preferred_element_type=F32)


def prepare_kernel(
    blocks, live, row_ref, col_ref, row_tail, col_tail, taps_ref,
    coarse_cos, coarse_sin, fine_cos, fine_sin,
    row_out, col_out, fwd_high, fwd_low, padded,
):
    del blocks
    fc, fs = fine_cos[...], fine_sin[...]
    for a in range(BINS // 8):
        cc = coarse_cos[a : a + 1, :]
        cs = coarse_sin[a : a + 1, :]
        rows = slice(8 * a, 8 * a + 8)
        for value, base in ((cc * fc - cs * fs, 0), (-(cs * fc + cc * fs), BINS)):
            high, low = split(value)
            fwd_high[base + rows.start : base + rows.stop, :] = high
            fwd_low[base + rows.start : base + rows.stop, :] = low

    record = jnp.concatenate([row_ref[0], col_ref[0]], axis=0)
    tail = jnp.concatenate([row_tail[0], col_tail[0]], axis=0)
    count = live[0]
    lane = lax.broadcasted_iota(jnp.int32, (1, LANE), 1)
    pieces = []
    for b in range(SEG // LANE):
        span = DECIM * LANE
        before = tail if b == 0 else record[:, b * span - LANE : b * span]
        both = dot(before, taps_ref[:LANE, :]) + dot(
            record[:, b * span : (b + 1) * span], taps_ref[LANE:, :]
        )
        value = both[:, :LANE] + both[:, LANE:]
        pieces.append(jnp.where(lane + b * LANE < count, value, 0.0))
    filtered = jnp.concatenate(pieces, axis=1)
    high, low = split(filtered)
    last = ((1,), (1,))
    spectra = (
        dot(fwd_high[...], low, last)
        + dot(fwd_low[...], high, last)
        + dot(fwd_high[...], high, last)
    )
    real, imag = spectra[:BINS], spectra[BINS:]
    amplitude = jnp.sqrt(real * real + imag * imag)
    padded[0:8, :] = jnp.zeros((8, LANE), F32)
    padded[8 + BINS : 16 + BINS, :] = jnp.zeros((8, LANE), F32)
    padded[8 : 8 + BINS, :] = amplitude
    smooth = padded[8 - SMOOTH : 8 - SMOOTH + BINS, :]
    for offset in range(1, 2 * SMOOTH + 1):
        start = 8 - SMOOTH + offset
        smooth = smooth + padded[start : start + BINS, :]
    mean = jnp.sum(amplitude, axis=0, keepdims=True) * (1.0 / BINS)
    level = smooth * (1.0 / (2 * SMOOTH + 1)) + 0.05 * mean + 1e-06
    inverse = 1.0 / level
    real = real * inverse
    imag = imag * inverse
    half = LANE // 2
    lower = lax.broadcasted_iota(jnp.int32, (BINS, LANE), 1) < half
    row_out[...] = jnp.where(lower, real, pltpu.roll(imag, half, 1)).astype(BF16)
    cols = jnp.where(lower, pltpu.roll(real, half, 1), imag)
    lanes = lax.broadcasted_iota(jnp.int32, (LANE, LANE), 1)
    for j in range(4):
        total = jnp.zeros((LANE, LANE), F32)
        for quarter in range(QUARTERS):
            part = cols[quarter * LANE : (quarter + 1) * LANE, :]
            for c in range(2):
                source = c * half + 16 * j
                target = quarter * 32 + 16 * c
                moved = part
                if (target - source) % LANE:
                    moved = pltpu.roll(part, (target - source) % LANE, 1)
                keep = (lanes >= target) & (lanes < target + 16)
                total = jnp.where(keep, moved, total)
        col_out[j] = total.astype(BF16)


def prepare(records, tails, tile_blocks, live):
    stations, length = records.shape[1], records.shape[2]
    whole = lambda *shape: pl.BlockSpec(shape, lambda i, b, l: (0,) * len(shape))
    taps = jnp.asarray(filter_table())
    tables = [jnp.asarray(table) for table in turn_tables()]
    return pl.pallas_call(
        prepare_kernel,
        grid_spec=pltpu.PrefetchScalarGridSpec(
            num_scalar_prefetch=2,
            grid=(1,),
            in_specs=[
                pl.BlockSpec((1, stations, length), lambda i, b, l: (b[0], 0, 0)),
                pl.BlockSpec((1, stations, length), lambda i, b, l: (b[1], 0, 0)),
                pl.BlockSpec((1, stations, LANE), lambda i, b, l: (b[0], 0, 0)),
                pl.BlockSpec((1, stations, LANE), lambda i, b, l: (b[1], 0, 0)),
                whole(5 * LANE, 2 * LANE),
                whole(BINS // 8, SEG),
                whole(BINS // 8, SEG),
                whole(8, SEG),
                whole(8, SEG),
            ],
            out_specs=[whole(BINS, LANE), whole(4, LANE, LANE)],
            scratch_shapes=[
                pltpu.VMEM((2 * BINS, SEG), BF16),
                pltpu.VMEM((2 * BINS, SEG), BF16),
                pltpu.VMEM((BINS + 16, LANE), F32),
            ],
        ),
        out_shape=[
            jax.ShapeDtypeStruct((BINS, LANE), BF16),
            jax.ShapeDtypeStruct((4, LANE, LANE), BF16),
        ],
        compiler_params=pltpu.CompilerParams(vmem_limit_bytes=40 << 20),
        name="prepare",
    )(tile_blocks, live, records, records, tails, tails, taps, *tables)


class Place:
    def __init__(self):
        pair, tm = lax.axis_index("pair"), lax.axis_index("tm")
        self.y, self.xl = pair // 2, lax.rem(pair, 2)
        self.xh, self.z, self.c = tm // 16, lax.rem(tm // 2, RING), lax.rem(tm, 2)

    def at(self, y=None, xl=None, xh=None, z=None, c=None):
        pick = lambda new, old: old if new is None else new
        y, xl, xh = pick(y, self.y), pick(xl, self.xl), pick(xh, self.xh)
        z, c = pick(z, self.z), pick(c, self.c)
        return {"pair": y * 2 + xl, "tm": xh * 16 + z * 2 + c}


def slot_of(xh, c, z):
    return xh * 16 + c * RING + z


def schedule():
    events = []
    for i in range(RING):
        for kind, late in COL_TIMES:
            events.append((late + COL_STEP * i, kind, i))
    for s in range(PARTS):
        events.append((OPP_TIME + 0.1 * s, "opposite", s))
        for d in range(1, 5):
            for h in range(2):
                at = ROW_START + ROW_STEP * (d - 1) + (0.5 * ROW_STEP * h + 0.45 * ROW_STEP * s / PARTS)
                events.append((at, "row", (h, d, s)))
    events.sort(key=lambda e: e[0])
    return [(kind, arg) for _, kind, arg in events]


def exchange_kernel(
    row_ref, col_ref, row_all, col_all, stage,
    row_send, row_recv, near_send, near_recv, stage_send, stage_recv,
    col_send, col_recv, local_sem,
):
    me = Place()
    size = BINS // PARTS
    group_xh = me.y // 2
    home_y = me.xh * 2 + me.z // 4
    home_xl = lax.rem(me.z // 2, 2)
    dy = lax.rem(me.y - home_y + YRING, YRING)
    root_pair = lax.rem(me.y, 2) * 2 + me.xl
    is_root = (me.z // 2) == root_pair
    is_near = is_root & (me.xh == group_xh)
    is_far = is_root & (me.xh != group_xh)
    is_other = (dy == 0) & (me.xl != home_xl)
    up, down = lax.rem(me.y + 1, YRING), lax.rem(me.y + YRING - 1, YRING)
    right, left = lax.rem(me.z + 1, RING), lax.rem(me.z + RING - 1, RING)

    barrier = pltpu.get_barrier_semaphore()

    def greet(device):
        pl.semaphore_signal(barrier, inc=1, device_id=device, device_id_type=MESH)

    for step in range(1, 2 * RING):
        other = lax.rem(me.z * 2 + me.c + step, 2 * RING)
        greet(me.at(z=other // 2, c=lax.rem(other, 2)))
    greet(me.at(xh=1 - me.xh))
    greet(me.at(xl=1 - me.xl))
    greet(me.at(xh=1 - me.xh, xl=1 - me.xl))
    greet(me.at(y=up))
    greet(me.at(y=down))
    pl.semaphore_wait(barrier, 2 * RING - 1 + 5)

    def remote(src, dst, send, recv, device):
        return pltpu.make_async_remote_copy(
            src_ref=src, dst_ref=dst, send_sem=send, recv_sem=recv,
            device_id=device, device_id_type=MESH,
        )

    pending = []

    def start(copy, when=None):
        if when is None:
            copy.start()
        else:
            pl.when(when)(copy.start)
        pending.append((copy, when))

    for j in range(4):
        root_z, root_c = root_pair * 2 + j // 2, j % 2
        mine = (me.z == root_z) & (me.c == root_c)
        index = me.c * RING + me.z
        copy = remote(
            col_ref.at[j], stage.at[index], stage_send.at[j], stage_recv.at[index],
            me.at(z=root_z, c=root_c),
        )
        start(copy, jnp.logical_not(mine))

        @pl.when(mine)
        def _():
            pltpu.make_async_copy(col_ref.at[j], stage.at[index], stage_recv.at[index]).start()

    own = slot_of(me.xh, me.c, me.z)
    own_local = pltpu.make_async_copy(row_ref, row_all.at[own], local_sem.at[2 * RING])

    def part(s):
        return pl.ds(s * size, size)

    def spread(source, slot, h, d, sign, s):
        lower = s < PARTS // 2
        for way, target in ((1, right), (-1, left)):
            if sign not in (0, way) or d > 3 or (d == 3 and lower != (way == 1)):
                continue
            start(
                remote(
                    source.at[part(s)], row_all.at[slot, part(s)],
                    row_send.at[h, (0 if way == 1 else 4) + d, s], row_recv.at[slot, s],
                    me.at(z=target),
                )
            )
        number = d + 3 if sign == -1 and d < 4 else (7 if d == 4 else d)
        start(
            remote(
                source.at[part(s)], row_all.at[slot, part(s)], near_send.at[h, number, s],
                near_recv.at[slot, s], me.at(c=1 - me.c),
            )
        )

    def got_row(slot, s, sems):
        ref = row_all.at[slot, part(s)]
        remote(ref, ref, row_send.at[0, 0, 0], sems.at[slot, s], me.at()).wait_recv()

    def got_col(slot):
        ref = col_all.at[slot]
        remote(ref, ref, col_send.at[0, 0], col_recv.at[slot], me.at()).wait_recv()

    for s in range(PARTS):
        start(
            remote(
                row_ref.at[part(s)], row_all.at[own, part(s)], row_send.at[2, 0, s],
                row_recv.at[own, s], me.at(xh=1 - me.xh),
            )
        )
    for s in range(PARTS):
        spread(row_ref, own, 0, 0, 0, s)
    own_local.start()

    def zpiece(i):
        return lax.rem(me.z + OFFSETS[i] + RING, RING)

    def along(source, slot, c, when):
        start(
            remote(
                source, col_all.at[slot], col_send.at[slot, 1], col_recv.at[slot],
                me.at(y=up if c == 0 else down),
            ),
            when,
        )

    def sideways(source, slot, when, **there):
        start(
            remote(
                source, col_all.at[slot], col_send.at[slot, 0], col_recv.at[slot],
                me.at(xl=1 - me.xl, **there),
            ),
            when,
        )

    def hop(slot, c, when):
        pl.when(when)(lambda: got_col(slot))
        along(col_all.at[slot], slot, c, when)

    for kind, arg in schedule():
        if kind == "opposite":
            slot = slot_of(1 - me.xh, me.c, me.z)
            got_row(slot, arg, row_recv)
            spread(row_all.at[slot], slot, 1, 0, 0, arg)
        elif kind == "row":
            h, d, s = arg
            xh = me.xh if h == 0 else 1 - me.xh
            signs = (1, -1) if d < 4 else ((1,) if s < PARTS // 2 else (-1,))
            for sign in signs:
                slot = slot_of(xh, me.c, lax.rem(me.z - sign * d + RING, RING))
                got_row(slot, s, row_recv)
                spread(row_all.at[slot], slot, h, d, sign, s)
        elif kind == "root":
            for c in range(2):
                index = c * RING + zpiece(arg)
                slot = slot_of(me.xh, c, zpiece(arg))

                @pl.when(is_root)
                def _():
                    pltpu.make_async_copy(
                        stage.at[index], stage.at[index], stage_recv.at[index]
                    ).wait()

                @pl.when(is_near)
                def _():
                    pltpu.make_async_copy(
                        stage.at[index], col_all.at[slot], local_sem.at[2 * arg + c]
                    ).start()

                sideways(stage.at[index], slot, is_near)
                sideways(stage.at[index], slot, is_far, xh=1 - me.xh)
                along(stage.at[index], slot, c, is_near)
        elif kind == "other":
            for c in range(2):
                slot = slot_of(1 - me.xh, c, zpiece(arg))
                pl.when(is_other)(lambda slot=slot: got_col(slot))
                sideways(col_all.at[slot], slot, is_other)
                along(col_all.at[slot], slot, c, is_other)
            for c in range(2):
                hop(slot_of(me.xh, c, zpiece(arg)), c, is_other)
        elif kind == "near":
            for c in range(2):
                hop(slot_of(1 - me.xh, c, zpiece(arg)), c, is_near)
        elif kind == "hop1":
            for xh in (me.xh, 1 - me.xh):
                hop(slot_of(xh, 0, zpiece(arg)), 0, dy == 1)
                hop(slot_of(xh, 1, zpiece(arg)), 1, dy == 3)
        elif kind == "hop2":
            for xh in (me.xh, 1 - me.xh):
                for c in range(2):
                    hop(slot_of(xh, c, zpiece(arg)), c, dy == 2)
        elif kind == "last":
            for xh in (me.xh, 1 - me.xh):
                pl.when(dy == 3)(lambda xh=xh: got_col(slot_of(xh, 0, zpiece(arg))))
                pl.when(dy == 1)(lambda xh=xh: got_col(slot_of(xh, 1, zpiece(arg))))

    for h in range(2):
        for z in range(RING):
            for s in range(PARTS):
                got_row(slot_of(h, 1 - me.c, z), s, near_recv)
    own_local.wait()
    for i in range(RING):
        for c in range(2):
            index = c * RING + zpiece(i)
            slot = slot_of(me.xh, c, zpiece(i))

            @pl.when(is_near)
            def _():
                pltpu.make_async_copy(
                    stage.at[index], col_all.at[slot], local_sem.at[2 * i + c]
                ).wait()

    for copy, when in pending:
        if when is None:
            copy.wait_send()
        else:
            pl.when(when)(copy.wait_send)


def exchange(row_own, col_own):
    anywhere = pl.BlockSpec(memory_space=pl.ANY)
    dma = pltpu.SemaphoreType.DMA
    return pl.pallas_call(
        exchange_kernel,
        in_specs=[anywhere, anywhere],
        out_specs=[anywhere, anywhere],
        out_shape=[
            jax.ShapeDtypeStruct((32,) + row_own.shape, BF16),
            jax.ShapeDtypeStruct((32,) + col_own.shape[1:], BF16),
        ],
        scratch_shapes=[
            pltpu.VMEM((2 * RING,) + col_own.shape[1:], BF16),
            dma((3, 8, PARTS)), dma((32, PARTS)), dma((2, 8, PARTS)), dma((32, PARTS)),
            dma((4,)), dma((2 * RING,)), dma((32, 2)), dma((32,)), dma((2 * RING + 1,)),
        ],
        compiler_params=pltpu.CompilerParams(collective_id=0, has_side_effects=True),
        name="exchange",
    )(row_own, col_own)


def correlate_kernel(segments, row_ref, col_ref, lag_ref, out_ref, rows, cols, cross, stacked):
    step = pl.program_id(0)
    half = LANE // 2
    group = 8
    count_k = QUARTERS * KCHUNK

    @pl.when(step < CHUNKS)
    def _():
        rows[...] = row_ref[...].reshape(segments * count_k, LANE).astype(F32)
        cols[...] = col_ref[...].reshape(segments * KCHUNK, LANE).astype(F32)
        lane = lax.broadcasted_iota(jnp.int32, (32, group * segments), 1)
        sign = jnp.where(
            lax.broadcasted_iota(jnp.int32, (1, LANE), 1) < half, 1.0, -1.0
        ).astype(F32)
        for block in range(KCHUNK // group):
            gathered = jnp.concatenate(
                [
                    cols[pl.ds(block * group + b, segments, stride=KCHUNK), :]
                    for b in range(group)
                ],
                axis=0,
            )
            turned = gathered.T.astype(BF16)
            for quarter in range(QUARTERS):
                left = turned[quarter * 32 : quarter * 32 + 32, :]
                zero = jnp.zeros_like(left)
                wide = jnp.concatenate(
                    [
                        jnp.where(
                            (lane >= b * segments) & (lane < (b + 1) * segments), left, zero
                        )
                        for b in range(group)
                    ],
                    axis=0,
                )
                base = quarter * KCHUNK + block * group
                right = jnp.concatenate(
                    [
                        rows[pl.ds(base + b, segments, stride=count_k), :]
                        for b in range(group)
                    ],
                    axis=0,
                ).astype(BF16)
                product = dot(wide, right)
                for b in range(group):
                    top = product[b * 32 : b * 32 + 16, :]
                    low = product[b * 32 + 16 : b * 32 + 32, :]
                    value = top + sign * pltpu.roll(low, half, 1)
                    cross[pl.ds(base + b, 16, stride=count_k), :] = value
        for q in range(16):
            turned = cross[q * count_k : (q + 1) * count_k, :].T.astype(BF16)
            for chunk in range(CHUNKS):

                @pl.when(step == chunk)
                def _():
                    at = chunk * count_k
                    stacked[q * half : (q + 1) * half, at : at + count_k] = turned[:half]
                    stacked[q * half : (q + 1) * half, BINS + at : BINS + at + count_k] = turned[half:]

    @pl.when(step >= CHUNKS)
    def _():
        for q in range(16):
            value = dot(stacked[q * half : (q + 1) * half, :], lag_ref[...])
            out_ref[pl.ds(q, half, stride=16), :] = value


def correlate(row_all, col_all):
    segments = row_all.shape[0]
    row_all = row_all.reshape(segments, QUARTERS, LANE, LANE)
    table = lag_table()
    width = LANE
    tiles = -(-LAGS // width)
    table = jnp.asarray(np.pad(table, ((0, 0), (0, tiles * width - LAGS))))
    pairs = 16 * (LANE // 2)

    body = functools.partial(correlate_kernel, segments)
    return pl.pallas_call(
        body,
        grid=(CHUNKS + tiles,),
        in_specs=[
            pl.BlockSpec(
                (segments, QUARTERS, KCHUNK, LANE),
                lambda i: (0, 0, jnp.minimum(i, CHUNKS - 1), 0),
            ),
            pl.BlockSpec(
                (segments, KCHUNK, LANE), lambda i: (0, jnp.minimum(i, CHUNKS - 1), 0)
            ),
            pl.BlockSpec((2 * BINS, width), lambda i: (0, jnp.maximum(i - CHUNKS, 0))),
        ],
        out_specs=pl.BlockSpec((pairs, width), lambda i: (0, jnp.maximum(i - CHUNKS, 0))),
        out_shape=jax.ShapeDtypeStruct((pairs, LAGS), F32),
        scratch_shapes=[
            pltpu.VMEM((segments * QUARTERS * KCHUNK, LANE), F32),
            pltpu.VMEM((segments * KCHUNK, LANE), F32),
            pltpu.VMEM((16 * QUARTERS * KCHUNK, LANE), F32),
            pltpu.VMEM((pairs, 2 * BINS), BF16),
        ],
        compiler_params=pltpu.CompilerParams(vmem_limit_bytes=48 << 20),
        name="correlate",
    )(row_all, col_all, table)


def shards(records, tile_blocks, live_len):
    length = records.shape[2]
    size = lax.axis_size("tm")
    tails = lax.ppermute(
        records[:, :, length - LANE :], "tm", [(i, i + 1) for i in range(size - 1)]
    )
    live = lax.dynamic_slice(live_len, (lax.axis_index("tm"),), (1,))
    row_own, col_own = prepare(records, tails, tile_blocks, live)
    row_all, col_all = exchange(row_own, col_own)
    result = correlate(row_all, col_all)
    return result.reshape(LANE // 2, 16, LAGS)


def solution(mesh):
    placed = (P(None, "pair", "tm"), P(), P())
    return jax.shard_map(
        shards, mesh=mesh, in_specs=placed, out_specs=P("pair", "tm", None), check_vma=False
    )
```

```python
import functools
import math

import jax
import jax.numpy as jnp
import ml_dtypes
import numpy as np
from jax import lax
from jax.experimental import pallas as pl
from jax.experimental.pallas import tpu as pltpu
from jax.sharding import PartitionSpec as P

DECIM = 4
TAPS = 64
SEG = 512
NFT = 1024
MAXLAG = 400
SMOOTH = 4
BINS = 512
LAGS = 801
LANE = 128
QUARTERS = 4
CHUNKS = 4
KCHUNK = LANE // CHUNKS
TWO_PI = 2.0 * math.pi / NFT
F32 = jnp.float32
BF16 = jnp.bfloat16
MESH = pl.DeviceIdType.MESH
RING = 8
YRING = 4
OFFSETS = (0, 1, -1, 2, -2, 3, -3, 4)
PARTS = 2
OPP_TIME = 3.0
ROW_START, ROW_STEP = 5.0, 5.0
COL_STEP = 1.5
COL_TIMES = (
    ("root", 1.5),
    ("other", 8.0),
    ("near", 10.5),
    ("hop1", 13.0),
    ("hop2", 16.0),
    ("last", 40.0),
)


def turns(rows, step, columns):
    row = lax.broadcasted_iota(jnp.int32, (rows, columns), 0) * step
    index = (row * lax.broadcasted_iota(jnp.int32, (rows, columns), 1)) & (NFT - 1)
    index = jnp.where(index >= NFT // 2, index - NFT, index)
    phase = index.astype(F32) * TWO_PI
    return jnp.cos(phase), jnp.sin(phase)


def fill_taps(taps_ref):
    row = lax.broadcasted_iota(jnp.int32, (8, LANE), 0)
    lane = lax.broadcasted_iota(jnp.int32, (8, LANE), 1)
    index = row - TAPS - DECIM * (lane - LANE)
    inside = (index >= 0) & (index < TAPS)
    position = jnp.where(inside, index, 0).astype(F32)
    centred = (position - (TAPS - 1) / 2.0) * (1.0 / DECIM)
    window = 0.5 * (1.0 - jnp.cos((2.0 * math.pi / TAPS) * (position + 0.5)))
    turn = math.pi * centred
    value = jnp.where(inside, window * jnp.sin(turn) / turn * (1.0 / DECIM), 0.0)
    shift = 8 // DECIM
    for r in range(0, 5 * LANE // 8, 2):
        pair = []
        for one in (r, r + 1):
            moved = value
            if one * shift % LANE:
                moved = pltpu.roll(value, one * shift % LANE, 1)
            offset = row - TAPS - DECIM * (lane - one * shift)
            pair.append(jnp.where((offset >= 0) & (offset < TAPS), moved, 0.0))
        high, low = split(jnp.concatenate(pair, axis=0))
        taps_ref[8 * r : 8 * r + 16, :LANE] = high
        taps_ref[8 * r : 8 * r + 16, LANE:] = low


def bin_order():
    chunk = np.arange(CHUNKS)[:, None, None]
    quarter = np.arange(QUARTERS)[None, :, None]
    inner = np.arange(KCHUNK)[None, None, :]
    return (quarter * LANE + chunk * KCHUNK + inner).reshape(-1)


def lag_table():
    bins = bin_order()
    shifts = np.arange(LAGS) - MAXLAG
    phase = (bins[:, None] * shifts[None, :] % NFT) * TWO_PI
    weights = np.where(bins == 0, 1.0, 2.0)[:, None] / math.sqrt(NFT)
    table = np.concatenate([weights * np.cos(phase), -weights * np.sin(phase)], axis=0)
    return table.astype(ml_dtypes.bfloat16)


def split(value):
    high = value.astype(BF16)
    return high, (value - high.astype(F32)).astype(BF16)


def dot(a, b, dims=((1,), (0,))):
    return lax.dot_general(a, b, (dims, ((), ())), preferred_element_type=F32)


def prepare_kernel(
    blocks, live, row_ref, col_ref, row_tail, col_tail,
    row_out, col_out, taps_ref, fwd_high, fwd_low, padded,
):
    del blocks
    fill_taps(taps_ref)
    coarse_cos, coarse_sin = turns(BINS // 8, 8, SEG)
    fine_cos, fine_sin = turns(8, 1, SEG)
    for a in range(0, BINS // 8, 2):
        reals, imags = [], []
        for one in (a, a + 1):
            cc, cs = coarse_cos[one : one + 1, :], coarse_sin[one : one + 1, :]
            reals.append(cc * fine_cos - cs * fine_sin)
            imags.append(-(cs * fine_cos + cc * fine_sin))
        for value, base in ((reals, 8 * a), (imags, BINS + 8 * a)):
            high, low = split(jnp.concatenate(value, axis=0))
            fwd_high[base : base + 16, :] = high
            fwd_low[base : base + 16, :] = low

    record = jnp.concatenate([row_ref[0], col_ref[0]], axis=0)
    tail = jnp.concatenate([row_tail[0], col_tail[0]], axis=0)
    count = live[lax.axis_index("tm")]
    lane = lax.broadcasted_iota(jnp.int32, (1, LANE), 1)
    pieces = []
    for b in range(SEG // LANE):
        span = DECIM * LANE
        before = tail if b == 0 else record[:, b * span - LANE : b * span]
        both = dot(before, taps_ref[:LANE, :]) + dot(
            record[:, b * span : (b + 1) * span], taps_ref[LANE:, :]
        )
        value = both[:, :LANE] + both[:, LANE:]
        pieces.append(jnp.where(lane + b * LANE < count, value, 0.0))
    filtered = jnp.concatenate(pieces, axis=1)
    high, low = split(filtered)
    last = ((1,), (1,))
    spectra = (
        dot(fwd_high[...], low, last)
        + dot(fwd_low[...], high, last)
        + dot(fwd_high[...], high, last)
    )
    real, imag = spectra[:BINS], spectra[BINS:]
    amplitude = jnp.sqrt(real * real + imag * imag)
    padded[0:8, :] = jnp.zeros((8, LANE), F32)
    padded[8 + BINS : 16 + BINS, :] = jnp.zeros((8, LANE), F32)
    padded[8 : 8 + BINS, :] = amplitude
    smooth = padded[8 - SMOOTH : 8 - SMOOTH + BINS, :]
    for offset in range(1, 2 * SMOOTH + 1):
        start = 8 - SMOOTH + offset
        smooth = smooth + padded[start : start + BINS, :]
    mean = jnp.sum(amplitude, axis=0, keepdims=True) * (1.0 / BINS)
    level = smooth * (1.0 / (2 * SMOOTH + 1)) + 0.05 * mean + 1e-06
    inverse = 1.0 / level
    real = real * inverse
    imag = imag * inverse
    half = LANE // 2
    lower = lax.broadcasted_iota(jnp.int32, (BINS, LANE), 1) < half
    row_out[...] = jnp.where(lower, real, pltpu.roll(imag, half, 1)).astype(BF16)
    cols = jnp.where(lower, pltpu.roll(real, half, 1), imag)
    lanes = lax.broadcasted_iota(jnp.int32, (LANE, LANE), 1)
    for j in range(4):
        total = jnp.zeros((LANE, LANE), F32)
        for quarter in range(QUARTERS):
            part = cols[quarter * LANE : (quarter + 1) * LANE, :]
            for c in range(2):
                source = c * half + 16 * j
                target = quarter * 32 + 16 * c
                moved = part
                if (target - source) % LANE:
                    moved = pltpu.roll(part, (target - source) % LANE, 1)
                keep = (lanes >= target) & (lanes < target + 16)
                total = jnp.where(keep, moved, total)
        col_out[j] = total.astype(BF16)


def prepare(records, tails, tile_blocks, live):
    stations, length = records.shape[1], records.shape[2]
    whole = lambda *shape: pl.BlockSpec(shape, lambda i, b, l: (0,) * len(shape))
    return pl.pallas_call(
        prepare_kernel,
        grid_spec=pltpu.PrefetchScalarGridSpec(
            num_scalar_prefetch=2,
            grid=(1,),
            in_specs=[
                pl.BlockSpec((1, stations, length), lambda i, b, l: (b[0], 0, 0)),
                pl.BlockSpec((1, stations, length), lambda i, b, l: (b[1], 0, 0)),
                pl.BlockSpec((1, stations, LANE), lambda i, b, l: (b[0], 0, 0)),
                pl.BlockSpec((1, stations, LANE), lambda i, b, l: (b[1], 0, 0)),
            ],
            out_specs=[whole(BINS, LANE), whole(4, LANE, LANE)],
            scratch_shapes=[
                pltpu.VMEM((5 * LANE, 2 * LANE), BF16),
                pltpu.VMEM((2 * BINS, SEG), BF16),
                pltpu.VMEM((2 * BINS, SEG), BF16),
                pltpu.VMEM((BINS + 16, LANE), F32),
            ],
        ),
        out_shape=[
            jax.ShapeDtypeStruct((BINS, LANE), BF16),
            jax.ShapeDtypeStruct((4, LANE, LANE), BF16),
        ],
        compiler_params=pltpu.CompilerParams(vmem_limit_bytes=40 << 20),
        name="prepare",
    )(tile_blocks, live, records, records, tails, tails)


class Place:
    def __init__(self):
        pair, tm = lax.axis_index("pair"), lax.axis_index("tm")
        self.y, self.xl = pair // 2, lax.rem(pair, 2)
        self.xh, self.z, self.c = tm // 16, lax.rem(tm // 2, RING), lax.rem(tm, 2)

    def at(self, y=None, xl=None, xh=None, z=None, c=None):
        pick = lambda new, old: old if new is None else new
        y, xl, xh = pick(y, self.y), pick(xl, self.xl), pick(xh, self.xh)
        z, c = pick(z, self.z), pick(c, self.c)
        return {"pair": y * 2 + xl, "tm": xh * 16 + z * 2 + c}


def slot_of(xh, c, z):
    return xh * 16 + c * RING + z


def schedule():
    events = []
    for i in range(RING):
        for kind, late in COL_TIMES:
            events.append((late + COL_STEP * i, kind, i))
    for s in range(PARTS):
        events.append((OPP_TIME + 0.1 * s, "opposite", s))
        for d in range(1, 5):
            for h in range(2):
                at = ROW_START + ROW_STEP * (d - 1) + (0.5 * ROW_STEP * h + 0.45 * ROW_STEP * s / PARTS)
                events.append((at, "row", (h, d, s)))
    events.sort(key=lambda e: e[0])
    return [(kind, arg) for _, kind, arg in events]


def exchange_kernel(
    row_ref, col_ref, row_all, col_all, stage,
    row_send, row_recv, near_send, near_recv, stage_send, stage_recv,
    col_send, col_recv, local_sem,
):
    me = Place()
    size = BINS // PARTS
    group_xh = me.y // 2
    home_y = me.xh * 2 + me.z // 4
    home_xl = lax.rem(me.z // 2, 2)
    dy = lax.rem(me.y - home_y + YRING, YRING)
    root_pair = lax.rem(me.y, 2) * 2 + me.xl
    is_root = (me.z // 2) == root_pair
    is_near = is_root & (me.xh == group_xh)
    is_far = is_root & (me.xh != group_xh)
    is_other = (dy == 0) & (me.xl != home_xl)
    up, down = lax.rem(me.y + 1, YRING), lax.rem(me.y + YRING - 1, YRING)
    right, left = lax.rem(me.z + 1, RING), lax.rem(me.z + RING - 1, RING)

    barrier = pltpu.get_barrier_semaphore()

    def greet(device):
        pl.semaphore_signal(barrier, inc=1, device_id=device, device_id_type=MESH)

    for step in range(1, 2 * RING):
        other = lax.rem(me.z * 2 + me.c + step, 2 * RING)
        greet(me.at(z=other // 2, c=lax.rem(other, 2)))
    greet(me.at(xh=1 - me.xh))
    greet(me.at(xl=1 - me.xl))
    greet(me.at(xh=1 - me.xh, xl=1 - me.xl))
    greet(me.at(y=up))
    greet(me.at(y=down))
    pl.semaphore_wait(barrier, 2 * RING - 1 + 5)

    def remote(src, dst, send, recv, device):
        return pltpu.make_async_remote_copy(
            src_ref=src, dst_ref=dst, send_sem=send, recv_sem=recv,
            device_id=device, device_id_type=MESH,
        )

    pending = []

    def start(copy, when=None):
        if when is None:
            copy.start()
        else:
            pl.when(when)(copy.start)
        pending.append((copy, when))

    for j in range(4):
        root_z, root_c = root_pair * 2 + j // 2, j % 2
        mine = (me.z == root_z) & (me.c == root_c)
        index = me.c * RING + me.z
        copy = remote(
            col_ref.at[j], stage.at[index], stage_send.at[j], stage_recv.at[index],
            me.at(z=root_z, c=root_c),
        )
        start(copy, jnp.logical_not(mine))

        @pl.when(mine)
        def _():
            pltpu.make_async_copy(col_ref.at[j], stage.at[index], stage_recv.at[index]).start()

    own = slot_of(me.xh, me.c, me.z)
    own_local = pltpu.make_async_copy(row_ref, row_all.at[own], local_sem.at[2 * RING])

    def part(s):
        return pl.ds(s * size, size)

    def spread(source, slot, h, d, sign, s):
        lower = s < PARTS // 2
        for way, target in ((1, right), (-1, left)):
            if sign not in (0, way) or d > 3 or (d == 3 and lower != (way == 1)):
                continue
            start(
                remote(
                    source.at[part(s)], row_all.at[slot, part(s)],
                    row_send.at[h, (0 if way == 1 else 4) + d, s], row_recv.at[slot, s],
                    me.at(z=target),
                )
            )
        number = d + 3 if sign == -1 and d < 4 else (7 if d == 4 else d)
        start(
            remote(
                source.at[part(s)], row_all.at[slot, part(s)], near_send.at[h, number, s],
                near_recv.at[slot, s], me.at(c=1 - me.c),
            )
        )

    def got_row(slot, s, sems):
        ref = row_all.at[slot, part(s)]
        remote(ref, ref, row_send.at[0, 0, 0], sems.at[slot, s], me.at()).wait_recv()

    def got_col(slot):
        ref = col_all.at[slot]
        remote(ref, ref, col_send.at[0, 0], col_recv.at[slot], me.at()).wait_recv()

    for s in range(PARTS):
        start(
            remote(
                row_ref.at[part(s)], row_all.at[own, part(s)], row_send.at[2, 0, s],
                row_recv.at[own, s], me.at(xh=1 - me.xh),
            )
        )
    for s in range(PARTS):
        spread(row_ref, own, 0, 0, 0, s)
    own_local.start()

    def zpiece(i):
        return lax.rem(me.z + OFFSETS[i] + RING, RING)

    def along(source, slot, c, when):
        start(
            remote(
                source, col_all.at[slot], col_send.at[slot, 1], col_recv.at[slot],
                me.at(y=up if c == 0 else down),
            ),
            when,
        )

    def sideways(source, slot, when, **there):
        start(
            remote(
                source, col_all.at[slot], col_send.at[slot, 0], col_recv.at[slot],
                me.at(xl=1 - me.xl, **there),
            ),
            when,
        )

    def hop(slot, c, when):
        pl.when(when)(lambda: got_col(slot))
        along(col_all.at[slot], slot, c, when)

    for kind, arg in schedule():
        if kind == "opposite":
            slot = slot_of(1 - me.xh, me.c, me.z)
            got_row(slot, arg, row_recv)
            spread(row_all.at[slot], slot, 1, 0, 0, arg)
        elif kind == "row":
            h, d, s = arg
            xh = me.xh if h == 0 else 1 - me.xh
            signs = (1, -1) if d < 4 else ((1,) if s < PARTS // 2 else (-1,))
            for sign in signs:
                slot = slot_of(xh, me.c, lax.rem(me.z - sign * d + RING, RING))
                got_row(slot, s, row_recv)
                spread(row_all.at[slot], slot, h, d, sign, s)
        elif kind == "root":
            for c in range(2):
                index = c * RING + zpiece(arg)
                slot = slot_of(me.xh, c, zpiece(arg))

                @pl.when(is_root)
                def _():
                    pltpu.make_async_copy(
                        stage.at[index], stage.at[index], stage_recv.at[index]
                    ).wait()

                @pl.when(is_near)
                def _():
                    pltpu.make_async_copy(
                        stage.at[index], col_all.at[slot], local_sem.at[2 * arg + c]
                    ).start()

                sideways(stage.at[index], slot, is_near)
                sideways(stage.at[index], slot, is_far, xh=1 - me.xh)
                along(stage.at[index], slot, c, is_near)
        elif kind == "other":
            for c in range(2):
                slot = slot_of(1 - me.xh, c, zpiece(arg))
                pl.when(is_other)(lambda slot=slot: got_col(slot))
                sideways(col_all.at[slot], slot, is_other)
                along(col_all.at[slot], slot, c, is_other)
            for c in range(2):
                hop(slot_of(me.xh, c, zpiece(arg)), c, is_other)
        elif kind == "near":
            for c in range(2):
                hop(slot_of(1 - me.xh, c, zpiece(arg)), c, is_near)
        elif kind == "hop1":
            for xh in (me.xh, 1 - me.xh):
                hop(slot_of(xh, 0, zpiece(arg)), 0, dy == 1)
                hop(slot_of(xh, 1, zpiece(arg)), 1, dy == 3)
        elif kind == "hop2":
            for xh in (me.xh, 1 - me.xh):
                for c in range(2):
                    hop(slot_of(xh, c, zpiece(arg)), c, dy == 2)
        elif kind == "last":
            for xh in (me.xh, 1 - me.xh):
                pl.when(dy == 3)(lambda xh=xh: got_col(slot_of(xh, 0, zpiece(arg))))
                pl.when(dy == 1)(lambda xh=xh: got_col(slot_of(xh, 1, zpiece(arg))))

    for h in range(2):
        for z in range(RING):
            for s in range(PARTS):
                got_row(slot_of(h, 1 - me.c, z), s, near_recv)
    own_local.wait()
    for i in range(RING):
        for c in range(2):
            index = c * RING + zpiece(i)
            slot = slot_of(me.xh, c, zpiece(i))

            @pl.when(is_near)
            def _():
                pltpu.make_async_copy(
                    stage.at[index], col_all.at[slot], local_sem.at[2 * i + c]
                ).wait()

    for copy, when in pending:
        if when is None:
            copy.wait_send()
        else:
            pl.when(when)(copy.wait_send)


def exchange(row_own, col_own):
    anywhere = pl.BlockSpec(memory_space=pl.ANY)
    dma = pltpu.SemaphoreType.DMA
    return pl.pallas_call(
        exchange_kernel,
        in_specs=[pl.BlockSpec(memory_space=pltpu.VMEM)] * 2,
        out_specs=[anywhere, anywhere],
        out_shape=[
            jax.ShapeDtypeStruct((32,) + row_own.shape, BF16),
            jax.ShapeDtypeStruct((32,) + col_own.shape[1:], BF16),
        ],
        scratch_shapes=[
            pltpu.VMEM((2 * RING,) + col_own.shape[1:], BF16),
            dma((3, 8, PARTS)), dma((32, PARTS)), dma((2, 8, PARTS)), dma((32, PARTS)),
            dma((4,)), dma((2 * RING,)), dma((32, 2)), dma((32,)), dma((2 * RING + 1,)),
        ],
        compiler_params=pltpu.CompilerParams(collective_id=0, has_side_effects=True),
        name="exchange",
    )(row_own, col_own)


def correlate_kernel(segments, row_ref, col_ref, lag_ref, out_ref, rows, cols, cross, stacked, spare):
    step = pl.program_id(0)
    half = LANE // 2
    group = 8
    count_k = QUARTERS * KCHUNK
    stride_k, stride_c, stride_p = count_k + 8, KCHUNK + 8, half + 8

    @pl.when(step < CHUNKS)
    def _():
        for g in range(segments):
            rows[g * stride_k : g * stride_k + count_k, :] = row_ref[g].reshape(count_k, LANE).astype(F32)
            cols[g * stride_c : g * stride_c + KCHUNK, :] = col_ref[g].astype(F32)
        lane = lax.broadcasted_iota(jnp.int32, (32, group * segments), 1)
        sign = jnp.where(
            lax.broadcasted_iota(jnp.int32, (1, LANE), 1) < half, 1.0, -1.0
        ).astype(F32)
        for block in range(KCHUNK // group):
            gathered = jnp.concatenate(
                [
                    cols[pl.ds(block * group + b, segments, stride=stride_c), :]
                    for b in range(group)
                ],
                axis=0,
            )
            turned = gathered.T.astype(BF16)
            for quarter in range(QUARTERS):
                left = turned[quarter * 32 : quarter * 32 + 32, :]
                zero = jnp.zeros_like(left)
                wide = jnp.concatenate(
                    [
                        jnp.where(
                            (lane >= b * segments) & (lane < (b + 1) * segments), left, zero
                        )
                        for b in range(group)
                    ],
                    axis=0,
                )
                base = quarter * KCHUNK + block * group
                right = jnp.concatenate(
                    [
                        rows[pl.ds(base + b, segments, stride=stride_k), :]
                        for b in range(group)
                    ],
                    axis=0,
                ).astype(BF16)
                product = dot(wide, right)
                for b in range(group):
                    top = product[b * 32 : b * 32 + 16, :]
                    low = product[b * 32 + 16 : b * 32 + 32, :]
                    value = top + sign * pltpu.roll(low, half, 1)
                    cross[pl.ds(base + b, 16, stride=stride_k), :] = value
        at = pl.multiple_of(step * count_k, LANE)
        for q in range(16):
            turned = cross[q * stride_k : q * stride_k + count_k, :].astype(BF16).T
            stacked[q * half : (q + 1) * half, pl.ds(at, count_k)] = turned[:half]
            stacked[q * half : (q + 1) * half, pl.ds(BINS + at, count_k)] = turned[half:]

    @pl.when(step >= CHUNKS)
    def _():
        for r in range(1):
            value = dot(stacked[...], lag_ref[...])
            for q in range(16):
                for side in range(2):
                    spare[side, (q) * 72 : (q) * 72 + half, :] = value[
                        q * half : (q + 1) * half, side * LANE : (side + 1) * LANE
                    ]
        for p in range(half):
            for side in range(2):
                out_ref[p * 16 : p * 16 + 16, side * LANE : (side + 1) * LANE] = spare[
                    side, pl.ds(p, 16, stride=stride_p), :
                ]


def correlate(row_all, col_all):
    segments = row_all.shape[0]
    row_all = row_all.reshape(segments, QUARTERS, LANE, LANE)
    table = lag_table()
    width = 2 * LANE
    tiles = -(-LAGS // width)
    table = jnp.asarray(np.pad(table, ((0, 0), (0, tiles * width - LAGS))))
    pairs = 16 * (LANE // 2)

    body = functools.partial(correlate_kernel, segments)
    return pl.pallas_call(
        body,
        grid=(CHUNKS + tiles,),
        in_specs=[
            pl.BlockSpec(
                (segments, QUARTERS, KCHUNK, LANE),
                lambda i: (0, 0, jnp.minimum(i, CHUNKS - 1), 0),
            ),
            pl.BlockSpec(
                (segments, KCHUNK, LANE), lambda i: (0, jnp.minimum(i, CHUNKS - 1), 0)
            ),
            pl.BlockSpec((2 * BINS, width), lambda i: (0, jnp.maximum(i - CHUNKS, 0))),
        ],
        out_specs=pl.BlockSpec((pairs, width), lambda i: (0, jnp.maximum(i - CHUNKS, 0))),
        out_shape=jax.ShapeDtypeStruct((pairs, LAGS), F32),
        scratch_shapes=[
            pltpu.VMEM((segments * (QUARTERS * KCHUNK + 8), LANE), F32),
            pltpu.VMEM((segments * (KCHUNK + 8), LANE), F32),
            pltpu.VMEM((16 * (QUARTERS * KCHUNK + 8), LANE), F32),
            pltpu.VMEM((pairs, 2 * BINS), BF16),
            pltpu.VMEM((2, 16 * 72, LANE), F32),
        ],
        compiler_params=pltpu.CompilerParams(vmem_limit_bytes=48 << 20),
        name="correlate",
    )(row_all, col_all, table)


def shards(records, tile_blocks, live_len):
    length = records.shape[2]
    size = lax.axis_size("tm")
    tails = lax.ppermute(
        records[:, :, length - LANE :], "tm", [(i, i + 1) for i in range(size - 1)]
    )
    row_own, col_own = prepare(records, tails, tile_blocks, live_len)
    row_all, col_all = exchange(row_own, col_own)
    result = correlate(row_all, col_all)
    return result.reshape(LANE // 2, 16, LAGS)


def solution(mesh):
    placed = (P(None, "pair", "tm"), P(), P())
    return jax.shard_map(
        shards, mesh=mesh, in_specs=placed, out_specs=P("pair", "tm", None), check_vma=False
    )
```

```python
import math

import jax
import jax.numpy as jnp
import ml_dtypes
import numpy as np
from jax import lax
from jax.experimental import pallas as pl
from jax.experimental.pallas import tpu as pltpu
from jax.sharding import PartitionSpec as P

DECIM = 4
TAPS = 64
SEG = 512
NFT = 1024
MAXLAG = 400
SMOOTH = 4
BINS = 512
LAGS = 801
LANE = 128
QUARTERS = 4
CHUNKS = 4
KCHUNK = LANE // CHUNKS
PAIRS = 1024
STRIDE_K = QUARTERS * KCHUNK + 8
STRIDE_C = KCHUNK + 8
STRIDE_P = LANE // 2 + 8
TWO_PI = 2.0 * math.pi / NFT
F32 = jnp.float32
BF16 = jnp.bfloat16
MESH = pl.DeviceIdType.MESH
RING = 8
YRING = 4
OFFSETS = (0, 1, -1, 2, -2, 3, -3, 4)
PARTS = 2
OPP_TIME = 3.0
ROW_START, ROW_STEP = 5.0, 5.0
COL_STEP = 1.5
COL_TIMES = (
    ("root", 1.5),
    ("other", 8.0),
    ("near", 10.5),
    ("hop1", 13.0),
    ("hop2", 16.0),
    ("last", 40.0),
)


def turns(rows, step, columns):
    row = lax.broadcasted_iota(jnp.int32, (rows, columns), 0) * step
    index = (row * lax.broadcasted_iota(jnp.int32, (rows, columns), 1)) & (NFT - 1)
    index = jnp.where(index >= NFT // 2, index - NFT, index)
    phase = index.astype(F32) * TWO_PI
    return jnp.cos(phase), jnp.sin(phase)


def fill_taps(taps_ref):
    row = lax.broadcasted_iota(jnp.int32, (8, LANE), 0)
    lane = lax.broadcasted_iota(jnp.int32, (8, LANE), 1)
    index = row - TAPS - DECIM * (lane - LANE)
    inside = (index >= 0) & (index < TAPS)
    position = jnp.where(inside, index, 0).astype(F32)
    centred = (position - (TAPS - 1) / 2.0) * (1.0 / DECIM)
    window = 0.5 * (1.0 - jnp.cos((2.0 * math.pi / TAPS) * (position + 0.5)))
    turn = math.pi * centred
    value = jnp.where(inside, window * jnp.sin(turn) / turn * (1.0 / DECIM), 0.0)
    shift = 8 // DECIM
    for r in range(0, 5 * LANE // 8, 2):
        pair = []
        for one in (r, r + 1):
            moved = value
            if one * shift % LANE:
                moved = pltpu.roll(value, one * shift % LANE, 1)
            offset = row - TAPS - DECIM * (lane - one * shift)
            pair.append(jnp.where((offset >= 0) & (offset < TAPS), moved, 0.0))
        high, low = split(jnp.concatenate(pair, axis=0))
        taps_ref[8 * r : 8 * r + 16, :LANE] = high
        taps_ref[8 * r : 8 * r + 16, LANE:] = low


def bin_order():
    chunk = np.arange(CHUNKS)[:, None, None]
    quarter = np.arange(QUARTERS)[None, :, None]
    inner = np.arange(KCHUNK)[None, None, :]
    return (quarter * LANE + chunk * KCHUNK + inner).reshape(-1)


def lag_table():
    bins = bin_order()
    shifts = np.arange(LAGS) - MAXLAG
    phase = (bins[:, None] * shifts[None, :] % NFT) * TWO_PI
    weights = np.where(bins == 0, 1.0, 2.0)[:, None] / math.sqrt(NFT)
    table = np.concatenate([weights * np.cos(phase), -weights * np.sin(phase)], axis=0)
    return table.astype(ml_dtypes.bfloat16)


def split(value):
    high = value.astype(BF16)
    return high, (value - high.astype(F32)).astype(BF16)


def dot(a, b, dims=((1,), (0,))):
    return lax.dot_general(a, b, (dims, ((), ())), preferred_element_type=F32)


def fill_transform(fwd_high, fwd_low):
    coarse_cos, coarse_sin = turns(BINS // 8, 8, SEG)
    fine_cos, fine_sin = turns(8, 1, SEG)
    for a in range(0, BINS // 8, 2):
        reals, imags = [], []
        for one in (a, a + 1):
            cc, cs = coarse_cos[one : one + 1, :], coarse_sin[one : one + 1, :]
            reals.append(cc * fine_cos - cs * fine_sin)
            imags.append(-(cs * fine_cos + cc * fine_sin))
        for value, base in ((reals, 8 * a), (imags, BINS + 8 * a)):
            high, low = split(jnp.concatenate(value, axis=0))
            fwd_high[base : base + 16, :] = high
            fwd_low[base : base + 16, :] = low


def whiten(filtered, fwd_high, fwd_low, padded):
    high, low = split(filtered)
    last = ((1,), (1,))
    spectra = (
        dot(fwd_high[...], low, last)
        + dot(fwd_low[...], high, last)
        + dot(fwd_high[...], high, last)
    )
    real, imag = spectra[:BINS], spectra[BINS:]
    amplitude = jnp.sqrt(real * real + imag * imag)
    padded[0:8, :] = jnp.zeros((8, LANE), F32)
    padded[8 + BINS : 16 + BINS, :] = jnp.zeros((8, LANE), F32)
    padded[8 : 8 + BINS, :] = amplitude
    smooth = padded[8 - SMOOTH : 8 - SMOOTH + BINS, :]
    for offset in range(1, 2 * SMOOTH + 1):
        start = 8 - SMOOTH + offset
        smooth = smooth + padded[start : start + BINS, :]
    mean = jnp.sum(amplitude, axis=0, keepdims=True) * (1.0 / BINS)
    level = smooth * (1.0 / (2 * SMOOTH + 1)) + 0.05 * mean + 1e-06
    inverse = 1.0 / level
    return real * inverse, imag * inverse


def pack_rows(real, imag, row_own):
    half = LANE // 2
    lower = lax.broadcasted_iota(jnp.int32, (BINS, LANE), 1) < half
    row_own[...] = jnp.where(lower, real, pltpu.roll(imag, half, 1)).astype(BF16)


def pack_columns(real, imag, col_own):
    half = LANE // 2
    lower = lax.broadcasted_iota(jnp.int32, (BINS, LANE), 1) < half
    cols = jnp.where(lower, pltpu.roll(real, half, 1), imag)
    lanes = lax.broadcasted_iota(jnp.int32, (LANE, LANE), 1)
    for j in range(4):
        total = jnp.zeros((LANE, LANE), F32)
        for quarter in range(QUARTERS):
            part = cols[quarter * LANE : (quarter + 1) * LANE, :]
            for c in range(2):
                source = c * half + 16 * j
                target = quarter * 32 + 16 * c
                moved = part
                if (target - source) % LANE:
                    moved = pltpu.roll(part, (target - source) % LANE, 1)
                keep = (lanes >= target) & (lanes < target + 16)
                total = jnp.where(keep, moved, total)
        col_own[j] = total.astype(BF16)


class Place:
    def __init__(self):
        pair, tm = lax.axis_index("pair"), lax.axis_index("tm")
        self.y, self.xl = pair // 2, lax.rem(pair, 2)
        self.xh, self.z, self.c = tm // 16, lax.rem(tm // 2, RING), lax.rem(tm, 2)

    def at(self, y=None, xl=None, xh=None, z=None, c=None):
        pick = lambda new, old: old if new is None else new
        y, xl, xh = pick(y, self.y), pick(xl, self.xl), pick(xh, self.xh)
        z, c = pick(z, self.z), pick(c, self.c)
        return {"pair": y * 2 + xl, "tm": xh * 16 + z * 2 + c}


def slot_of(xh, c, z):
    return xh * 16 + c * RING + z


def schedule():
    events = []
    for i in range(RING):
        for kind, late in COL_TIMES:
            events.append((late + COL_STEP * i, kind, i))
    for s in range(PARTS):
        events.append((OPP_TIME + 0.1 * s, "opposite", s))
        for d in range(1, 5):
            for h in range(2):
                at = ROW_START + ROW_STEP * (d - 1) + (0.5 * ROW_STEP * h + 0.45 * ROW_STEP * s / PARTS)
                events.append((at, "row", (h, d, s)))
    events.sort(key=lambda e: e[0])
    return [(kind, arg) for _, kind, arg in events]


def spectra_kernel(
    blocks, live, records, stacked,
    tail_own, tail_in, taps_ref, fwd_high, fwd_low, padded, row_ref, col_ref,
    row_all, col_all, stage, rows, cols, cross,
    tail_sem, row_send, row_recv, near_send, near_recv, stage_send, stage_recv,
    col_send, col_recv, local_sem,
):
    me = Place()
    size = BINS // PARTS
    group_xh = me.y // 2
    home_y = me.xh * 2 + me.z // 4
    home_xl = lax.rem(me.z // 2, 2)
    dy = lax.rem(me.y - home_y + YRING, YRING)
    root_pair = lax.rem(me.y, 2) * 2 + me.xl
    is_root = (me.z // 2) == root_pair
    is_near = is_root & (me.xh == group_xh)
    is_far = is_root & (me.xh != group_xh)
    is_other = (dy == 0) & (me.xl != home_xl)
    up, down = lax.rem(me.y + 1, YRING), lax.rem(me.y + YRING - 1, YRING)
    right, left = lax.rem(me.z + 1, RING), lax.rem(me.z + RING - 1, RING)

    barrier = pltpu.get_barrier_semaphore()

    def greet(device):
        pl.semaphore_signal(barrier, inc=1, device_id=device, device_id_type=MESH)

    for step in range(1, 2 * RING):
        other = lax.rem(me.z * 2 + me.c + step, 2 * RING)
        greet(me.at(z=other // 2, c=lax.rem(other, 2)))
    greet(me.at(xh=1 - me.xh))
    greet(me.at(xl=1 - me.xl))
    greet(me.at(xh=1 - me.xh, xl=1 - me.xl))
    greet(me.at(y=up))
    greet(me.at(y=down))
    greet(me.at(xh=1 - me.xh, z=RING - 1 - me.z, c=1 - me.c))

    def remote(src, dst, send, recv, device):
        return pltpu.make_async_remote_copy(
            src_ref=src, dst_ref=dst, send_sem=send, recv_sem=recv,
            device_id=device, device_id_type=MESH,
        )

    fill_taps(taps_ref)
    fill_transform(fwd_high, fwd_low)
    length = records.shape[2]
    stations = records.shape[1]
    for side in range(2):
        tail_own[side * stations : (side + 1) * stations, :] = records[
            blocks[side], :, length - LANE :
        ]
    pl.semaphore_wait(barrier, 2 * RING - 1 + 6)

    tm = lax.axis_index("tm")
    after = lax.rem(tm + 1, 4 * RING)
    tail_copy = remote(
        tail_own, tail_in, tail_sem.at[0], tail_sem.at[1],
        {"pair": lax.axis_index("pair"), "tm": after},
    )
    pl.when(tm < 4 * RING - 1)(tail_copy.start)
    count = live[tm]
    lane = lax.broadcasted_iota(jnp.int32, (1, LANE), 1)
    record = jnp.concatenate([records[blocks[0]], records[blocks[1]]], axis=0)
    span = DECIM * LANE
    pieces = []
    for b in range(SEG // LANE):
        both = dot(record[:, b * span : (b + 1) * span], taps_ref[LANE:, :])
        if b > 0:
            both = both + dot(record[:, b * span - LANE : b * span], taps_ref[:LANE, :])
        pieces.append(both)

    @pl.when(tm == 0)
    def _():
        tail_in[...] = jnp.zeros_like(tail_in)

    pl.when(tm > 0)(tail_copy.wait_recv)
    pieces[0] = pieces[0] + dot(tail_in[...], taps_ref[:LANE, :])
    filtered = jnp.concatenate(
        [
            jnp.where(lane + b * LANE < count, both[:, :LANE] + both[:, LANE:], 0.0)
            for b, both in enumerate(pieces)
        ],
        axis=1,
    )
    real, imag = whiten(filtered, fwd_high, fwd_low, padded)
    pack_columns(real, imag, col_ref)

    pending = []

    def start(copy, when=None):
        if when is None:
            copy.start()
        else:
            pl.when(when)(copy.start)
        pending.append((copy, when))

    for j in range(4):
        root_z, root_c = root_pair * 2 + j // 2, j % 2
        mine = (me.z == root_z) & (me.c == root_c)
        index = me.c * RING + me.z
        copy = remote(
            col_ref.at[j], stage.at[index], stage_send.at[j], stage_recv.at[index],
            me.at(z=root_z, c=root_c),
        )
        start(copy, jnp.logical_not(mine))

        @pl.when(mine)
        def _():
            pltpu.make_async_copy(col_ref.at[j], stage.at[index], stage_recv.at[index]).start()

    pack_rows(real, imag, row_ref)
    own = slot_of(me.xh, me.c, me.z)
    own_local = pltpu.make_async_copy(row_ref, row_all.at[own], local_sem.at[2 * RING])

    def part(s):
        return pl.ds(s * size, size)

    def spread(source, slot, h, d, sign, s):
        lower = s < PARTS // 2
        for way, target in ((1, right), (-1, left)):
            if sign not in (0, way) or d > 3 or (d == 3 and lower != (way == 1)):
                continue
            start(
                remote(
                    source.at[part(s)], row_all.at[slot, part(s)],
                    row_send.at[h, (0 if way == 1 else 4) + d, s], row_recv.at[slot, s],
                    me.at(z=target),
                )
            )
        number = d + 3 if sign == -1 and d < 4 else (7 if d == 4 else d)
        start(
            remote(
                source.at[part(s)], row_all.at[slot, part(s)], near_send.at[h, number, s],
                near_recv.at[slot, s], me.at(c=1 - me.c),
            )
        )

    def got_row(slot, s, sems):
        ref = row_all.at[slot, part(s)]
        remote(ref, ref, row_send.at[0, 0, 0], sems.at[slot, s], me.at()).wait_recv()

    def got_col(slot):
        ref = col_all.at[slot]
        remote(ref, ref, col_send.at[0, 0], col_recv.at[slot], me.at()).wait_recv()

    for s in range(PARTS):
        start(
            remote(
                row_ref.at[part(s)], row_all.at[own, part(s)], row_send.at[2, 0, s],
                row_recv.at[own, s], me.at(xh=1 - me.xh),
            )
        )
    for s in range(PARTS):
        spread(row_ref, own, 0, 0, 0, s)
    own_local.start()

    def zpiece(i):
        return lax.rem(me.z + OFFSETS[i] + RING, RING)

    def along(source, slot, c, when):
        start(
            remote(
                source, col_all.at[slot], col_send.at[slot, 1], col_recv.at[slot],
                me.at(y=up if c == 0 else down),
            ),
            when,
        )

    def sideways(source, slot, when, **there):
        start(
            remote(
                source, col_all.at[slot], col_send.at[slot, 0], col_recv.at[slot],
                me.at(xl=1 - me.xl, **there),
            ),
            when,
        )

    def hop(slot, c, when):
        pl.when(when)(lambda: got_col(slot))
        along(col_all.at[slot], slot, c, when)

    for kind, arg in schedule():
        if kind == "opposite":
            slot = slot_of(1 - me.xh, me.c, me.z)
            got_row(slot, arg, row_recv)
            spread(row_all.at[slot], slot, 1, 0, 0, arg)
        elif kind == "row":
            h, d, s = arg
            xh = me.xh if h == 0 else 1 - me.xh
            signs = (1, -1) if d < 4 else ((1,) if s < PARTS // 2 else (-1,))
            for sign in signs:
                slot = slot_of(xh, me.c, lax.rem(me.z - sign * d + RING, RING))
                got_row(slot, s, row_recv)
                spread(row_all.at[slot], slot, h, d, sign, s)
        elif kind == "root":
            for c in range(2):
                index = c * RING + zpiece(arg)
                slot = slot_of(me.xh, c, zpiece(arg))

                @pl.when(is_root)
                def _():
                    pltpu.make_async_copy(
                        stage.at[index], stage.at[index], stage_recv.at[index]
                    ).wait()

                @pl.when(is_near)
                def _():
                    pltpu.make_async_copy(
                        stage.at[index], col_all.at[slot], local_sem.at[2 * arg + c]
                    ).start()

                sideways(stage.at[index], slot, is_near)
                sideways(stage.at[index], slot, is_far, xh=1 - me.xh)
                along(stage.at[index], slot, c, is_near)
        elif kind == "other":
            for c in range(2):
                slot = slot_of(1 - me.xh, c, zpiece(arg))
                pl.when(is_other)(lambda slot=slot: got_col(slot))
                sideways(col_all.at[slot], slot, is_other)
                along(col_all.at[slot], slot, c, is_other)
            for c in range(2):
                hop(slot_of(me.xh, c, zpiece(arg)), c, is_other)
        elif kind == "near":
            for c in range(2):
                hop(slot_of(1 - me.xh, c, zpiece(arg)), c, is_near)
        elif kind == "hop1":
            for xh in (me.xh, 1 - me.xh):
                hop(slot_of(xh, 0, zpiece(arg)), 0, dy == 1)
                hop(slot_of(xh, 1, zpiece(arg)), 1, dy == 3)
        elif kind == "hop2":
            for xh in (me.xh, 1 - me.xh):
                for c in range(2):
                    hop(slot_of(xh, c, zpiece(arg)), c, dy == 2)
        elif kind == "last":
            for xh in (me.xh, 1 - me.xh):
                pl.when(dy == 3)(lambda xh=xh: got_col(slot_of(xh, 0, zpiece(arg))))
                pl.when(dy == 1)(lambda xh=xh: got_col(slot_of(xh, 1, zpiece(arg))))

    for h in range(2):
        for z in range(RING):
            for s in range(PARTS):
                got_row(slot_of(h, 1 - me.c, z), s, near_recv)
    own_local.wait()
    for i in range(RING):
        for c in range(2):
            index = c * RING + zpiece(i)
            slot = slot_of(me.xh, c, zpiece(i))

            @pl.when(is_near)
            def _():
                pltpu.make_async_copy(
                    stage.at[index], col_all.at[slot], local_sem.at[2 * i + c]
                ).wait()

    for copy, when in pending:
        if when is None:
            copy.wait_send()
        else:
            pl.when(when)(copy.wait_send)
    pl.when(tm < 4 * RING - 1)(tail_copy.wait_send)

    @pl.loop(0, CHUNKS)
    def _(chunk):
        cross_chunk(chunk, row_all, col_all, rows, cols, cross, stacked)


def cross_chunk(chunk, row_all, col_all, rows, cols, cross, stacked):
    segments = row_all.shape[0]
    half = LANE // 2
    group = 8
    count_k = QUARTERS * KCHUNK
    first = pl.multiple_of(chunk * KCHUNK, KCHUNK)
    for g in range(segments):
        for quarter in range(QUARTERS):
            at = g * STRIDE_K + quarter * KCHUNK
            rows[at : at + KCHUNK, :] = row_all[
                g, pl.ds(quarter * LANE + first, KCHUNK), :
            ].astype(F32)
        cols[g * STRIDE_C : g * STRIDE_C + KCHUNK, :] = col_all[
            g, pl.ds(first, KCHUNK), :
        ].astype(F32)
    lane = lax.broadcasted_iota(jnp.int32, (32, group * segments), 1)
    sign = jnp.where(
        lax.broadcasted_iota(jnp.int32, (1, LANE), 1) < half, 1.0, -1.0
    ).astype(F32)
    for block in range(KCHUNK // group):
        gathered = jnp.concatenate(
            [cols[pl.ds(block * group + b, segments, stride=STRIDE_C), :] for b in range(group)],
            axis=0,
        )
        turned = gathered.T.astype(BF16)
        for quarter in range(QUARTERS):
            left = turned[quarter * 32 : quarter * 32 + 32, :]
            zero = jnp.zeros_like(left)
            wide = jnp.concatenate(
                [
                    jnp.where((lane >= b * segments) & (lane < (b + 1) * segments), left, zero)
                    for b in range(group)
                ],
                axis=0,
            )
            base = quarter * KCHUNK + block * group
            right = jnp.concatenate(
                [rows[pl.ds(base + b, segments, stride=STRIDE_K), :] for b in range(group)],
                axis=0,
            ).astype(BF16)
            product = dot(wide, right)
            for b in range(group):
                top = product[b * 32 : b * 32 + 16, :]
                low = product[b * 32 + 16 : b * 32 + 32, :]
                cross[pl.ds(base + b, 16, stride=STRIDE_K), :] = top + sign * pltpu.roll(
                    low, half, 1
                )
    at = pl.multiple_of(chunk * count_k, LANE)
    for q in range(16):
        turned = cross[q * STRIDE_K : q * STRIDE_K + count_k, :].astype(BF16).T
        stacked[q * half : (q + 1) * half, pl.ds(at, count_k)] = turned[:half]
        stacked[q * half : (q + 1) * half, pl.ds(BINS + at, count_k)] = turned[half:]


def spectra(records, tile_blocks, live_len):
    dma = pltpu.SemaphoreType.DMA
    vmem = pl.BlockSpec(memory_space=pltpu.VMEM)
    smem = pl.BlockSpec(memory_space=pltpu.SMEM)
    return pl.pallas_call(
        spectra_kernel,
        in_specs=[smem, smem, vmem],
        out_specs=vmem,
        out_shape=jax.ShapeDtypeStruct((PAIRS, 2 * BINS), BF16),
        scratch_shapes=[
            pltpu.VMEM((LANE, LANE), BF16),
            pltpu.VMEM((LANE, LANE), BF16),
            pltpu.VMEM((5 * LANE, 2 * LANE), BF16),
            pltpu.VMEM((2 * BINS, SEG), BF16),
            pltpu.VMEM((2 * BINS, SEG), BF16),
            pltpu.VMEM((BINS + 16, LANE), F32),
            pltpu.VMEM((BINS, LANE), BF16),
            pltpu.VMEM((4, LANE, LANE), BF16),
            pltpu.VMEM((4 * RING, BINS, LANE), BF16),
            pltpu.VMEM((4 * RING, LANE, LANE), BF16),
            pltpu.VMEM((2 * RING, LANE, LANE), BF16),
            pltpu.VMEM((4 * RING * STRIDE_K, LANE), F32),
            pltpu.VMEM((4 * RING * STRIDE_C, LANE), F32),
            pltpu.VMEM((16 * STRIDE_K, LANE), F32),
            dma((2,)),
            dma((3, 8, PARTS)), dma((32, PARTS)), dma((2, 8, PARTS)), dma((32, PARTS)),
            dma((4,)), dma((2 * RING,)), dma((32, 2)), dma((32,)), dma((2 * RING + 1,)),
        ],
        compiler_params=pltpu.CompilerParams(
            collective_id=0, has_side_effects=True, vmem_limit_bytes=48 << 20
        ),
        name="spectra",
    )(tile_blocks, live_len, records)


def lags_kernel(stacked, lag_ref, out_ref, spare):
    half = LANE // 2
    value = dot(stacked[...], lag_ref[...])
    for q in range(16):
        for side in range(2):
            spare[side, q * STRIDE_P : q * STRIDE_P + half, :] = value[
                q * half : (q + 1) * half, side * LANE : (side + 1) * LANE
            ]
    for p in range(half):
        for side in range(2):
            out_ref[p * 16 : p * 16 + 16, side * LANE : (side + 1) * LANE] = spare[
                side, pl.ds(p, 16, stride=STRIDE_P), :
            ]


def lags(stacked):
    width = 2 * LANE
    tiles = -(-LAGS // width)
    table = jnp.asarray(np.pad(lag_table(), ((0, 0), (0, tiles * width - LAGS))))
    return pl.pallas_call(
        lags_kernel,
        grid=(tiles,),
        in_specs=[
            pl.BlockSpec((PAIRS, 2 * BINS), lambda i: (0, 0)),
            pl.BlockSpec((2 * BINS, width), lambda i: (0, i)),
        ],
        out_specs=pl.BlockSpec((PAIRS, width), lambda i: (0, i)),
        out_shape=jax.ShapeDtypeStruct((PAIRS, LAGS), F32),
        scratch_shapes=[pltpu.VMEM((2, 16 * STRIDE_P, LANE), F32)],
        compiler_params=pltpu.CompilerParams(vmem_limit_bytes=32 << 20),
        name="lags",
    )(stacked, table)


def shards(records, tile_blocks, live_len):
    result = lags(spectra(records, tile_blocks, live_len))
    return result.reshape(LANE // 2, 16, LAGS)


def solution(mesh):
    placed = (P(None, "pair", "tm"), P(), P())
    return jax.shard_map(
        shards, mesh=mesh, in_specs=placed, out_specs=P("pair", "tm", None), check_vma=False
    )
```

```python
import math

import jax
import jax.numpy as jnp
import ml_dtypes
import numpy as np
from jax import lax
from jax.experimental import pallas as pl
from jax.experimental.pallas import tpu as pltpu
from jax.sharding import PartitionSpec as P

DECIM = 4
TAPS = 64
SEG = 512
NFT = 1024
MAXLAG = 400
SMOOTH = 4
BINS = 512
LAGS = 801
LANE = 128
QUARTERS = 4
CHUNKS = 4
KCHUNK = LANE // CHUNKS
PAIRS = 1024
STRIDE_K = QUARTERS * KCHUNK + 8
STRIDE_C = KCHUNK + 8
STRIDE_P = LANE // 2 + 8
TWO_PI = 2.0 * math.pi / NFT
F32 = jnp.float32
BF16 = jnp.bfloat16
MESH = pl.DeviceIdType.MESH
RING = 8
YRING = 4
OFFSETS = (0, 1, -1, 2, -2, 3, -3, 4)
PARTS = 2
OPP_TIME = 3.0
ROW_START, ROW_STEP = 6.0, 6.0
COL_STEP = 1.5
COL_TIMES = (
    ("root", 1.5),
    ("other", 8.0),
    ("near", 10.5),
    ("hop1", 13.0),
    ("hop2", 16.0),
    ("last", 40.0),
)


def turns(rows, step, columns):
    row = lax.broadcasted_iota(jnp.int32, (rows, columns), 0) * step
    index = (row * lax.broadcasted_iota(jnp.int32, (rows, columns), 1)) & (NFT - 1)
    index = jnp.where(index >= NFT // 2, index - NFT, index)
    phase = index.astype(F32) * TWO_PI
    return jnp.cos(phase), jnp.sin(phase)


def fill_taps(taps_ref):
    row = lax.broadcasted_iota(jnp.int32, (8, LANE), 0)
    lane = lax.broadcasted_iota(jnp.int32, (8, LANE), 1)
    index = row - TAPS - DECIM * (lane - LANE)
    inside = (index >= 0) & (index < TAPS)
    position = jnp.where(inside, index, 0).astype(F32)
    centred = (position - (TAPS - 1) / 2.0) * (1.0 / DECIM)
    window = 0.5 * (1.0 - jnp.cos((2.0 * math.pi / TAPS) * (position + 0.5)))
    turn = math.pi * centred
    value = jnp.where(inside, window * jnp.sin(turn) / turn * (1.0 / DECIM), 0.0)
    shift = 8 // DECIM
    for r in range(0, 5 * LANE // 8, 2):
        pair = []
        for one in (r, r + 1):
            moved = value
            if one * shift % LANE:
                moved = pltpu.roll(value, one * shift % LANE, 1)
            offset = row - TAPS - DECIM * (lane - one * shift)
            pair.append(jnp.where((offset >= 0) & (offset < TAPS), moved, 0.0))
        high, low = split(jnp.concatenate(pair, axis=0))
        taps_ref[8 * r : 8 * r + 16, :LANE] = high
        taps_ref[8 * r : 8 * r + 16, LANE:] = low


def bin_order():
    chunk = np.arange(CHUNKS)[:, None, None]
    quarter = np.arange(QUARTERS)[None, :, None]
    inner = np.arange(KCHUNK)[None, None, :]
    return (quarter * LANE + chunk * KCHUNK + inner).reshape(-1)


def lag_table():
    bins = bin_order()
    shifts = np.arange(LAGS) - MAXLAG
    phase = (bins[:, None] * shifts[None, :] % NFT) * TWO_PI
    weights = np.where(bins == 0, 1.0, 2.0)[:, None] / math.sqrt(NFT)
    table = np.concatenate([weights * np.cos(phase), -weights * np.sin(phase)], axis=0)
    return table.astype(ml_dtypes.bfloat16)


def split(value):
    high = value.astype(BF16)
    return high, (value - high.astype(F32)).astype(BF16)


def dot(a, b, dims=((1,), (0,))):
    return lax.dot_general(a, b, (dims, ((), ())), preferred_element_type=F32)


def fill_transform(fwd_high, fwd_low):
    coarse_cos, coarse_sin = turns(BINS // 8, 8, SEG)
    fine_cos, fine_sin = turns(8, 1, SEG)
    for a in range(0, BINS // 8, 2):
        reals, imags = [], []
        for one in (a, a + 1):
            cc, cs = coarse_cos[one : one + 1, :], coarse_sin[one : one + 1, :]
            reals.append(cc * fine_cos - cs * fine_sin)
            imags.append(-(cs * fine_cos + cc * fine_sin))
        for value, base in ((reals, 8 * a), (imags, BINS + 8 * a)):
            high, low = split(jnp.concatenate(value, axis=0))
            fwd_high[base : base + 16, :] = high
            fwd_low[base : base + 16, :] = low


def whiten(filtered, fwd_high, fwd_low, padded):
    high, low = split(filtered)
    last = ((1,), (1,))
    spectra = (
        dot(fwd_high[...], low, last)
        + dot(fwd_low[...], high, last)
        + dot(fwd_high[...], high, last)
    )
    real, imag = spectra[:BINS], spectra[BINS:]
    amplitude = jnp.sqrt(real * real + imag * imag)
    padded[0:8, :] = jnp.zeros((8, LANE), F32)
    padded[8 + BINS : 16 + BINS, :] = jnp.zeros((8, LANE), F32)
    padded[8 : 8 + BINS, :] = amplitude
    smooth = padded[8 - SMOOTH : 8 - SMOOTH + BINS, :]
    for offset in range(1, 2 * SMOOTH + 1):
        start = 8 - SMOOTH + offset
        smooth = smooth + padded[start : start + BINS, :]
    mean = jnp.sum(amplitude, axis=0, keepdims=True) * (1.0 / BINS)
    level = smooth * (1.0 / (2 * SMOOTH + 1)) + 0.05 * mean + 1e-06
    inverse = 1.0 / level
    return real * inverse, imag * inverse


def pack_rows(real, imag, row_own):
    half = LANE // 2
    lower = lax.broadcasted_iota(jnp.int32, (BINS, LANE), 1) < half
    row_own[...] = jnp.where(lower, real, pltpu.roll(imag, half, 1)).astype(BF16)


def pack_columns(real, imag, col_own):
    half = LANE // 2
    lower = lax.broadcasted_iota(jnp.int32, (BINS, LANE), 1) < half
    cols = jnp.where(lower, pltpu.roll(real, half, 1), imag)
    lanes = lax.broadcasted_iota(jnp.int32, (LANE, LANE), 1)
    for j in range(4):
        total = jnp.zeros((LANE, LANE), F32)
        for quarter in range(QUARTERS):
            part = cols[quarter * LANE : (quarter + 1) * LANE, :]
            for c in range(2):
                source = c * half + 16 * j
                target = quarter * 32 + 16 * c
                moved = part
                if (target - source) % LANE:
                    moved = pltpu.roll(part, (target - source) % LANE, 1)
                keep = (lanes >= target) & (lanes < target + 16)
                total = jnp.where(keep, moved, total)
        col_own[j] = total.astype(BF16)


class Place:
    def __init__(self):
        pair, tm = lax.axis_index("pair"), lax.axis_index("tm")
        self.y, self.xl = pair // 2, lax.rem(pair, 2)
        self.xh, self.z, self.c = tm // 16, lax.rem(tm // 2, RING), lax.rem(tm, 2)

    def at(self, y=None, xl=None, xh=None, z=None, c=None):
        pick = lambda new, old: old if new is None else new
        y, xl, xh = pick(y, self.y), pick(xl, self.xl), pick(xh, self.xh)
        z, c = pick(z, self.z), pick(c, self.c)
        return {"pair": y * 2 + xl, "tm": xh * 16 + z * 2 + c}


def slot_of(xh, c, z):
    return xh * 16 + c * RING + z


def schedule():
    events = []
    for i in range(RING):
        for kind, late in COL_TIMES:
            events.append((late + COL_STEP * i, kind, i))
    for s in range(PARTS):
        events.append((OPP_TIME + 0.1 * s, "opposite", s))
        for d in range(1, 5):
            for h in range(2):
                at = ROW_START + ROW_STEP * (d - 1) + (0.5 * ROW_STEP * h + 0.45 * ROW_STEP * s / PARTS)
                events.append((at, "row", (h, d, s)))
    events.sort(key=lambda e: e[0])
    return [(kind, arg) for _, kind, arg in events]


def spectra_kernel(
    blocks_in, live_in, records_in, stacked_out,
    stacked, blocks, live, records, tail_own, tail_in, taps_ref, fwd_high, fwd_low, padded, row_ref, col_ref,
    row_all, col_all, stage, rows, cols, cross,
    out_sem, load_sem, tail_sem, row_send, row_recv, near_send, near_recv, stage_send, stage_recv,
    col_send, col_recv, local_sem,
):
    me = Place()
    size = BINS // PARTS
    group_xh = me.y // 2
    home_y = me.xh * 2 + me.z // 4
    home_xl = lax.rem(me.z // 2, 2)
    dy = lax.rem(me.y - home_y + YRING, YRING)
    root_pair = lax.rem(me.y, 2) * 2 + me.xl
    is_root = (me.z // 2) == root_pair
    is_near = is_root & (me.xh == group_xh)
    is_far = is_root & (me.xh != group_xh)
    is_other = (dy == 0) & (me.xl != home_xl)
    up, down = lax.rem(me.y + 1, YRING), lax.rem(me.y + YRING - 1, YRING)
    right, left = lax.rem(me.z + 1, RING), lax.rem(me.z + RING - 1, RING)

    loads = [
        pltpu.make_async_copy(source, target, load_sem.at[i])
        for i, (source, target) in enumerate(
            ((records_in, records), (blocks_in, blocks), (live_in, live))
        )
    ]
    for load in loads:
        load.start()
    barrier = pltpu.get_barrier_semaphore()

    def greet(device):
        pl.semaphore_signal(barrier, inc=1, device_id=device, device_id_type=MESH)

    for step in range(1, 2 * RING):
        other = lax.rem(me.z * 2 + me.c + step, 2 * RING)
        greet(me.at(z=other // 2, c=lax.rem(other, 2)))
    greet(me.at(xh=1 - me.xh))
    greet(me.at(xl=1 - me.xl))
    greet(me.at(xh=1 - me.xh, xl=1 - me.xl))
    greet(me.at(y=up))
    greet(me.at(y=down))
    greet(me.at(xh=1 - me.xh, z=RING - 1 - me.z, c=1 - me.c))

    def remote(src, dst, send, recv, device):
        return pltpu.make_async_remote_copy(
            src_ref=src, dst_ref=dst, send_sem=send, recv_sem=recv,
            device_id=device, device_id_type=MESH,
        )

    fill_taps(taps_ref)
    for load in loads:
        load.wait()
    length = records.shape[2]
    stations = records.shape[1]
    for side in range(2):
        tail_own[side * stations : (side + 1) * stations, :] = records[
            blocks[side], :, length - LANE :
        ]
    pl.semaphore_wait(barrier, 2 * RING - 1 + 6)

    tm = lax.axis_index("tm")
    after = lax.rem(tm + 1, 4 * RING)
    tail_copy = remote(
        tail_own, tail_in, tail_sem.at[0], tail_sem.at[1],
        {"pair": lax.axis_index("pair"), "tm": after},
    )
    pl.when(tm < 4 * RING - 1)(tail_copy.start)
    fill_transform(fwd_high, fwd_low)
    count = live[tm]
    lane = lax.broadcasted_iota(jnp.int32, (1, LANE), 1)
    record = jnp.concatenate([records[blocks[0]], records[blocks[1]]], axis=0)
    span = DECIM * LANE
    pieces = []
    for b in range(SEG // LANE):
        both = dot(record[:, b * span : (b + 1) * span], taps_ref[LANE:, :])
        if b > 0:
            both = both + dot(record[:, b * span - LANE : b * span], taps_ref[:LANE, :])
        pieces.append(both)

    @pl.when(tm == 0)
    def _():
        tail_in[...] = jnp.zeros_like(tail_in)

    pl.when(tm > 0)(tail_copy.wait_recv)
    pieces[0] = pieces[0] + dot(tail_in[...], taps_ref[:LANE, :])
    filtered = jnp.concatenate(
        [
            jnp.where(lane + b * LANE < count, both[:, :LANE] + both[:, LANE:], 0.0)
            for b, both in enumerate(pieces)
        ],
        axis=1,
    )
    real, imag = whiten(filtered, fwd_high, fwd_low, padded)
    pack_columns(real, imag, col_ref)

    pending = []

    def start(copy, when=None):
        if when is None:
            copy.start()
        else:
            pl.when(when)(copy.start)
        pending.append((copy, when))

    for j in range(4):
        root_z, root_c = root_pair * 2 + j // 2, j % 2
        mine = (me.z == root_z) & (me.c == root_c)
        index = me.c * RING + me.z
        copy = remote(
            col_ref.at[j], stage.at[index], stage_send.at[j], stage_recv.at[index],
            me.at(z=root_z, c=root_c),
        )
        start(copy, jnp.logical_not(mine))

        @pl.when(mine)
        def _():
            pltpu.make_async_copy(col_ref.at[j], stage.at[index], stage_recv.at[index]).start()

    pack_rows(real, imag, row_ref)
    own = slot_of(me.xh, me.c, me.z)
    own_local = pltpu.make_async_copy(row_ref, row_all.at[own], local_sem.at[2 * RING])

    def part(s):
        return pl.ds(s * size, size)

    def spread(source, slot, h, d, sign, s):
        lower = s < PARTS // 2
        for way, target in ((1, right), (-1, left)):
            if sign not in (0, way) or d > 3 or (d == 3 and lower != (way == 1)):
                continue
            start(
                remote(
                    source.at[part(s)], row_all.at[slot, part(s)],
                    row_send.at[h, (0 if way == 1 else 4) + d, s], row_recv.at[slot, s],
                    me.at(z=target),
                )
            )
        number = d + 3 if sign == -1 and d < 4 else (7 if d == 4 else d)
        start(
            remote(
                source.at[part(s)], row_all.at[slot, part(s)], near_send.at[h, number, s],
                near_recv.at[slot, s], me.at(c=1 - me.c),
            )
        )

    def got_row(slot, s, sems):
        ref = row_all.at[slot, part(s)]
        remote(ref, ref, row_send.at[0, 0, 0], sems.at[slot, s], me.at()).wait_recv()

    def got_col(slot):
        ref = col_all.at[slot]
        remote(ref, ref, col_send.at[0, 0], col_recv.at[slot], me.at()).wait_recv()

    for s in range(PARTS):
        start(
            remote(
                row_ref.at[part(s)], row_all.at[own, part(s)], row_send.at[2, 0, s],
                row_recv.at[own, s], me.at(xh=1 - me.xh),
            )
        )
    for s in range(PARTS):
        spread(row_ref, own, 0, 0, 0, s)
    own_local.start()

    def zpiece(i):
        return lax.rem(me.z + OFFSETS[i] + RING, RING)

    def along(source, slot, c, when):
        start(
            remote(
                source, col_all.at[slot], col_send.at[slot, 1], col_recv.at[slot],
                me.at(y=up if c == 0 else down),
            ),
            when,
        )

    def sideways(source, slot, when, **there):
        start(
            remote(
                source, col_all.at[slot], col_send.at[slot, 0], col_recv.at[slot],
                me.at(xl=1 - me.xl, **there),
            ),
            when,
        )

    def hop(slot, c, when):
        pl.when(when)(lambda: got_col(slot))
        along(col_all.at[slot], slot, c, when)

    for kind, arg in schedule():
        if kind == "opposite":
            slot = slot_of(1 - me.xh, me.c, me.z)
            got_row(slot, arg, row_recv)
            spread(row_all.at[slot], slot, 1, 0, 0, arg)
        elif kind == "row":
            h, d, s = arg
            xh = me.xh if h == 0 else 1 - me.xh
            signs = (1, -1) if d < 4 else ((1,) if s < PARTS // 2 else (-1,))
            for sign in signs:
                slot = slot_of(xh, me.c, lax.rem(me.z - sign * d + RING, RING))
                got_row(slot, s, row_recv)
                spread(row_all.at[slot], slot, h, d, sign, s)
        elif kind == "root":
            for c in range(2):
                index = c * RING + zpiece(arg)
                slot = slot_of(me.xh, c, zpiece(arg))

                @pl.when(is_root)
                def _():
                    pltpu.make_async_copy(
                        stage.at[index], stage.at[index], stage_recv.at[index]
                    ).wait()

                @pl.when(is_near)
                def _():
                    pltpu.make_async_copy(
                        stage.at[index], col_all.at[slot], local_sem.at[2 * arg + c]
                    ).start()

                sideways(stage.at[index], slot, is_near)
                sideways(stage.at[index], slot, is_far, xh=1 - me.xh)
                along(stage.at[index], slot, c, is_near)
        elif kind == "other":
            for c in range(2):
                slot = slot_of(1 - me.xh, c, zpiece(arg))
                pl.when(is_other)(lambda slot=slot: got_col(slot))
                sideways(col_all.at[slot], slot, is_other)
                along(col_all.at[slot], slot, c, is_other)
            for c in range(2):
                hop(slot_of(me.xh, c, zpiece(arg)), c, is_other)
        elif kind == "near":
            for c in range(2):
                hop(slot_of(1 - me.xh, c, zpiece(arg)), c, is_near)
        elif kind == "hop1":
            for xh in (me.xh, 1 - me.xh):
                hop(slot_of(xh, 0, zpiece(arg)), 0, dy == 1)
                hop(slot_of(xh, 1, zpiece(arg)), 1, dy == 3)
        elif kind == "hop2":
            for xh in (me.xh, 1 - me.xh):
                for c in range(2):
                    hop(slot_of(xh, c, zpiece(arg)), c, dy == 2)
        elif kind == "last":
            for xh in (me.xh, 1 - me.xh):
                pl.when(dy == 3)(lambda xh=xh: got_col(slot_of(xh, 0, zpiece(arg))))
                pl.when(dy == 1)(lambda xh=xh: got_col(slot_of(xh, 1, zpiece(arg))))

    for h in range(2):
        for z in range(RING):
            for s in range(PARTS):
                got_row(slot_of(h, 1 - me.c, z), s, near_recv)
    own_local.wait()
    for i in range(RING):
        for c in range(2):
            index = c * RING + zpiece(i)
            slot = slot_of(me.xh, c, zpiece(i))

            @pl.when(is_near)
            def _():
                pltpu.make_async_copy(
                    stage.at[index], col_all.at[slot], local_sem.at[2 * i + c]
                ).wait()

    for copy, when in pending:
        if when is None:
            copy.wait_send()
        else:
            pl.when(when)(copy.wait_send)
    pl.when(tm < 4 * RING - 1)(tail_copy.wait_send)

    def chunk_copies(chunk):
        return [
            pltpu.make_async_copy(
                stacked.at[:, pl.ds(pl.multiple_of(side * BINS + chunk * LANE, LANE), LANE)],
                stacked_out.at[:, pl.ds(pl.multiple_of(side * BINS + chunk * LANE, LANE), LANE)],
                out_sem.at[side, chunk],
            )
            for side in range(2)
        ]

    @pl.loop(0, CHUNKS)
    def _(chunk):
        cross_chunk(chunk, row_all, col_all, rows, cols, cross, stacked)
        for copy in chunk_copies(chunk):
            copy.start()

    @pl.loop(0, CHUNKS)
    def _(chunk):
        for copy in chunk_copies(chunk):
            copy.wait()


def cross_chunk(chunk, row_all, col_all, rows, cols, cross, stacked):
    segments = row_all.shape[0]
    half = LANE // 2
    group = 8
    count_k = QUARTERS * KCHUNK
    first = pl.multiple_of(chunk * KCHUNK, KCHUNK)
    for g in range(segments):
        for quarter in range(QUARTERS):
            at = g * STRIDE_K + quarter * KCHUNK
            rows[at : at + KCHUNK, :] = row_all[
                g, pl.ds(quarter * LANE + first, KCHUNK), :
            ].astype(F32)
        cols[g * STRIDE_C : g * STRIDE_C + KCHUNK, :] = col_all[
            g, pl.ds(first, KCHUNK), :
        ].astype(F32)
    lane = lax.broadcasted_iota(jnp.int32, (32, group * segments), 1)
    sign = jnp.where(
        lax.broadcasted_iota(jnp.int32, (1, LANE), 1) < half, 1.0, -1.0
    ).astype(F32)
    for block in range(KCHUNK // group):
        gathered = jnp.concatenate(
            [cols[pl.ds(block * group + b, segments, stride=STRIDE_C), :] for b in range(group)],
            axis=0,
        )
        turned = gathered.T.astype(BF16)
        for quarter in range(QUARTERS):
            left = turned[quarter * 32 : quarter * 32 + 32, :]
            zero = jnp.zeros_like(left)
            wide = jnp.concatenate(
                [
                    jnp.where((lane >= b * segments) & (lane < (b + 1) * segments), left, zero)
                    for b in range(group)
                ],
                axis=0,
            )
            base = quarter * KCHUNK + block * group
            right = jnp.concatenate(
                [rows[pl.ds(base + b, segments, stride=STRIDE_K), :] for b in range(group)],
                axis=0,
            ).astype(BF16)
            product = dot(wide, right)
            for b in range(group):
                top = product[b * 32 : b * 32 + 16, :]
                low = product[b * 32 + 16 : b * 32 + 32, :]
                cross[pl.ds(base + b, 16, stride=STRIDE_K), :] = top + sign * pltpu.roll(
                    low, half, 1
                )
    at = pl.multiple_of(chunk * count_k, LANE)
    for q in range(16):
        turned = cross[q * STRIDE_K : q * STRIDE_K + count_k, :].astype(BF16).T
        stacked[q * half : (q + 1) * half, pl.ds(at, count_k)] = turned[:half]
        stacked[q * half : (q + 1) * half, pl.ds(BINS + at, count_k)] = turned[half:]


def spectra(records, tile_blocks, live_len):
    dma = pltpu.SemaphoreType.DMA
    return pl.pallas_call(
        spectra_kernel,
        in_specs=[pl.BlockSpec(memory_space=pltpu.HBM)] * 3,
        out_specs=pl.BlockSpec(memory_space=pltpu.HBM),
        out_shape=jax.ShapeDtypeStruct((PAIRS, 2 * BINS), BF16),
        scratch_shapes=[
            pltpu.VMEM((PAIRS, 2 * BINS), BF16),
            pltpu.SMEM(tile_blocks.shape, jnp.int32),
            pltpu.SMEM(live_len.shape, jnp.int32),
            pltpu.VMEM(records.shape, BF16),
            pltpu.VMEM((LANE, LANE), BF16),
            pltpu.VMEM((LANE, LANE), BF16),
            pltpu.VMEM((5 * LANE, 2 * LANE), BF16),
            pltpu.VMEM((2 * BINS, SEG), BF16),
            pltpu.VMEM((2 * BINS, SEG), BF16),
            pltpu.VMEM((BINS + 16, LANE), F32),
            pltpu.VMEM((BINS, LANE), BF16),
            pltpu.VMEM((4, LANE, LANE), BF16),
            pltpu.VMEM((4 * RING, BINS, LANE), BF16),
            pltpu.VMEM((4 * RING, LANE, LANE), BF16),
            pltpu.VMEM((2 * RING, LANE, LANE), BF16),
            pltpu.VMEM((4 * RING * STRIDE_K, LANE), F32),
            pltpu.VMEM((4 * RING * STRIDE_C, LANE), F32),
            pltpu.VMEM((16 * STRIDE_K, LANE), F32),
            dma((2, CHUNKS)), dma((3,)), dma((2,)),
            dma((3, 8, PARTS)), dma((32, PARTS)), dma((2, 8, PARTS)), dma((32, PARTS)),
            dma((4,)), dma((2 * RING,)), dma((32, 2)), dma((32,)), dma((2 * RING + 1,)),
        ],
        compiler_params=pltpu.CompilerParams(
            collective_id=0, has_side_effects=True, vmem_limit_bytes=60 << 20
        ),
        name="spectra",
    )(tile_blocks, live_len, records)


def lags_kernel(stacked, lag_ref, out_ref, spare):
    half = LANE // 2
    value = dot(stacked[...], lag_ref[...])
    for q in range(16):
        for side in range(2):
            spare[side, q * STRIDE_P : q * STRIDE_P + half, :] = value[
                q * half : (q + 1) * half, side * LANE : (side + 1) * LANE
            ]
    for p in range(half):
        for side in range(2):
            out_ref[p * 16 : p * 16 + 16, side * LANE : (side + 1) * LANE] = spare[
                side, pl.ds(p, 16, stride=STRIDE_P), :
            ]


def lags(stacked):
    width = 2 * LANE
    tiles = -(-LAGS // width)
    table = jnp.asarray(np.pad(lag_table(), ((0, 0), (0, tiles * width - LAGS))))
    return pl.pallas_call(
        lags_kernel,
        grid=(tiles,),
        in_specs=[
            pl.BlockSpec((PAIRS, 2 * BINS), lambda i: (0, 0)),
            pl.BlockSpec((2 * BINS, width), lambda i: (0, i)),
        ],
        out_specs=pl.BlockSpec((PAIRS, width), lambda i: (0, i)),
        out_shape=jax.ShapeDtypeStruct((PAIRS, LAGS), F32),
        scratch_shapes=[pltpu.VMEM((2, 16 * STRIDE_P, LANE), F32)],
        compiler_params=pltpu.CompilerParams(vmem_limit_bytes=32 << 20),
        name="lags",
    )(stacked, table)


def shards(records, tile_blocks, live_len):
    result = lags(spectra(records, tile_blocks, live_len))
    return result.reshape(LANE // 2, 16, LAGS)


def solution(mesh):
    placed = (P(None, "pair", "tm"), P(), P())
    return jax.shard_map(
        shards, mesh=mesh, in_specs=placed, out_specs=P("pair", "tm", None), check_vma=False
    )
```

```python
import math

import jax
import jax.numpy as jnp
import ml_dtypes
import numpy as np
from jax import lax
from jax.experimental import pallas as pl
from jax.experimental.pallas import tpu as pltpu
from jax.sharding import PartitionSpec as P

DECIM = 4
TAPS = 64
SEG = 512
NFT = 1024
MAXLAG = 400
SMOOTH = 4
BINS = 512
LAGS = 801
LANE = 128
QUARTERS = 4
CHUNKS = 4
KCHUNK = LANE // CHUNKS
PAIRS = 1024
STRIDE_K = QUARTERS * KCHUNK + 8
STRIDE_C = KCHUNK + 8
STRIDE_P = LANE // 2 + 8
TWO_PI = 2.0 * math.pi / NFT
F32 = jnp.float32
BF16 = jnp.bfloat16
MESH = pl.DeviceIdType.MESH
RING = 8
YRING = 4
OFFSETS = (0, 1, -1, 2, -2, 3, -3, 4)
PARTS = 2
OPP_TIME = 3.0
ROW_START, ROW_STEP = 6.0, 6.0
COL_STEP = 1.5
COL_TIMES = (
    ("root", 1.5),
    ("other", 8.0),
    ("near", 8.1),
    ("hop1", 11.0),
    ("hop2", 14.0),
    ("last", 40.0),
)


def turns(rows, step, columns):
    row = lax.broadcasted_iota(jnp.int32, (rows, columns), 0) * step
    index = (row * lax.broadcasted_iota(jnp.int32, (rows, columns), 1)) & (NFT - 1)
    index = jnp.where(index >= NFT // 2, index - NFT, index)
    phase = index.astype(F32) * TWO_PI
    return jnp.cos(phase), jnp.sin(phase)


def fill_taps(taps_ref):
    row = lax.broadcasted_iota(jnp.int32, (8, LANE), 0)
    lane = lax.broadcasted_iota(jnp.int32, (8, LANE), 1)
    index = row - TAPS - DECIM * (lane - LANE)
    inside = (index >= 0) & (index < TAPS)
    position = jnp.where(inside, index, 0).astype(F32)
    centred = (position - (TAPS - 1) / 2.0) * (1.0 / DECIM)
    window = 0.5 * (1.0 - jnp.cos((2.0 * math.pi / TAPS) * (position + 0.5)))
    turn = math.pi * centred
    value = jnp.where(inside, window * jnp.sin(turn) / turn * (1.0 / DECIM), 0.0)
    shift = 8 // DECIM
    for r in range(0, 5 * LANE // 8, 2):
        pair = []
        for one in (r, r + 1):
            moved = value
            if one * shift % LANE:
                moved = pltpu.roll(value, one * shift % LANE, 1)
            offset = row - TAPS - DECIM * (lane - one * shift)
            pair.append(jnp.where((offset >= 0) & (offset < TAPS), moved, 0.0))
        high, low = split(jnp.concatenate(pair, axis=0))
        taps_ref[8 * r : 8 * r + 16, :LANE] = high
        taps_ref[8 * r : 8 * r + 16, LANE:] = low


def bin_order():
    chunk = np.arange(CHUNKS)[:, None, None]
    quarter = np.arange(QUARTERS)[None, :, None]
    inner = np.arange(KCHUNK)[None, None, :]
    return (quarter * LANE + chunk * KCHUNK + inner).reshape(-1)


def lag_table():
    bins = bin_order()
    shifts = np.arange(LAGS) - MAXLAG
    phase = (bins[:, None] * shifts[None, :] % NFT) * TWO_PI
    weights = np.where(bins == 0, 1.0, 2.0)[:, None] / math.sqrt(NFT)
    table = np.concatenate([weights * np.cos(phase), -weights * np.sin(phase)], axis=0)
    return table.astype(ml_dtypes.bfloat16)


def split(value):
    high = value.astype(BF16)
    return high, (value - high.astype(F32)).astype(BF16)


def dot(a, b, dims=((1,), (0,))):
    return lax.dot_general(a, b, (dims, ((), ())), preferred_element_type=F32)


def fill_transform(fwd_high, fwd_low):
    coarse_cos, coarse_sin = turns(BINS // 8, 8, SEG)
    fine_cos, fine_sin = turns(8, 1, SEG)
    for a in range(0, BINS // 8, 2):
        reals, imags = [], []
        for one in (a, a + 1):
            cc, cs = coarse_cos[one : one + 1, :], coarse_sin[one : one + 1, :]
            reals.append(cc * fine_cos - cs * fine_sin)
            imags.append(-(cs * fine_cos + cc * fine_sin))
        for value, base in ((reals, 8 * a), (imags, BINS + 8 * a)):
            high, low = split(jnp.concatenate(value, axis=0))
            fwd_high[base : base + 16, :] = high
            fwd_low[base : base + 16, :] = low


def whiten(filtered, fwd_high, fwd_low, padded):
    high, low = split(filtered)
    last = ((1,), (1,))
    spectra = (
        dot(fwd_high[...], low, last)
        + dot(fwd_low[...], high, last)
        + dot(fwd_high[...], high, last)
    )
    real, imag = spectra[:BINS], spectra[BINS:]
    amplitude = jnp.sqrt(real * real + imag * imag)
    padded[0:8, :] = jnp.zeros((8, LANE), F32)
    padded[8 + BINS : 16 + BINS, :] = jnp.zeros((8, LANE), F32)
    padded[8 : 8 + BINS, :] = amplitude
    smooth = padded[8 - SMOOTH : 8 - SMOOTH + BINS, :]
    for offset in range(1, 2 * SMOOTH + 1):
        start = 8 - SMOOTH + offset
        smooth = smooth + padded[start : start + BINS, :]
    mean = jnp.sum(amplitude, axis=0, keepdims=True) * (1.0 / BINS)
    level = smooth * (1.0 / (2 * SMOOTH + 1)) + 0.05 * mean + 1e-06
    inverse = 1.0 / level
    return real * inverse, imag * inverse


def pack_rows(real, imag, row_own):
    half = LANE // 2
    lower = lax.broadcasted_iota(jnp.int32, (BINS, LANE), 1) < half
    row_own[...] = jnp.where(lower, real, pltpu.roll(imag, half, 1)).astype(BF16)


def pack_columns(real, imag, col_own):
    half = LANE // 2
    lower = lax.broadcasted_iota(jnp.int32, (BINS, LANE), 1) < half
    cols = jnp.where(lower, pltpu.roll(real, half, 1), imag)
    lanes = lax.broadcasted_iota(jnp.int32, (LANE, LANE), 1)
    for j in range(4):
        total = jnp.zeros((LANE, LANE), F32)
        for quarter in range(QUARTERS):
            part = cols[quarter * LANE : (quarter + 1) * LANE, :]
            for c in range(2):
                source = c * half + 16 * j
                target = quarter * 32 + 16 * c
                moved = part
                if (target - source) % LANE:
                    moved = pltpu.roll(part, (target - source) % LANE, 1)
                keep = (lanes >= target) & (lanes < target + 16)
                total = jnp.where(keep, moved, total)
        col_own[j] = total.astype(BF16)


class Place:
    def __init__(self):
        pair, tm = lax.axis_index("pair"), lax.axis_index("tm")
        self.y, self.xl = pair // 2, lax.rem(pair, 2)
        self.xh, self.z, self.c = tm // 16, lax.rem(tm // 2, RING), lax.rem(tm, 2)

    def at(self, y=None, xl=None, xh=None, z=None, c=None):
        pick = lambda new, old: old if new is None else new
        y, xl, xh = pick(y, self.y), pick(xl, self.xl), pick(xh, self.xh)
        z, c = pick(z, self.z), pick(c, self.c)
        return {"pair": y * 2 + xl, "tm": xh * 16 + z * 2 + c}


def slot_of(xh, c, z):
    return xh * 16 + c * RING + z


def schedule():
    events = []
    for i in range(RING):
        for kind, late in COL_TIMES:
            events.append((late + COL_STEP * i, kind, i))
    for s in range(PARTS):
        events.append((OPP_TIME + 0.1 * s, "opposite", s))
        for d in range(1, 5):
            for h in range(2):
                at = ROW_START + ROW_STEP * (d - 1) + (0.5 * ROW_STEP * h + 0.45 * ROW_STEP * s / PARTS)
                events.append((at, "row", (h, d, s)))
    events.sort(key=lambda e: e[0])
    return [(kind, arg) for _, kind, arg in events]


def spectra_kernel(
    blocks_in, live_in, records_in, stacked_out,
    stacked, blocks, live, records, tail_own, tail_in, taps_ref, fwd_high, fwd_low, padded, row_ref, col_ref,
    row_all, col_all, stage, rows, cols, cross,
    out_sem, load_sem, tail_sem, row_send, row_recv, near_send, near_recv, stage_send, stage_recv,
    col_send, col_recv, local_sem,
):
    me = Place()
    size = BINS // PARTS
    group_xh = me.y // 2
    home_y = me.xh * 2 + me.z // 4
    home_xl = lax.rem(me.z // 2, 2)
    dy = lax.rem(me.y - home_y + YRING, YRING)
    root_pair = lax.rem(me.y, 2) * 2 + me.xl
    is_root = (me.z // 2) == root_pair
    is_near = is_root & (me.xh == group_xh)
    is_far = is_root & (me.xh != group_xh)
    is_other = (dy == 0) & (me.xl != home_xl)
    up, down = lax.rem(me.y + 1, YRING), lax.rem(me.y + YRING - 1, YRING)
    right, left = lax.rem(me.z + 1, RING), lax.rem(me.z + RING - 1, RING)

    loads = [
        pltpu.make_async_copy(source, target, load_sem.at[i])
        for i, (source, target) in enumerate(
            ((records_in, records), (blocks_in, blocks), (live_in, live))
        )
    ]
    for load in loads:
        load.start()
    barrier = pltpu.get_barrier_semaphore()

    def greet(device):
        pl.semaphore_signal(barrier, inc=1, device_id=device, device_id_type=MESH)

    for step in range(1, 2 * RING):
        other = lax.rem(me.z * 2 + me.c + step, 2 * RING)
        greet(me.at(z=other // 2, c=lax.rem(other, 2)))
    greet(me.at(xh=1 - me.xh))
    greet(me.at(xl=1 - me.xl))
    greet(me.at(xh=1 - me.xh, xl=1 - me.xl))
    greet(me.at(y=up))
    greet(me.at(y=down))
    greet(me.at(xh=1 - me.xh, z=RING - 1 - me.z, c=1 - me.c))

    def remote(src, dst, send, recv, device):
        return pltpu.make_async_remote_copy(
            src_ref=src, dst_ref=dst, send_sem=send, recv_sem=recv,
            device_id=device, device_id_type=MESH,
        )

    fill_taps(taps_ref)
    for load in loads:
        load.wait()
    length = records.shape[2]
    stations = records.shape[1]
    for side in range(2):
        tail_own[side * stations : (side + 1) * stations, :] = records[
            blocks[side], :, length - LANE :
        ]
    pl.semaphore_wait(barrier, 2 * RING - 1 + 6)

    tm = lax.axis_index("tm")
    after = lax.rem(tm + 1, 4 * RING)
    tail_copy = remote(
        tail_own, tail_in, tail_sem.at[0], tail_sem.at[1],
        {"pair": lax.axis_index("pair"), "tm": after},
    )
    pl.when(tm < 4 * RING - 1)(tail_copy.start)
    fill_transform(fwd_high, fwd_low)
    count = live[tm]
    lane = lax.broadcasted_iota(jnp.int32, (1, LANE), 1)
    record = jnp.concatenate([records[blocks[0]], records[blocks[1]]], axis=0)
    span = DECIM * LANE
    pieces = []
    for b in range(SEG // LANE):
        both = dot(record[:, b * span : (b + 1) * span], taps_ref[LANE:, :])
        if b > 0:
            both = both + dot(record[:, b * span - LANE : b * span], taps_ref[:LANE, :])
        pieces.append(both)

    @pl.when(tm == 0)
    def _():
        tail_in[...] = jnp.zeros_like(tail_in)

    pl.when(tm > 0)(tail_copy.wait_recv)
    pieces[0] = pieces[0] + dot(tail_in[...], taps_ref[:LANE, :])
    filtered = jnp.concatenate(
        [
            jnp.where(lane + b * LANE < count, both[:, :LANE] + both[:, LANE:], 0.0)
            for b, both in enumerate(pieces)
        ],
        axis=1,
    )
    real, imag = whiten(filtered, fwd_high, fwd_low, padded)
    pack_columns(real, imag, col_ref)

    pending = []

    def start(copy, when=None):
        if when is None:
            copy.start()
        else:
            pl.when(when)(copy.start)
        pending.append((copy, when))

    for j in range(4):
        root_z, root_c = root_pair * 2 + j // 2, j % 2
        mine = (me.z == root_z) & (me.c == root_c)
        index = me.c * RING + me.z
        copy = remote(
            col_ref.at[j], stage.at[index], stage_send.at[j], stage_recv.at[index],
            me.at(z=root_z, c=root_c),
        )
        start(copy, jnp.logical_not(mine))

        @pl.when(mine)
        def _():
            pltpu.make_async_copy(col_ref.at[j], stage.at[index], stage_recv.at[index]).start()

    pack_rows(real, imag, row_ref)
    own = slot_of(me.xh, me.c, me.z)

    def part(s):
        return pl.ds(s * size, size)

    def spread(source, slot, h, d, sign, s):
        lower = s < PARTS // 2
        for way, target in ((1, right), (-1, left)):
            if sign not in (0, way) or d > 3 or (d == 3 and lower != (way == 1)):
                continue
            start(
                remote(
                    source.at[part(s)], row_all.at[slot, part(s)],
                    row_send.at[h, (0 if way == 1 else 4) + d, s], row_recv.at[slot, s],
                    me.at(z=target),
                )
            )
        number = d + 3 if sign == -1 and d < 4 else (7 if d == 4 else d)
        start(
            remote(
                source.at[part(s)], row_all.at[slot, part(s)], near_send.at[h, number, s],
                near_recv.at[slot, s], me.at(c=1 - me.c),
            )
        )

    def got_row(slot, s, sems):
        ref = row_all.at[slot, part(s)]
        remote(ref, ref, row_send.at[0, 0, 0], sems.at[slot, s], me.at()).wait_recv()

    def widen_part(slot, s):
        each = QUARTERS // PARTS
        widen(row_all.at[slot], slot, range(s * each, (s + 1) * each), rows)

    def got_col(slot):
        ref = col_all.at[slot]
        remote(ref, ref, col_send.at[0, 0], col_recv.at[slot], me.at()).wait_recv()

    for s in range(PARTS):
        start(
            remote(
                row_ref.at[part(s)], row_all.at[own, part(s)], row_send.at[2, 0, s],
                row_recv.at[own, s], me.at(xh=1 - me.xh),
            )
        )
    for s in range(PARTS):
        spread(row_ref, own, 0, 0, 0, s)
    widen(row_ref, own, range(QUARTERS), rows)

    def zpiece(i):
        return lax.rem(me.z + OFFSETS[i] + RING, RING)

    def along(source, slot, c, when):
        start(
            remote(
                source, col_all.at[slot], col_send.at[slot, 1], col_recv.at[slot],
                me.at(y=up if c == 0 else down),
            ),
            when,
        )

    def sideways(source, slot, when, **there):
        start(
            remote(
                source, col_all.at[slot], col_send.at[slot, 0], col_recv.at[slot],
                me.at(xl=1 - me.xl, **there),
            ),
            when,
        )

    def hop(slot, c, when):
        pl.when(when)(lambda: got_col(slot))
        along(col_all.at[slot], slot, c, when)

    for kind, arg in schedule():
        if kind == "opposite":
            slot = slot_of(1 - me.xh, me.c, me.z)
            got_row(slot, arg, row_recv)
            spread(row_all.at[slot], slot, 1, 0, 0, arg)
            widen_part(slot, arg)
        elif kind == "row":
            h, d, s = arg
            xh = me.xh if h == 0 else 1 - me.xh
            signs = (1, -1) if d < 4 else ((1,) if s < PARTS // 2 else (-1,))
            for sign in signs:
                slot = slot_of(xh, me.c, lax.rem(me.z - sign * d + RING, RING))
                got_row(slot, s, row_recv)
                spread(row_all.at[slot], slot, h, d, sign, s)
                widen_part(slot, s)
        elif kind == "root":
            for c in range(2):
                index = c * RING + zpiece(arg)
                slot = slot_of(me.xh, c, zpiece(arg))

                @pl.when(is_root)
                def _():
                    pltpu.make_async_copy(
                        stage.at[index], stage.at[index], stage_recv.at[index]
                    ).wait()

                @pl.when(is_near)
                def _():
                    pltpu.make_async_copy(
                        stage.at[index], col_all.at[slot], local_sem.at[2 * arg + c]
                    ).start()

                sideways(stage.at[index], slot, is_near)
                sideways(stage.at[index], slot, is_far, xh=1 - me.xh)
                start(
                    remote(
                        stage.at[index], col_all.at[slot], col_send.at[slot, 2],
                        col_recv.at[slot], me.at(xh=1 - me.xh),
                    ),
                    is_far,
                )
                along(stage.at[index], slot, c, is_near)
        elif kind == "other":
            for c in range(2):
                hop(slot_of(1 - me.xh, c, zpiece(arg)), c, is_other)
            for c in range(2):
                hop(slot_of(me.xh, c, zpiece(arg)), c, is_other)
        elif kind == "near":
            for c in range(2):
                hop(slot_of(1 - me.xh, c, zpiece(arg)), c, is_near)
        elif kind == "hop1":
            for xh in (me.xh, 1 - me.xh):
                hop(slot_of(xh, 0, zpiece(arg)), 0, dy == 1)
                hop(slot_of(xh, 1, zpiece(arg)), 1, dy == 3)
        elif kind == "hop2":
            for xh in (me.xh, 1 - me.xh):
                for c in range(2):
                    hop(slot_of(xh, c, zpiece(arg)), c, dy == 2)
        elif kind == "last":
            for xh in (me.xh, 1 - me.xh):
                pl.when(dy == 3)(lambda xh=xh: got_col(slot_of(xh, 0, zpiece(arg))))
                pl.when(dy == 1)(lambda xh=xh: got_col(slot_of(xh, 1, zpiece(arg))))

    for h in range(2):
        for z in range(RING):
            for s in range(PARTS):
                slot = slot_of(h, 1 - me.c, z)
                got_row(slot, s, near_recv)
                widen_part(slot, s)
    for i in range(RING):
        for c in range(2):
            index = c * RING + zpiece(i)
            slot = slot_of(me.xh, c, zpiece(i))

            @pl.when(is_near)
            def _():
                pltpu.make_async_copy(
                    stage.at[index], col_all.at[slot], local_sem.at[2 * i + c]
                ).wait()

    for copy, when in pending:
        if when is None:
            copy.wait_send()
        else:
            pl.when(when)(copy.wait_send)
    pl.when(tm < 4 * RING - 1)(tail_copy.wait_send)

    def chunk_copies(chunk):
        return [
            pltpu.make_async_copy(
                stacked.at[:, pl.ds(pl.multiple_of(side * BINS + chunk * LANE, LANE), LANE)],
                stacked_out.at[:, pl.ds(pl.multiple_of(side * BINS + chunk * LANE, LANE), LANE)],
                out_sem.at[side, chunk],
            )
            for side in range(2)
        ]

    @pl.loop(0, CHUNKS)
    def _(chunk):
        cross_chunk(chunk, row_all, col_all, rows, cols, cross, stacked)
        for copy in chunk_copies(chunk):
            copy.start()

    @pl.loop(0, CHUNKS)
    def _(chunk):
        for copy in chunk_copies(chunk):
            copy.wait()


def widen(source, slot, quarters, rows):
    for chunk in range(CHUNKS):
        for quarter in quarters:
            at = (chunk * (4 * RING) + slot) * STRIDE_K + quarter * KCHUNK
            first = quarter * LANE + chunk * KCHUNK
            rows[pl.ds(pl.multiple_of(at, 8), KCHUNK), :] = source[
                first : first + KCHUNK, :
            ].astype(F32)


def cross_chunk(chunk, row_all, col_all, rows, cols, cross, stacked):
    segments = row_all.shape[0]
    half = LANE // 2
    group = 8
    count_k = QUARTERS * KCHUNK
    first = pl.multiple_of(chunk * KCHUNK, KCHUNK)
    for g in range(segments):
        cols[g * STRIDE_C : g * STRIDE_C + KCHUNK, :] = col_all[
            g, pl.ds(first, KCHUNK), :
        ].astype(F32)
    lane = lax.broadcasted_iota(jnp.int32, (32, group * segments), 1)
    sign = jnp.where(
        lax.broadcasted_iota(jnp.int32, (1, LANE), 1) < half, 1.0, -1.0
    ).astype(F32)
    for block in range(KCHUNK // group):
        gathered = jnp.concatenate(
            [cols[pl.ds(block * group + b, segments, stride=STRIDE_C), :] for b in range(group)],
            axis=0,
        )
        turned = gathered.T.astype(BF16)
        for quarter in range(QUARTERS):
            left = turned[quarter * 32 : quarter * 32 + 32, :]
            zero = jnp.zeros_like(left)
            wide = jnp.concatenate(
                [
                    jnp.where((lane >= b * segments) & (lane < (b + 1) * segments), left, zero)
                    for b in range(group)
                ],
                axis=0,
            )
            base = quarter * KCHUNK + block * group
            right = jnp.concatenate(
                [rows[pl.ds(chunk * (segments * STRIDE_K) + base + b, segments, stride=STRIDE_K), :] for b in range(group)],
                axis=0,
            ).astype(BF16)
            product = dot(wide, right)
            for b in range(group):
                top = product[b * 32 : b * 32 + 16, :]
                low = product[b * 32 + 16 : b * 32 + 32, :]
                cross[pl.ds(base + b, 16, stride=STRIDE_K), :] = top + sign * pltpu.roll(
                    low, half, 1
                )
    at = pl.multiple_of(chunk * count_k, LANE)
    for q in range(16):
        turned = cross[q * STRIDE_K : q * STRIDE_K + count_k, :].astype(BF16).T
        stacked[q * half : (q + 1) * half, pl.ds(at, count_k)] = turned[:half]
        stacked[q * half : (q + 1) * half, pl.ds(BINS + at, count_k)] = turned[half:]


def spectra(records, tile_blocks, live_len):
    dma = pltpu.SemaphoreType.DMA
    return pl.pallas_call(
        spectra_kernel,
        in_specs=[pl.BlockSpec(memory_space=pltpu.HBM)] * 3,
        out_specs=pl.BlockSpec(memory_space=pltpu.HBM),
        out_shape=jax.ShapeDtypeStruct((PAIRS, 2 * BINS), BF16),
        scratch_shapes=[
            pltpu.VMEM((PAIRS, 2 * BINS), BF16),
            pltpu.SMEM(tile_blocks.shape, jnp.int32),
            pltpu.SMEM(live_len.shape, jnp.int32),
            pltpu.VMEM(records.shape, BF16),
            pltpu.VMEM((LANE, LANE), BF16),
            pltpu.VMEM((LANE, LANE), BF16),
            pltpu.VMEM((5 * LANE, 2 * LANE), BF16),
            pltpu.VMEM((2 * BINS, SEG), BF16),
            pltpu.VMEM((2 * BINS, SEG), BF16),
            pltpu.VMEM((BINS + 16, LANE), F32),
            pltpu.VMEM((BINS, LANE), BF16),
            pltpu.VMEM((4, LANE, LANE), BF16),
            pltpu.VMEM((4 * RING, BINS, LANE), BF16),
            pltpu.VMEM((4 * RING, LANE, LANE), BF16),
            pltpu.VMEM((2 * RING, LANE, LANE), BF16),
            pltpu.VMEM((CHUNKS * 4 * RING * STRIDE_K, LANE), F32),
            pltpu.VMEM((4 * RING * STRIDE_C, LANE), F32),
            pltpu.VMEM((16 * STRIDE_K, LANE), F32),
            dma((2, CHUNKS)), dma((3,)), dma((2,)),
            dma((3, 8, PARTS)), dma((32, PARTS)), dma((2, 8, PARTS)), dma((32, PARTS)),
            dma((4,)), dma((2 * RING,)), dma((32, 3)), dma((32,)), dma((2 * RING + 1,)),
        ],
        compiler_params=pltpu.CompilerParams(
            collective_id=0, has_side_effects=True, vmem_limit_bytes=60 << 20
        ),
        name="spectra",
    )(tile_blocks, live_len, records)


def lags_kernel(stacked, lag_ref, out_ref, spare):
    half = LANE // 2
    value = dot(stacked[...], lag_ref[...])
    for q in range(16):
        for side in range(2):
            spare[side, q * STRIDE_P : q * STRIDE_P + half, :] = value[
                q * half : (q + 1) * half, side * LANE : (side + 1) * LANE
            ]
    for p in range(half):
        for side in range(2):
            out_ref[p * 16 : p * 16 + 16, side * LANE : (side + 1) * LANE] = spare[
                side, pl.ds(p, 16, stride=STRIDE_P), :
            ]


def lags(stacked):
    width = 2 * LANE
    tiles = -(-LAGS // width)
    table = jnp.asarray(np.pad(lag_table(), ((0, 0), (0, tiles * width - LAGS))))
    return pl.pallas_call(
        lags_kernel,
        grid=(tiles,),
        in_specs=[
            pl.BlockSpec((PAIRS, 2 * BINS), lambda i: (0, 0)),
            pl.BlockSpec((2 * BINS, width), lambda i: (0, i)),
        ],
        out_specs=pl.BlockSpec((PAIRS, width), lambda i: (0, i)),
        out_shape=jax.ShapeDtypeStruct((PAIRS, LAGS), F32),
        scratch_shapes=[pltpu.VMEM((2, 16 * STRIDE_P, LANE), F32)],
        compiler_params=pltpu.CompilerParams(vmem_limit_bytes=32 << 20),
        name="lags",
    )(stacked, table)


def shards(records, tile_blocks, live_len):
    result = lags(spectra(records, tile_blocks, live_len))
    return result.reshape(LANE // 2, 16, LAGS)


def solution(mesh):
    placed = (P(None, "pair", "tm"), P(), P())
    return jax.shard_map(
        shards, mesh=mesh, in_specs=placed, out_specs=P("pair", "tm", None), check_vma=False
    )
```

```python
import math

import jax
import jax.numpy as jnp
import ml_dtypes
import numpy as np
from jax import lax
from jax.experimental import pallas as pl
from jax.experimental.pallas import tpu as pltpu
from jax.sharding import PartitionSpec as P

DECIM = 4
TAPS = 64
SEG = 512
NFT = 1024
MAXLAG = 400
SMOOTH = 4
BINS = 512
LAGS = 801
LANE = 128
QUARTERS = 4
CHUNKS = 4
KCHUNK = LANE // CHUNKS
PAIRS = 1024
STRIDE_K = QUARTERS * KCHUNK + 8
STRIDE_C = KCHUNK + 8
STRIDE_P = LANE // 2 + 8
TWO_PI = 2.0 * math.pi / NFT
F32 = jnp.float32
BF16 = jnp.bfloat16
MESH = pl.DeviceIdType.MESH
RING = 8
YRING = 4
OFFSETS = (0, 1, -1, 2, -2, 3, -3, 4)
PARTS = 1
OPP_TIME = 3.0
ROW_START, ROW_STEP = 6.5, 6.5
COL_STEP = 1.5
COL_TIMES = (
    ("root", 1.5),
    ("other", 8.0),
    ("near", 8.1),
    ("hop1", 11.0),
    ("hop2", 14.0),
    ("last", 40.0),
)


def turns(rows, step, columns):
    row = lax.broadcasted_iota(jnp.int32, (rows, columns), 0) * step
    index = (row * lax.broadcasted_iota(jnp.int32, (rows, columns), 1)) & (NFT - 1)
    index = jnp.where(index >= NFT // 2, index - NFT, index)
    phase = index.astype(F32) * TWO_PI
    return jnp.cos(phase), jnp.sin(phase)


def fill_taps(taps_ref):
    row = lax.broadcasted_iota(jnp.int32, (8, LANE), 0)
    lane = lax.broadcasted_iota(jnp.int32, (8, LANE), 1)
    index = row - TAPS - DECIM * (lane - LANE)
    inside = (index >= 0) & (index < TAPS)
    position = jnp.where(inside, index, 0).astype(F32)
    centred = (position - (TAPS - 1) / 2.0) * (1.0 / DECIM)
    window = 0.5 * (1.0 - jnp.cos((2.0 * math.pi / TAPS) * (position + 0.5)))
    turn = math.pi * centred
    value = jnp.where(inside, window * jnp.sin(turn) / turn * (1.0 / DECIM), 0.0)
    shift = 8 // DECIM
    for r in range(0, 5 * LANE // 8, 2):
        pair = []
        for one in (r, r + 1):
            moved = value
            if one * shift % LANE:
                moved = pltpu.roll(value, one * shift % LANE, 1)
            offset = row - TAPS - DECIM * (lane - one * shift)
            pair.append(jnp.where((offset >= 0) & (offset < TAPS), moved, 0.0))
        high, low = split(jnp.concatenate(pair, axis=0))
        taps_ref[8 * r : 8 * r + 16, :LANE] = high
        taps_ref[8 * r : 8 * r + 16, LANE:] = low


def bin_order():
    chunk = np.arange(CHUNKS)[:, None, None]
    quarter = np.arange(QUARTERS)[None, :, None]
    inner = np.arange(KCHUNK)[None, None, :]
    return (quarter * LANE + chunk * KCHUNK + inner).reshape(-1)


def lag_table():
    bins = bin_order()
    shifts = np.arange(LAGS) - MAXLAG
    phase = (bins[:, None] * shifts[None, :] % NFT) * TWO_PI
    weights = np.where(bins == 0, 1.0, 2.0)[:, None] / math.sqrt(NFT)
    table = np.concatenate([weights * np.cos(phase), -weights * np.sin(phase)], axis=0)
    return table.astype(ml_dtypes.bfloat16)


def split(value):
    high = value.astype(BF16)
    return high, (value - high.astype(F32)).astype(BF16)


def dot(a, b, dims=((1,), (0,))):
    return lax.dot_general(a, b, (dims, ((), ())), preferred_element_type=F32)


def fill_transform(fwd_high, fwd_low):
    coarse_cos, coarse_sin = turns(BINS // 8, 8, SEG)
    fine_cos, fine_sin = turns(8, 1, SEG)
    for a in range(0, BINS // 8, 2):
        reals, imags = [], []
        for one in (a, a + 1):
            cc, cs = coarse_cos[one : one + 1, :], coarse_sin[one : one + 1, :]
            reals.append(cc * fine_cos - cs * fine_sin)
            imags.append(-(cs * fine_cos + cc * fine_sin))
        for value, base in ((reals, 8 * a), (imags, BINS + 8 * a)):
            high, low = split(jnp.concatenate(value, axis=0))
            fwd_high[base : base + 16, :] = high
            fwd_low[base : base + 16, :] = low


def whiten(filtered, fwd_high, fwd_low, padded):
    high, low = split(filtered)
    last = ((1,), (1,))
    spectra = (
        dot(fwd_high[...], low, last)
        + dot(fwd_low[...], high, last)
        + dot(fwd_high[...], high, last)
    )
    real, imag = spectra[:BINS], spectra[BINS:]
    amplitude = jnp.sqrt(real * real + imag * imag)
    padded[0:8, :] = jnp.zeros((8, LANE), F32)
    padded[8 + BINS : 16 + BINS, :] = jnp.zeros((8, LANE), F32)
    padded[8 : 8 + BINS, :] = amplitude
    smooth = padded[8 - SMOOTH : 8 - SMOOTH + BINS, :]
    for offset in range(1, 2 * SMOOTH + 1):
        start = 8 - SMOOTH + offset
        smooth = smooth + padded[start : start + BINS, :]
    mean = jnp.sum(amplitude, axis=0, keepdims=True) * (1.0 / BINS)
    level = smooth * (1.0 / (2 * SMOOTH + 1)) + 0.05 * mean + 1e-06
    inverse = 1.0 / level
    return real * inverse, imag * inverse


def pack_rows(real, imag, row_own):
    half = LANE // 2
    lower = lax.broadcasted_iota(jnp.int32, (BINS, LANE), 1) < half
    row_own[...] = jnp.where(lower, real, pltpu.roll(imag, half, 1)).astype(BF16)


def pack_columns(real, imag, col_own):
    half = LANE // 2
    lower = lax.broadcasted_iota(jnp.int32, (BINS, LANE), 1) < half
    cols = jnp.where(lower, pltpu.roll(real, half, 1), imag)
    lanes = lax.broadcasted_iota(jnp.int32, (LANE, LANE), 1)
    for j in range(4):
        total = jnp.zeros((LANE, LANE), F32)
        for quarter in range(QUARTERS):
            part = cols[quarter * LANE : (quarter + 1) * LANE, :]
            for c in range(2):
                source = c * half + 16 * j
                target = quarter * 32 + 16 * c
                moved = part
                if (target - source) % LANE:
                    moved = pltpu.roll(part, (target - source) % LANE, 1)
                keep = (lanes >= target) & (lanes < target + 16)
                total = jnp.where(keep, moved, total)
        col_own[j] = total.astype(BF16)


class Place:
    def __init__(self):
        pair, tm = lax.axis_index("pair"), lax.axis_index("tm")
        self.y, self.xl = pair // 2, lax.rem(pair, 2)
        self.xh, self.z, self.c = tm // 16, lax.rem(tm // 2, RING), lax.rem(tm, 2)

    def at(self, y=None, xl=None, xh=None, z=None, c=None):
        pick = lambda new, old: old if new is None else new
        y, xl, xh = pick(y, self.y), pick(xl, self.xl), pick(xh, self.xh)
        z, c = pick(z, self.z), pick(c, self.c)
        return {"pair": y * 2 + xl, "tm": xh * 16 + z * 2 + c}


def slot_of(xh, c, z):
    return xh * 16 + c * RING + z


def schedule():
    events = []
    for i in range(RING):
        for kind, late in COL_TIMES:
            events.append((late + COL_STEP * i, kind, i))
    for s in range(PARTS):
        events.append((OPP_TIME + 0.1 * s, "opposite", s))
        for d in range(1, 5):
            for h in range(2):
                at = ROW_START + ROW_STEP * (d - 1) + (0.5 * ROW_STEP * h + 0.45 * ROW_STEP * s / PARTS)
                events.append((at, "row", (h, d, s)))
    events.sort(key=lambda e: e[0])
    return [(kind, arg) for _, kind, arg in events]


def spectra_kernel(
    blocks_in, live_in, records_in, stacked_out,
    stacked, blocks, live, records, tail_own, tail_in, taps_ref, fwd_high, fwd_low, padded, row_ref, col_ref,
    row_all, col_all, stage, rows, cols, cross,
    out_sem, load_sem, tail_sem, row_send, row_recv, near_send, near_recv, stage_send, stage_recv,
    col_send, col_recv, local_sem,
):
    me = Place()
    size = BINS // PARTS
    group_xh = me.y // 2
    home_y = me.xh * 2 + me.z // 4
    home_xl = lax.rem(me.z // 2, 2)
    dy = lax.rem(me.y - home_y + YRING, YRING)
    root_pair = lax.rem(me.y, 2) * 2 + me.xl
    is_root = (me.z // 2) == root_pair
    is_near = is_root & (me.xh == group_xh)
    is_far = is_root & (me.xh != group_xh)
    is_other = (dy == 0) & (me.xl != home_xl)
    up, down = lax.rem(me.y + 1, YRING), lax.rem(me.y + YRING - 1, YRING)
    right, left = lax.rem(me.z + 1, RING), lax.rem(me.z + RING - 1, RING)

    loads = [
        pltpu.make_async_copy(source, target, load_sem.at[i])
        for i, (source, target) in enumerate(
            ((records_in, records), (blocks_in, blocks), (live_in, live))
        )
    ]
    for load in loads:
        load.start()
    barrier = pltpu.get_barrier_semaphore()

    def greet(device):
        pl.semaphore_signal(barrier, inc=1, device_id=device, device_id_type=MESH)

    for step in range(1, 2 * RING):
        other = lax.rem(me.z * 2 + me.c + step, 2 * RING)
        greet(me.at(z=other // 2, c=lax.rem(other, 2)))
    greet(me.at(xh=1 - me.xh))
    greet(me.at(xl=1 - me.xl))
    greet(me.at(xh=1 - me.xh, xl=1 - me.xl))
    greet(me.at(y=up))
    greet(me.at(y=down))
    greet(me.at(xh=1 - me.xh, z=RING - 1 - me.z, c=1 - me.c))

    def remote(src, dst, send, recv, device):
        return pltpu.make_async_remote_copy(
            src_ref=src, dst_ref=dst, send_sem=send, recv_sem=recv,
            device_id=device, device_id_type=MESH,
        )

    fill_taps(taps_ref)
    for load in loads:
        load.wait()
    length = records.shape[2]
    stations = records.shape[1]
    for side in range(2):
        tail_own[side * stations : (side + 1) * stations, :] = records[
            blocks[side], :, length - LANE :
        ]
    pl.semaphore_wait(barrier, 2 * RING - 1 + 6)

    tm = lax.axis_index("tm")
    after = lax.rem(tm + 1, 4 * RING)
    tail_copy = remote(
        tail_own, tail_in, tail_sem.at[0], tail_sem.at[1],
        {"pair": lax.axis_index("pair"), "tm": after},
    )
    pl.when(tm < 4 * RING - 1)(tail_copy.start)
    fill_transform(fwd_high, fwd_low)
    count = live[tm]
    lane = lax.broadcasted_iota(jnp.int32, (1, LANE), 1)
    record = jnp.concatenate([records[blocks[0]], records[blocks[1]]], axis=0)
    span = DECIM * LANE
    pieces = []
    for b in range(SEG // LANE):
        both = dot(record[:, b * span : (b + 1) * span], taps_ref[LANE:, :])
        if b > 0:
            both = both + dot(record[:, b * span - LANE : b * span], taps_ref[:LANE, :])
        pieces.append(both)

    @pl.when(tm == 0)
    def _():
        tail_in[...] = jnp.zeros_like(tail_in)

    pl.when(tm > 0)(tail_copy.wait_recv)
    pieces[0] = pieces[0] + dot(tail_in[...], taps_ref[:LANE, :])
    filtered = jnp.concatenate(
        [
            jnp.where(lane + b * LANE < count, both[:, :LANE] + both[:, LANE:], 0.0)
            for b, both in enumerate(pieces)
        ],
        axis=1,
    )
    real, imag = whiten(filtered, fwd_high, fwd_low, padded)
    pack_columns(real, imag, col_ref)

    pending = []

    def start(copy, when=None):
        if when is None:
            copy.start()
        else:
            pl.when(when)(copy.start)
        pending.append((copy, when))

    for j in range(4):
        root_z, root_c = root_pair * 2 + j // 2, j % 2
        mine = (me.z == root_z) & (me.c == root_c)
        index = me.c * RING + me.z
        copy = remote(
            col_ref.at[j], stage.at[index], stage_send.at[j], stage_recv.at[index],
            me.at(z=root_z, c=root_c),
        )
        start(copy, jnp.logical_not(mine))

        @pl.when(mine)
        def _():
            pltpu.make_async_copy(col_ref.at[j], stage.at[index], stage_recv.at[index]).start()

    pack_rows(real, imag, row_ref)
    own = slot_of(me.xh, me.c, me.z)

    def part(s):
        return pl.ds(s * size, size)

    def spread(source, slot, h, d, sign, s):
        lower = h == 0
        for way, target in ((1, right), (-1, left)):
            if sign not in (0, way) or d > 3 or (d == 3 and lower != (way == 1)):
                continue
            start(
                remote(
                    source.at[part(s)], row_all.at[slot, part(s)],
                    row_send.at[h, (0 if way == 1 else 4) + d, s], row_recv.at[slot, s],
                    me.at(z=target),
                )
            )
        number = d + 3 if sign == -1 and d < 4 else (7 if d == 4 else d)
        start(
            remote(
                source.at[part(s)], row_all.at[slot, part(s)], near_send.at[h, number, s],
                near_recv.at[slot, s], me.at(c=1 - me.c),
            )
        )

    def got_row(slot, s, sems):
        ref = row_all.at[slot, part(s)]
        remote(ref, ref, row_send.at[0, 0, 0], sems.at[slot, s], me.at()).wait_recv()

    def widen_part(slot, s):
        each = QUARTERS // PARTS
        widen(row_all.at[slot], slot, range(s * each, (s + 1) * each), rows)

    def got_col(slot):
        ref = col_all.at[slot]
        remote(ref, ref, col_send.at[0, 0], col_recv.at[slot], me.at()).wait_recv()

    for s in range(PARTS):
        start(
            remote(
                row_ref.at[part(s)], row_all.at[own, part(s)], row_send.at[2, 0, s],
                row_recv.at[own, s], me.at(xh=1 - me.xh),
            )
        )
    for s in range(PARTS):
        spread(row_ref, own, 0, 0, 0, s)
    widen(row_ref, own, range(QUARTERS), rows)

    def zpiece(i):
        return lax.rem(me.z + OFFSETS[i] + RING, RING)

    def along(source, slot, c, when):
        start(
            remote(
                source, col_all.at[slot], col_send.at[slot, 1], col_recv.at[slot],
                me.at(y=up if c == 0 else down),
            ),
            when,
        )

    def sideways(source, slot, when, **there):
        start(
            remote(
                source, col_all.at[slot], col_send.at[slot, 0], col_recv.at[slot],
                me.at(xl=1 - me.xl, **there),
            ),
            when,
        )

    def hop(slot, c, when):
        pl.when(when)(lambda: got_col(slot))
        along(col_all.at[slot], slot, c, when)

    for kind, arg in schedule():
        if kind == "opposite":
            slot = slot_of(1 - me.xh, me.c, me.z)
            got_row(slot, arg, row_recv)
            spread(row_all.at[slot], slot, 1, 0, 0, arg)
            widen_part(slot, arg)
        elif kind == "row":
            h, d, s = arg
            xh = me.xh if h == 0 else 1 - me.xh
            signs = (1, -1) if d < 4 else ((1,) if h == 0 else (-1,))
            for sign in signs:
                slot = slot_of(xh, me.c, lax.rem(me.z - sign * d + RING, RING))
                got_row(slot, s, row_recv)
                spread(row_all.at[slot], slot, h, d, sign, s)
                widen_part(slot, s)
        elif kind == "root":
            for c in range(2):
                index = c * RING + zpiece(arg)
                slot = slot_of(me.xh, c, zpiece(arg))

                @pl.when(is_root)
                def _():
                    pltpu.make_async_copy(
                        stage.at[index], stage.at[index], stage_recv.at[index]
                    ).wait()

                @pl.when(is_near)
                def _():
                    pltpu.make_async_copy(
                        stage.at[index], col_all.at[slot], local_sem.at[2 * arg + c]
                    ).start()

                sideways(stage.at[index], slot, is_near)
                sideways(stage.at[index], slot, is_far, xh=1 - me.xh)
                start(
                    remote(
                        stage.at[index], col_all.at[slot], col_send.at[slot, 2],
                        col_recv.at[slot], me.at(xh=1 - me.xh),
                    ),
                    is_far,
                )
                along(stage.at[index], slot, c, is_near)
        elif kind == "other":
            for c in range(2):
                hop(slot_of(1 - me.xh, c, zpiece(arg)), c, is_other)
            for c in range(2):
                hop(slot_of(me.xh, c, zpiece(arg)), c, is_other)
        elif kind == "near":
            for c in range(2):
                hop(slot_of(1 - me.xh, c, zpiece(arg)), c, is_near)
        elif kind == "hop1":
            for xh in (me.xh, 1 - me.xh):
                hop(slot_of(xh, 0, zpiece(arg)), 0, dy == 1)
                hop(slot_of(xh, 1, zpiece(arg)), 1, dy == 3)
        elif kind == "hop2":
            for xh in (me.xh, 1 - me.xh):
                for c in range(2):
                    hop(slot_of(xh, c, zpiece(arg)), c, dy == 2)
        elif kind == "last":
            for xh in (me.xh, 1 - me.xh):
                pl.when(dy == 3)(lambda xh=xh: got_col(slot_of(xh, 0, zpiece(arg))))
                pl.when(dy == 1)(lambda xh=xh: got_col(slot_of(xh, 1, zpiece(arg))))

    for h in range(2):
        for z in range(RING):
            for s in range(PARTS):
                slot = slot_of(h, 1 - me.c, z)
                got_row(slot, s, near_recv)
                widen_part(slot, s)
    for i in range(RING):
        for c in range(2):
            index = c * RING + zpiece(i)
            slot = slot_of(me.xh, c, zpiece(i))

            @pl.when(is_near)
            def _():
                pltpu.make_async_copy(
                    stage.at[index], col_all.at[slot], local_sem.at[2 * i + c]
                ).wait()

    for copy, when in pending:
        if when is None:
            copy.wait_send()
        else:
            pl.when(when)(copy.wait_send)
    pl.when(tm < 4 * RING - 1)(tail_copy.wait_send)

    def chunk_copies(chunk):
        return [
            pltpu.make_async_copy(
                stacked.at[:, pl.ds(pl.multiple_of(side * BINS + chunk * LANE, LANE), LANE)],
                stacked_out.at[:, pl.ds(pl.multiple_of(side * BINS + chunk * LANE, LANE), LANE)],
                out_sem.at[side, chunk],
            )
            for side in range(2)
        ]

    @pl.loop(0, CHUNKS)
    def _(chunk):
        cross_chunk(chunk, row_all, col_all, rows, cols, cross, stacked)
        for copy in chunk_copies(chunk):
            copy.start()

    @pl.loop(0, CHUNKS)
    def _(chunk):
        for copy in chunk_copies(chunk):
            copy.wait()


def widen(source, slot, quarters, rows):
    for chunk in range(CHUNKS):
        for quarter in quarters:
            at = (chunk * (4 * RING) + slot) * STRIDE_K + quarter * KCHUNK
            first = quarter * LANE + chunk * KCHUNK
            rows[pl.ds(pl.multiple_of(at, 8), KCHUNK), :] = source[
                first : first + KCHUNK, :
            ].astype(F32)


def cross_chunk(chunk, row_all, col_all, rows, cols, cross, stacked):
    segments = row_all.shape[0]
    half = LANE // 2
    group = 8
    count_k = QUARTERS * KCHUNK
    first = pl.multiple_of(chunk * KCHUNK, KCHUNK)
    for g in range(segments):
        cols[g * STRIDE_C : g * STRIDE_C + KCHUNK, :] = col_all[
            g, pl.ds(first, KCHUNK), :
        ].astype(F32)
    lane = lax.broadcasted_iota(jnp.int32, (32, group * segments), 1)
    sign = jnp.where(
        lax.broadcasted_iota(jnp.int32, (1, LANE), 1) < half, 1.0, -1.0
    ).astype(F32)
    for block in range(KCHUNK // group):
        gathered = jnp.concatenate(
            [cols[pl.ds(block * group + b, segments, stride=STRIDE_C), :] for b in range(group)],
            axis=0,
        )
        turned = gathered.T.astype(BF16)
        for quarter in range(QUARTERS):
            left = turned[quarter * 32 : quarter * 32 + 32, :]
            zero = jnp.zeros_like(left)
            wide = jnp.concatenate(
                [
                    jnp.where((lane >= b * segments) & (lane < (b + 1) * segments), left, zero)
                    for b in range(group)
                ],
                axis=0,
            )
            base = quarter * KCHUNK + block * group
            right = jnp.concatenate(
                [rows[pl.ds(chunk * (segments * STRIDE_K) + base + b, segments, stride=STRIDE_K), :] for b in range(group)],
                axis=0,
            ).astype(BF16)
            product = dot(wide, right)
            for b in range(group):
                top = product[b * 32 : b * 32 + 16, :]
                low = product[b * 32 + 16 : b * 32 + 32, :]
                cross[pl.ds(base + b, 16, stride=STRIDE_K), :] = top + sign * pltpu.roll(
                    low, half, 1
                )
    at = pl.multiple_of(chunk * count_k, LANE)
    for q in range(16):
        turned = cross[q * STRIDE_K : q * STRIDE_K + count_k, :].astype(BF16).T
        stacked[q * half : (q + 1) * half, pl.ds(at, count_k)] = turned[:half]
        stacked[q * half : (q + 1) * half, pl.ds(BINS + at, count_k)] = turned[half:]


def spectra(records, tile_blocks, live_len):
    dma = pltpu.SemaphoreType.DMA
    return pl.pallas_call(
        spectra_kernel,
        in_specs=[pl.BlockSpec(memory_space=pltpu.HBM)] * 3,
        out_specs=pl.BlockSpec(memory_space=pltpu.HBM),
        out_shape=jax.ShapeDtypeStruct((PAIRS, 2 * BINS), BF16),
        scratch_shapes=[
            pltpu.VMEM((PAIRS, 2 * BINS), BF16),
            pltpu.SMEM(tile_blocks.shape, jnp.int32),
            pltpu.SMEM(live_len.shape, jnp.int32),
            pltpu.VMEM(records.shape, BF16),
            pltpu.VMEM((LANE, LANE), BF16),
            pltpu.VMEM((LANE, LANE), BF16),
            pltpu.VMEM((5 * LANE, 2 * LANE), BF16),
            pltpu.VMEM((2 * BINS, SEG), BF16),
            pltpu.VMEM((2 * BINS, SEG), BF16),
            pltpu.VMEM((BINS + 16, LANE), F32),
            pltpu.VMEM((BINS, LANE), BF16),
            pltpu.VMEM((4, LANE, LANE), BF16),
            pltpu.VMEM((4 * RING, BINS, LANE), BF16),
            pltpu.VMEM((4 * RING, LANE, LANE), BF16),
            pltpu.VMEM((2 * RING, LANE, LANE), BF16),
            pltpu.VMEM((CHUNKS * 4 * RING * STRIDE_K, LANE), F32),
            pltpu.VMEM((4 * RING * STRIDE_C, LANE), F32),
            pltpu.VMEM((16 * STRIDE_K, LANE), F32),
            dma((2, CHUNKS)), dma((3,)), dma((2,)),
            dma((3, 8, PARTS)), dma((32, PARTS)), dma((2, 8, PARTS)), dma((32, PARTS)),
            dma((4,)), dma((2 * RING,)), dma((32, 3)), dma((32,)), dma((2 * RING + 1,)),
        ],
        compiler_params=pltpu.CompilerParams(
            collective_id=0, has_side_effects=True, vmem_limit_bytes=60 << 20
        ),
        name="spectra",
    )(tile_blocks, live_len, records)


def lags_kernel(stacked, lag_ref, out_ref, spare):
    half = LANE // 2
    value = dot(stacked[...], lag_ref[...])
    for q in range(16):
        for side in range(2):
            spare[side, q * STRIDE_P : q * STRIDE_P + half, :] = value[
                q * half : (q + 1) * half, side * LANE : (side + 1) * LANE
            ]
    for p in range(half):
        for side in range(2):
            out_ref[p * 16 : p * 16 + 16, side * LANE : (side + 1) * LANE] = spare[
                side, pl.ds(p, 16, stride=STRIDE_P), :
            ]


def lags(stacked):
    width = 2 * LANE
    tiles = -(-LAGS // width)
    table = jnp.asarray(np.pad(lag_table(), ((0, 0), (0, tiles * width - LAGS))))
    return pl.pallas_call(
        lags_kernel,
        grid=(tiles,),
        in_specs=[
            pl.BlockSpec((PAIRS, 2 * BINS), lambda i: (0, 0)),
            pl.BlockSpec((2 * BINS, width), lambda i: (0, i)),
        ],
        out_specs=pl.BlockSpec((PAIRS, width), lambda i: (0, i)),
        out_shape=jax.ShapeDtypeStruct((PAIRS, LAGS), F32),
        scratch_shapes=[pltpu.VMEM((2, 16 * STRIDE_P, LANE), F32)],
        compiler_params=pltpu.CompilerParams(vmem_limit_bytes=32 << 20),
        name="lags",
    )(stacked, table)


def shards(records, tile_blocks, live_len):
    result = lags(spectra(records, tile_blocks, live_len))
    return result.reshape(LANE // 2, 16, LAGS)


def solution(mesh):
    placed = (P(None, "pair", "tm"), P(), P())
    return jax.shard_map(
        shards, mesh=mesh, in_specs=placed, out_specs=P("pair", "tm", None), check_vma=False
    )
```

```python
import math

import jax
import jax.numpy as jnp
import ml_dtypes
import numpy as np
from jax import lax
from jax.experimental import pallas as pl
from jax.experimental.pallas import tpu as pltpu
from jax.sharding import PartitionSpec as P

DECIM = 4
TAPS = 64
SEG = 512
NFT = 1024
MAXLAG = 400
SMOOTH = 4
BINS = 512
LAGS = 801
LANE = 128
QUARTERS = 4
CHUNKS = 4
KCHUNK = LANE // CHUNKS
PAIRS = 1024
STRIDE_K = QUARTERS * KCHUNK + 8
STRIDE_C = KCHUNK + 8
STRIDE_P = LANE // 2 + 8
TWO_PI = 2.0 * math.pi / NFT
F32 = jnp.float32
BF16 = jnp.bfloat16
MESH = pl.DeviceIdType.MESH
RING = 8
YRING = 4
OFFSETS = (0, 1, -1, 2, -2, 3, -3, 4)
PARTS = 1
OPP_TIME = 3.0
ROW_START, ROW_STEP = 6.5, 6.5
COL_STEP = 1.5
COL_TIMES = (
    ("root", 1.5),
    ("other", 8.0),
    ("near", 8.1),
    ("hop1", 11.0),
    ("hop2", 14.0),
    ("last", 40.0),
)


def turns(rows, step, columns):
    row = lax.broadcasted_iota(jnp.int32, (rows, columns), 0) * step
    index = (row * lax.broadcasted_iota(jnp.int32, (rows, columns), 1)) & (NFT - 1)
    index = jnp.where(index >= NFT // 2, index - NFT, index)
    phase = index.astype(F32) * TWO_PI
    return jnp.cos(phase), jnp.sin(phase)


def fill_taps(taps_ref):
    row = lax.broadcasted_iota(jnp.int32, (8, LANE), 0)
    lane = lax.broadcasted_iota(jnp.int32, (8, LANE), 1)
    index = row - TAPS - DECIM * (lane - LANE)
    inside = (index >= 0) & (index < TAPS)
    position = jnp.where(inside, index, 0).astype(F32)
    centred = (position - (TAPS - 1) / 2.0) * (1.0 / DECIM)
    window = 0.5 * (1.0 - jnp.cos((2.0 * math.pi / TAPS) * (position + 0.5)))
    turn = math.pi * centred
    value = jnp.where(inside, window * jnp.sin(turn) / turn * (1.0 / DECIM), 0.0)
    shift = 8 // DECIM
    for r in range(0, 5 * LANE // 8, 2):
        pair = []
        for one in (r, r + 1):
            moved = value
            if one * shift % LANE:
                moved = pltpu.roll(value, one * shift % LANE, 1)
            offset = row - TAPS - DECIM * (lane - one * shift)
            pair.append(jnp.where((offset >= 0) & (offset < TAPS), moved, 0.0))
        high, low = split(jnp.concatenate(pair, axis=0))
        taps_ref[8 * r : 8 * r + 16, :LANE] = high
        taps_ref[8 * r : 8 * r + 16, LANE:] = low


def bin_order():
    chunk = np.arange(CHUNKS)[:, None, None]
    quarter = np.arange(QUARTERS)[None, :, None]
    inner = np.arange(KCHUNK)[None, None, :]
    return (quarter * LANE + chunk * KCHUNK + inner).reshape(-1)


def lag_table():
    bins = bin_order()
    shifts = np.arange(LAGS) - MAXLAG
    phase = (bins[:, None] * shifts[None, :] % NFT) * TWO_PI
    weights = np.where(bins == 0, 1.0, 2.0)[:, None] / math.sqrt(NFT)
    table = np.concatenate([weights * np.cos(phase), -weights * np.sin(phase)], axis=0)
    return table.astype(ml_dtypes.bfloat16)


def split(value):
    high = value.astype(BF16)
    return high, (value - high.astype(F32)).astype(BF16)


def dot(a, b, dims=((1,), (0,))):
    return lax.dot_general(a, b, (dims, ((), ())), preferred_element_type=F32)


def fill_transform(fwd_high, fwd_low):
    coarse_cos, coarse_sin = turns(BINS // 8, 8, SEG)
    fine_cos, fine_sin = turns(8, 1, SEG)
    for a in range(0, BINS // 8, 2):
        reals, imags = [], []
        for one in (a, a + 1):
            cc, cs = coarse_cos[one : one + 1, :], coarse_sin[one : one + 1, :]
            reals.append(cc * fine_cos - cs * fine_sin)
            imags.append(-(cs * fine_cos + cc * fine_sin))
        for value, base in ((reals, 8 * a), (imags, BINS + 8 * a)):
            high, low = split(jnp.concatenate(value, axis=0))
            fwd_high[base : base + 16, :] = high
            fwd_low[base : base + 16, :] = low


def whiten(filtered, fwd_high, fwd_low, padded):
    high, low = split(filtered)
    last = ((1,), (1,))
    spectra = (
        dot(fwd_high[...], low, last)
        + dot(fwd_low[...], high, last)
        + dot(fwd_high[...], high, last)
    )
    real, imag = spectra[:BINS], spectra[BINS:]
    amplitude = jnp.sqrt(real * real + imag * imag)
    padded[0:8, :] = jnp.zeros((8, LANE), F32)
    padded[8 + BINS : 16 + BINS, :] = jnp.zeros((8, LANE), F32)
    padded[8 : 8 + BINS, :] = amplitude
    smooth = padded[8 - SMOOTH : 8 - SMOOTH + BINS, :]
    for offset in range(1, 2 * SMOOTH + 1):
        start = 8 - SMOOTH + offset
        smooth = smooth + padded[start : start + BINS, :]
    mean = jnp.sum(amplitude, axis=0, keepdims=True) * (1.0 / BINS)
    level = smooth * (1.0 / (2 * SMOOTH + 1)) + 0.05 * mean + 1e-06
    inverse = 1.0 / level
    return real * inverse, imag * inverse


def pack_rows(real, imag, row_own):
    half = LANE // 2
    lower = lax.broadcasted_iota(jnp.int32, (BINS, LANE), 1) < half
    row_own[...] = jnp.where(lower, real, pltpu.roll(imag, half, 1)).astype(BF16)


def pack_columns(real, imag, col_own):
    half = LANE // 2
    lower = lax.broadcasted_iota(jnp.int32, (BINS, LANE), 1) < half
    cols = jnp.where(lower, pltpu.roll(real, half, 1), imag)
    lanes = lax.broadcasted_iota(jnp.int32, (LANE, LANE), 1)
    for j in range(4):
        total = jnp.zeros((LANE, LANE), F32)
        for quarter in range(QUARTERS):
            part = cols[quarter * LANE : (quarter + 1) * LANE, :]
            for c in range(2):
                source = c * half + 16 * j
                target = quarter * 32 + 16 * c
                moved = part
                if (target - source) % LANE:
                    moved = pltpu.roll(part, (target - source) % LANE, 1)
                keep = (lanes >= target) & (lanes < target + 16)
                total = jnp.where(keep, moved, total)
        col_own[j] = total.astype(BF16)


class Place:
    def __init__(self):
        pair, tm = lax.axis_index("pair"), lax.axis_index("tm")
        self.y, self.xl = pair // 2, lax.rem(pair, 2)
        self.xh, self.z, self.c = tm // 16, lax.rem(tm // 2, RING), lax.rem(tm, 2)

    def at(self, y=None, xl=None, xh=None, z=None, c=None):
        pick = lambda new, old: old if new is None else new
        y, xl, xh = pick(y, self.y), pick(xl, self.xl), pick(xh, self.xh)
        z, c = pick(z, self.z), pick(c, self.c)
        return {"pair": y * 2 + xl, "tm": xh * 16 + z * 2 + c}


def slot_of(xh, c, z):
    return xh * 16 + c * RING + z


def schedule():
    events = []
    for i in range(RING):
        for kind, late in COL_TIMES:
            events.append((late + COL_STEP * i, kind, i))
    for s in range(PARTS):
        events.append((OPP_TIME + 0.1 * s, "opposite", s))
        for d in range(1, 5):
            for h in range(2):
                at = ROW_START + ROW_STEP * (d - 1) + (0.5 * ROW_STEP * h + 0.45 * ROW_STEP * s / PARTS)
                events.append((at, "row", (h, d, s)))
    events.sort(key=lambda e: e[0])
    return [(kind, arg) for _, kind, arg in events]


def spectra_kernel(
    blocks_in, live_in, records_in, stacked_out,
    stacked, blocks, live, records, tail_own, tail_in, taps_ref, fwd_high, fwd_low, padded, row_ref, col_ref,
    row_all, col_all, stage, rows, cols, cross,
    out_sem, load_sem, tail_sem, row_send, row_recv, near_send, near_recv, stage_send, stage_recv,
    col_send, col_recv, local_sem,
):
    me = Place()
    size = BINS // PARTS
    group_xh = me.y // 2
    home_y = me.xh * 2 + me.z // 4
    home_xl = lax.rem(me.z // 2, 2)
    dy = lax.rem(me.y - home_y + YRING, YRING)
    root_pair = lax.rem(me.y, 2) * 2 + me.xl
    is_root = (me.z // 2) == root_pair
    is_near = is_root & (me.xh == group_xh)
    is_far = is_root & (me.xh != group_xh)
    is_other = (dy == 0) & (me.xl != home_xl)
    up, down = lax.rem(me.y + 1, YRING), lax.rem(me.y + YRING - 1, YRING)
    right, left = lax.rem(me.z + 1, RING), lax.rem(me.z + RING - 1, RING)

    loads = [
        pltpu.make_async_copy(source, target, load_sem.at[i])
        for i, (source, target) in enumerate(
            ((records_in, records), (blocks_in, blocks), (live_in, live))
        )
    ]
    for load in loads:
        load.start()
    barrier = pltpu.get_barrier_semaphore()

    def greet(device):
        pl.semaphore_signal(barrier, inc=1, device_id=device, device_id_type=MESH)

    for step in range(1, 2 * RING):
        other = lax.rem(me.z * 2 + me.c + step, 2 * RING)
        greet(me.at(z=other // 2, c=lax.rem(other, 2)))
    greet(me.at(xh=1 - me.xh))
    greet(me.at(xl=1 - me.xl))
    greet(me.at(xh=1 - me.xh, xl=1 - me.xl))
    greet(me.at(y=up))
    greet(me.at(y=down))
    greet(me.at(xh=1 - me.xh, z=RING - 1 - me.z, c=1 - me.c))

    def remote(src, dst, send, recv, device):
        return pltpu.make_async_remote_copy(
            src_ref=src, dst_ref=dst, send_sem=send, recv_sem=recv,
            device_id=device, device_id_type=MESH,
        )

    fill_taps(taps_ref)
    for load in loads:
        load.wait()
    length = records.shape[2]
    stations = records.shape[1]
    for side in range(2):
        tail_own[side * stations : (side + 1) * stations, :] = records[
            blocks[side], :, length - LANE :
        ]
    pl.semaphore_wait(barrier, 2 * RING - 1 + 6)

    tm = lax.axis_index("tm")
    after = lax.rem(tm + 1, 4 * RING)
    tail_copy = remote(
        tail_own, tail_in, tail_sem.at[0], tail_sem.at[1],
        {"pair": lax.axis_index("pair"), "tm": after},
    )
    pl.when(tm < 4 * RING - 1)(tail_copy.start)
    fill_transform(fwd_high, fwd_low)
    count = live[tm]
    lane = lax.broadcasted_iota(jnp.int32, (1, LANE), 1)
    record = jnp.concatenate([records[blocks[0]], records[blocks[1]]], axis=0)
    span = DECIM * LANE
    pieces = []
    for b in range(SEG // LANE):
        both = dot(record[:, b * span : (b + 1) * span], taps_ref[LANE:, :])
        if b > 0:
            both = both + dot(record[:, b * span - LANE : b * span], taps_ref[:LANE, :])
        pieces.append(both)

    @pl.when(tm == 0)
    def _():
        tail_in[...] = jnp.zeros_like(tail_in)

    pl.when(tm > 0)(tail_copy.wait_recv)
    pieces[0] = pieces[0] + dot(tail_in[...], taps_ref[:LANE, :])
    filtered = jnp.concatenate(
        [
            jnp.where(lane + b * LANE < count, both[:, :LANE] + both[:, LANE:], 0.0)
            for b, both in enumerate(pieces)
        ],
        axis=1,
    )
    real, imag = whiten(filtered, fwd_high, fwd_low, padded)
    pack_columns(real, imag, col_ref)

    pending = []

    def start(copy, when=None):
        if when is None:
            copy.start()
        else:
            pl.when(when)(copy.start)
        pending.append((copy, when))

    for j in range(4):
        root_z, root_c = root_pair * 2 + j // 2, j % 2
        mine = (me.z == root_z) & (me.c == root_c)
        index = me.c * RING + me.z
        copy = remote(
            col_ref.at[j], stage.at[index], stage_send.at[j], stage_recv.at[index],
            me.at(z=root_z, c=root_c),
        )
        start(copy, jnp.logical_not(mine))

        @pl.when(mine)
        def _():
            pltpu.make_async_copy(col_ref.at[j], stage.at[index], stage_recv.at[index]).start()

    pack_rows(real, imag, row_ref)
    own = slot_of(me.xh, me.c, me.z)

    def part(s):
        return pl.ds(s * size, size)

    def spread(source, slot, h, d, sign, s):
        lower = h == 0
        for way, target in ((1, right), (-1, left)):
            if sign not in (0, way) or d > 3 or (d == 3 and lower != (way == 1)):
                continue
            start(
                remote(
                    source.at[part(s)], row_all.at[slot, part(s)],
                    row_send.at[h, (0 if way == 1 else 4) + d, s], row_recv.at[slot, s],
                    me.at(z=target),
                )
            )
        number = d + 3 if sign == -1 and d < 4 else (7 if d == 4 else d)
        start(
            remote(
                source.at[part(s)], row_all.at[slot, part(s)], near_send.at[h, number, s],
                near_recv.at[slot, s], me.at(c=1 - me.c),
            )
        )

    def got_row(slot, s, sems):
        ref = row_all.at[slot, part(s)]
        remote(ref, ref, row_send.at[0, 0, 0], sems.at[slot, s], me.at()).wait_recv()

    def widen_part(slot, s):
        each = QUARTERS // PARTS
        widen(row_all.at[slot], slot, range(s * each, (s + 1) * each), rows)

    def got_col(slot):
        ref = col_all.at[slot]
        remote(ref, ref, col_send.at[0, 0], col_recv.at[slot], me.at()).wait_recv()

    for s in range(PARTS):
        start(
            remote(
                row_ref.at[part(s)], row_all.at[own, part(s)], row_send.at[2, 0, s],
                row_recv.at[own, s], me.at(xh=1 - me.xh),
            )
        )
    for s in range(PARTS):
        spread(row_ref, own, 0, 0, 0, s)
    widen(row_ref, own, range(QUARTERS), rows)

    def zpiece(i):
        return lax.rem(me.z + OFFSETS[i] + RING, RING)

    def along(source, slot, c, when):
        start(
            remote(
                source, col_all.at[slot], col_send.at[slot, 1], col_recv.at[slot],
                me.at(y=up if c == 0 else down),
            ),
            when,
        )

    def sideways(source, slot, when, **there):
        start(
            remote(
                source, col_all.at[slot], col_send.at[slot, 0], col_recv.at[slot],
                me.at(xl=1 - me.xl, **there),
            ),
            when,
        )

    def hop(slot, c, when):
        pl.when(when)(lambda: got_col(slot))
        along(col_all.at[slot], slot, c, when)

    for kind, arg in schedule():
        if kind == "opposite":
            slot = slot_of(1 - me.xh, me.c, me.z)
            got_row(slot, arg, row_recv)
            spread(row_all.at[slot], slot, 1, 0, 0, arg)
            widen_part(slot, arg)
        elif kind == "row":
            h, d, s = arg
            xh = me.xh if h == 0 else 1 - me.xh
            signs = (1, -1) if d < 4 else ((1,) if h == 0 else (-1,))
            for sign in signs:
                slot = slot_of(xh, me.c, lax.rem(me.z - sign * d + RING, RING))
                got_row(slot, s, row_recv)
                spread(row_all.at[slot], slot, h, d, sign, s)
                widen_part(slot, s)
        elif kind == "root":
            for c in range(2):
                index = c * RING + zpiece(arg)
                slot = slot_of(me.xh, c, zpiece(arg))

                @pl.when(is_root)
                def _():
                    pltpu.make_async_copy(
                        stage.at[index], stage.at[index], stage_recv.at[index]
                    ).wait()

                @pl.when(is_near)
                def _():
                    pltpu.make_async_copy(
                        stage.at[index], col_all.at[slot], local_sem.at[2 * arg + c]
                    ).start()

                sideways(stage.at[index], slot, is_near)
                sideways(stage.at[index], slot, is_far, xh=1 - me.xh)
                start(
                    remote(
                        stage.at[index], col_all.at[slot], col_send.at[slot, 2],
                        col_recv.at[slot], me.at(xh=1 - me.xh),
                    ),
                    is_far,
                )
                along(stage.at[index], slot, c, is_near)
        elif kind == "other":
            for c in range(2):
                hop(slot_of(1 - me.xh, c, zpiece(arg)), c, is_other)
            for c in range(2):
                hop(slot_of(me.xh, c, zpiece(arg)), c, is_other)
        elif kind == "near":
            for c in range(2):
                hop(slot_of(1 - me.xh, c, zpiece(arg)), c, is_near)
        elif kind == "hop1":
            for xh in (me.xh, 1 - me.xh):
                hop(slot_of(xh, 0, zpiece(arg)), 0, dy == 1)
                hop(slot_of(xh, 1, zpiece(arg)), 1, dy == 3)
        elif kind == "hop2":
            for xh in (me.xh, 1 - me.xh):
                for c in range(2):
                    hop(slot_of(xh, c, zpiece(arg)), c, dy == 2)
        elif kind == "last":
            for xh in (me.xh, 1 - me.xh):
                pl.when(dy == 3)(lambda xh=xh: got_col(slot_of(xh, 0, zpiece(arg))))
                pl.when(dy == 1)(lambda xh=xh: got_col(slot_of(xh, 1, zpiece(arg))))

    for h in range(2):
        for z in range(RING):
            for s in range(PARTS):
                slot = slot_of(h, 1 - me.c, z)
                got_row(slot, s, near_recv)
                widen_part(slot, s)
    for i in range(RING):
        for c in range(2):
            index = c * RING + zpiece(i)
            slot = slot_of(me.xh, c, zpiece(i))

            @pl.when(is_near)
            def _():
                pltpu.make_async_copy(
                    stage.at[index], col_all.at[slot], local_sem.at[2 * i + c]
                ).wait()

    for copy, when in pending:
        if when is None:
            copy.wait_send()
        else:
            pl.when(when)(copy.wait_send)
    pl.when(tm < 4 * RING - 1)(tail_copy.wait_send)

    def chunk_copies(chunk):
        return [
            pltpu.make_async_copy(
                stacked.at[:, pl.ds(pl.multiple_of(side * BINS + chunk * LANE, LANE), LANE)],
                stacked_out.at[:, pl.ds(pl.multiple_of(side * BINS + chunk * LANE, LANE), LANE)],
                out_sem.at[side, chunk],
            )
            for side in range(2)
        ]

    @pl.loop(0, CHUNKS)
    def _(chunk):
        cross_chunk(chunk, row_all, col_all, rows, cols, cross, stacked)
        for copy in chunk_copies(chunk):
            copy.start()

    @pl.loop(0, CHUNKS)
    def _(chunk):
        for copy in chunk_copies(chunk):
            copy.wait()


def widen(source, slot, quarters, rows):
    for chunk in range(CHUNKS):
        for quarter in quarters:
            at = (chunk * (4 * RING) + slot) * STRIDE_K + quarter * KCHUNK
            first = quarter * LANE + chunk * KCHUNK
            rows[pl.ds(pl.multiple_of(at, 8), KCHUNK), :] = source[
                first : first + KCHUNK, :
            ].astype(F32)


def cross_chunk(chunk, row_all, col_all, rows, cols, cross, stacked):
    segments = row_all.shape[0]
    half = LANE // 2
    group = 8
    count_k = QUARTERS * KCHUNK
    first = pl.multiple_of(chunk * KCHUNK, KCHUNK)
    for g in range(segments):
        cols[g * STRIDE_C : g * STRIDE_C + KCHUNK, :] = col_all[
            g, pl.ds(first, KCHUNK), :
        ].astype(F32)
    lane = lax.broadcasted_iota(jnp.int32, (32, group * segments), 1)
    sign = jnp.where(
        lax.broadcasted_iota(jnp.int32, (1, LANE), 1) < half, 1.0, -1.0
    ).astype(F32)
    for block in range(KCHUNK // group):
        gathered = jnp.concatenate(
            [cols[pl.ds(block * group + b, segments, stride=STRIDE_C), :] for b in range(group)],
            axis=0,
        )
        turned = gathered.T.astype(BF16)
        for quarter in range(QUARTERS):
            left = turned[quarter * 32 : quarter * 32 + 32, :]
            zero = jnp.zeros_like(left)
            wide = jnp.concatenate(
                [
                    jnp.where((lane >= b * segments) & (lane < (b + 1) * segments), left, zero)
                    for b in range(group)
                ],
                axis=0,
            )
            base = quarter * KCHUNK + block * group
            right = jnp.concatenate(
                [rows[pl.ds(chunk * (segments * STRIDE_K) + base + b, segments, stride=STRIDE_K), :] for b in range(group)],
                axis=0,
            ).astype(BF16)
            product = dot(wide, right)
            for b in range(group):
                top = product[b * 32 : b * 32 + 16, :]
                low = product[b * 32 + 16 : b * 32 + 32, :]
                cross[pl.ds(base + b, 16, stride=STRIDE_K), :] = top + sign * pltpu.roll(
                    low, half, 1
                )
    at = pl.multiple_of(chunk * count_k, LANE)
    for q in range(16):
        turned = cross[q * STRIDE_K : q * STRIDE_K + count_k, :].astype(BF16).T
        stacked[q * half : (q + 1) * half, pl.ds(at, count_k)] = turned[:half]
        stacked[q * half : (q + 1) * half, pl.ds(BINS + at, count_k)] = turned[half:]


def spectra(records, tile_blocks, live_len):
    dma = pltpu.SemaphoreType.DMA
    return pl.pallas_call(
        spectra_kernel,
        in_specs=[pl.BlockSpec(memory_space=pltpu.HBM)] * 3,
        out_specs=pl.BlockSpec(memory_space=pltpu.HBM),
        out_shape=jax.ShapeDtypeStruct((PAIRS, 2 * BINS), BF16),
        scratch_shapes=[
            pltpu.VMEM((PAIRS, 2 * BINS), BF16),
            pltpu.SMEM(tile_blocks.shape, jnp.int32),
            pltpu.SMEM(live_len.shape, jnp.int32),
            pltpu.VMEM(records.shape, BF16),
            pltpu.VMEM((LANE, LANE), BF16),
            pltpu.VMEM((LANE, LANE), BF16),
            pltpu.VMEM((5 * LANE, 2 * LANE), BF16),
            pltpu.VMEM((2 * BINS, SEG), BF16),
            pltpu.VMEM((2 * BINS, SEG), BF16),
            pltpu.VMEM((BINS + 16, LANE), F32),
            pltpu.VMEM((BINS, LANE), BF16),
            pltpu.VMEM((4, LANE, LANE), BF16),
            pltpu.VMEM((4 * RING, BINS, LANE), BF16),
            pltpu.VMEM((4 * RING, LANE, LANE), BF16),
            pltpu.VMEM((2 * RING, LANE, LANE), BF16),
            pltpu.VMEM((CHUNKS * 4 * RING * STRIDE_K, LANE), F32),
            pltpu.VMEM((4 * RING * STRIDE_C, LANE), F32),
            pltpu.VMEM((16 * STRIDE_K, LANE), F32),
            dma((2, CHUNKS)), dma((3,)), dma((2,)),
            dma((3, 8, PARTS)), dma((32, PARTS)), dma((2, 8, PARTS)), dma((32, PARTS)),
            dma((4,)), dma((2 * RING,)), dma((32, 3)), dma((32,)), dma((2 * RING + 1,)),
        ],
        compiler_params=pltpu.CompilerParams(
            collective_id=0, has_side_effects=True, vmem_limit_bytes=60 << 20
        ),
        name="spectra",
    )(tile_blocks, live_len, records)


def lags_kernel(stacked, lag_ref, out_ref, spare):
    half = LANE // 2
    full = LAGS // (2 * LANE)

    def tile(sides):
        value = dot(stacked[...], lag_ref[:, : sides * LANE])
        for q in range(16):
            for side in range(sides):
                spare[side, q * STRIDE_P : q * STRIDE_P + half, :] = value[
                    q * half : (q + 1) * half, side * LANE : (side + 1) * LANE
                ]
        for p in range(half):
            for side in range(sides):
                out_ref[p * 16 : p * 16 + 16, side * LANE : (side + 1) * LANE] = spare[
                    side, pl.ds(p, 16, stride=STRIDE_P), :
                ]

    pl.when(pl.program_id(0) < full)(lambda: tile(2))
    pl.when(pl.program_id(0) == full)(lambda: tile(1))


def lags(stacked):
    width = 2 * LANE
    tiles = -(-LAGS // width)
    table = jnp.asarray(np.pad(lag_table(), ((0, 0), (0, tiles * width - LAGS))))
    return pl.pallas_call(
        lags_kernel,
        grid=(tiles,),
        in_specs=[
            pl.BlockSpec((PAIRS, 2 * BINS), lambda i: (0, 0)),
            pl.BlockSpec((2 * BINS, width), lambda i: (0, i)),
        ],
        out_specs=pl.BlockSpec((PAIRS, width), lambda i: (0, i)),
        out_shape=jax.ShapeDtypeStruct((PAIRS, LAGS), F32),
        scratch_shapes=[pltpu.VMEM((2, 16 * STRIDE_P, LANE), F32)],
        compiler_params=pltpu.CompilerParams(vmem_limit_bytes=32 << 20),
        name="lags",
    )(stacked, table)


def shards(records, tile_blocks, live_len):
    result = lags(spectra(records, tile_blocks, live_len))
    return result.reshape(LANE // 2, 16, LAGS)


def solution(mesh):
    placed = (P(None, "pair", "tm"), P(), P())
    return jax.shard_map(
        shards, mesh=mesh, in_specs=placed, out_specs=P("pair", "tm", None), check_vma=False
    )
```
